256 devices in a mesh: group: 8 (over z_lo, y), dev: 32 (over z_hi, x, core).
Axes of the slice: x: 4, y: 4, z: 8 (z_hi: 4, z_lo: 2; z = z_hi * 2 + z_lo), core: 2. Of those that a mesh axis runs over, the one named last changes fastest.
Arguments:
- right_side: float32 [3, 16, 64, 64, 128], P(None, 'group', 'dev'), may hold values from -60 to 60
- stiff_diag: float32 [3, 3, 16, 4096], P(None, None, 'group', 'dev'), may hold values from -0.1 to 12.75, as said below
- stiff_lower: float32 [3, 3, 13, 16, 4096], P(None, None, None, 'group', 'dev'), may hold values from -0.08 to 0.08
- fsai_diag: float32 [3, 3, 16, 4096], P(None, None, 'group', 'dev'), may hold values from -0.1 to 1, as said below
- fsai_lower: float32 [3, 3, 13, 16, 4096], P(None, None, None, 'group', 'dev'), may hold values from -0.12 to 0.12
- fsai_pattern: int32 [13, 16, 4096], P(None, 'group', 'dev'), may hold values 0 or 1
Outputs:
- solution: float32 [3, 16, 64, 64, 128], P(None, 'group', 'dev')
- residual: float32 [3, 16, 64, 64, 128], P(None, 'group', 'dev')
The draws below stay inside these ranges and needn't reach their ends.
Inputs may be any that keep to these rules, and one draw needn't show every extreme that they name: `stiff_diag`: each 3 by 3 block is symmetric. `fsai_diag`: each 3 by 3 block is zero above its diagonal and positive on it.
All inputs are finite; a program needn't handle non-finite values. No bound on the sum of `fsai_pattern` on one device may be relied on, other than what follows from the above.
Results may differ from the reference program's by a relative error of at most 0.0003.
Values sent between devices are 32-bit elements; how exact they have to be, the bound alone decides.
A program may use at most 128 MiB of HBM per device.

```python
import jax
import jax.numpy as jnp
from jax import lax

PX = 64
PY = 64
NRHS = 128
KL = 13
ITERS = 2
NZ = 16
PLANE = 4096


def draw_right_side(key, part):
    subkeys = jax.random.split(jax.random.fold_in(key, 101), 4)
    depth_pos = jnp.arange(NZ, dtype=jnp.float32) / NZ
    row_pos = jnp.arange(PX, dtype=jnp.float32) / PX
    rising = jnp.exp(jnp.log(3.0) * (depth_pos[:, None, None] + row_pos[None, :, None]))
    row_scale = jnp.exp(jax.random.uniform(subkeys[0], (NZ, PX, PY), dtype=jnp.float32) * jnp.log(10.0)) * rising
    col_scale = jnp.exp(jax.random.uniform(subkeys[1], (NRHS,), dtype=jnp.float32) * jnp.log(10.0))
    values = jax.random.normal(subkeys[3], (3, NZ, PX, PY, NRHS), dtype=jnp.float32)
    values = jnp.clip(values, -4.0, 4.0)
    return values * row_scale[None, :, :, :, None] * col_scale[None, None, None, None, :] / 60.0


def draw_stiff_diag(key, part):
    subkeys = jax.random.split(jax.random.fold_in(key, 202), 2)
    coupling = jax.random.uniform(subkeys[0], (3, 3, NZ, PLANE), dtype=jnp.float32, minval=-0.1, maxval=0.1)
    coupling = 0.5 * (coupling + jnp.transpose(coupling, (1, 0, 2, 3)))
    spread = jnp.exp(jax.random.uniform(subkeys[1], (3, NZ, PLANE), dtype=jnp.float32, minval=jnp.log(0.5), maxval=jnp.log(6.0)))
    identity = jnp.eye(3, dtype=jnp.float32)[:, :, None, None]
    return coupling * (1.0 - identity) + identity * (6.75 + spread)[:, None, :, :]


def draw_fsai_diag(key, part):
    subkeys = jax.random.split(jax.random.fold_in(key, 303), 2)
    lower_mask = jnp.tril(jnp.ones((3, 3), jnp.float32), -1)[:, :, None, None]
    coupling = jax.random.uniform(subkeys[0], (3, 3, NZ, PLANE), dtype=jnp.float32, minval=-0.1, maxval=0.1) * lower_mask
    diagonal_values = jnp.exp(jax.random.uniform(subkeys[1], (3, NZ, PLANE), dtype=jnp.float32, minval=jnp.log(0.3), maxval=0.0))
    identity = jnp.eye(3, dtype=jnp.float32)[:, :, None, None]
    return coupling + identity * diagonal_values[:, None, :, :]


def plant(values, stream_key, low, largest):
    place = [jax.random.randint(jax.random.fold_in(stream_key, axis), (), 0, length) for axis, length in enumerate(values.shape)]
    longest = values.shape.index(max(values.shape))
    neighbour = place[:longest] + [(place[longest] + 1) % values.shape[longest]] + place[longest + 1:]
    return values.at[tuple(place)].set(low).at[tuple(neighbour)].set(largest)


def block_scale(key, shape, cuts, least, top_value):
    gain, own = 1.0, jax.random.fold_in(key, 6)
    for axis_at, shards_of in cuts:
        draws = jnp.exp(jax.random.uniform(jax.random.fold_in(own, axis_at), (shards_of,), jnp.float32, least / len(cuts), top_value / len(cuts)))
        gain = gain * jnp.repeat(draws, shape[axis_at] // shards_of).reshape([-1 if axis == axis_at else 1 for axis in range(len(shape))])
    return gain


def setup_inputs(seed: int = 0) -> dict:
    arg_keys = jax.random.split(jax.random.key(seed), 7)
    return {
        "right_side": draw_right_side(jax.random.fold_in(arg_keys[6], 71), 0),
        "stiff_diag": draw_stiff_diag(jax.random.fold_in(arg_keys[6], 71), 0),
        "stiff_lower": jnp.clip(jax.random.uniform(arg_keys[2], (3, 3, KL, NZ, PLANE), jnp.float32, -0.08, 0.08) * block_scale(arg_keys[2], (3, 3, KL, NZ, PLANE), ((3, 8), (4, 32)), -0.4, 0.0), -0.08, 0.08),
        "fsai_diag": draw_fsai_diag(jax.random.fold_in(arg_keys[6], 71), 0),
        "fsai_lower": jnp.clip(jax.random.uniform(arg_keys[4], (3, 3, KL, NZ, PLANE), jnp.float32, -0.12, 0.12) * block_scale(arg_keys[4], (3, 3, KL, NZ, PLANE), ((3, 8), (4, 32)), -0.4, 0.0), -0.12, 0.12),
        "fsai_pattern": plant((jax.random.randint(arg_keys[5], (KL, NZ, PLANE), 0, 4) < 3).astype(jnp.int32), jax.random.fold_in(arg_keys[5], 1), 0, 1),
    }


highest = lax.Precision.HIGHEST
lower_offsets = [(0, 0, -1), (0, -1, -1), (0, -1, 0), (0, -1, 1)] + [(-1, row_step, column_step) for row_step in (-1, 0, 1) for column_step in (-1, 0, 1)]

def block_mul(coeffs, vector):
    return jnp.stack([coeffs[target, 0][..., None] * vector[0] + coeffs[target, 1][..., None] * vector[1] + coeffs[target, 2][..., None] * vector[2] for target in range(3)])

def block_mul_transposed(coeffs, vector):
    return jnp.stack([coeffs[0, target][..., None] * vector[0] + coeffs[1, target][..., None] * vector[1] + coeffs[2, target][..., None] * vector[2] for target in range(3)])

def pad_grid(vector):
    return jnp.pad(vector, ((0, 0), (1, 1), (1, 1), (1, 1), (0, 0)))

def window(padded, depth_step, row_step, column_step, extent):
    return padded[:, 1 + depth_step:1 + depth_step + extent[0], 1 + row_step:1 + row_step + extent[1], 1 + column_step:1 + column_step + extent[2]]

def lower_part(diag_blocks, low_blocks, vector):
    extent = vector.shape[1:4]
    padded = pad_grid(vector)
    result = block_mul(diag_blocks, vector)
    for slot_index, (depth_step, row_step, column_step) in enumerate(lower_offsets):
        result = result + block_mul(low_blocks[:, :, slot_index], window(padded, depth_step, row_step, column_step, extent))
    return result

def upper_part(low_blocks, vector):
    extent = vector.shape[1:4]
    result = jnp.zeros_like(vector)
    for slot_index, (depth_step, row_step, column_step) in enumerate(lower_offsets):
        moved_terms = pad_grid(block_mul_transposed(low_blocks[:, :, slot_index], vector))
        result = result + window(moved_terms, -depth_step, -row_step, -column_step, extent)
    return result

def local_gram(left_block, right_block):
    return jnp.einsum('azxyr,azxys->rs', left_block, right_block, precision=highest)

def combine(vector, coeffs):
    return jnp.einsum('azxyr,rs->azxys', vector, coeffs, precision=highest)

def gram_solve(matrix, right_terms):
    factor = jnp.linalg.cholesky(matrix)
    halfway = lax.linalg.triangular_solve(factor, right_terms, left_side=True, lower=True)
    return lax.linalg.triangular_solve(factor, halfway, left_side=True, lower=True, transpose_a=True)

def reference(right_side, stiff_diag, stiff_lower, fsai_diag, fsai_lower, fsai_pattern):
    stiff_d = stiff_diag.reshape(3, 3, NZ, PX, PY)
    fsai_d = fsai_diag.reshape(3, 3, NZ, PX, PY)
    stiff_low = stiff_lower.reshape(3, 3, KL, NZ, PX, PY)
    kept = fsai_pattern.astype(fsai_lower.dtype)
    fsai_low = (fsai_lower * kept[None, None]).reshape(3, 3, KL, NZ, PX, PY)

    def apply_matrix(vector):
        return lower_part(stiff_d, stiff_low, vector) + upper_part(stiff_low, vector)

    def apply_fsai(vector):
        return lower_part(fsai_d, fsai_low, vector)

    def apply_fsai_transposed(vector):
        return block_mul_transposed(fsai_d, vector) + upper_part(fsai_low, vector)
    solution = jnp.zeros_like(right_side)
    residual = right_side
    weighted = apply_fsai(residual)
    resid_gram = local_gram(weighted, weighted)
    direction = apply_fsai_transposed(weighted)
    for iteration in range(ITERS):
        product = apply_matrix(direction)
        step_size = gram_solve(local_gram(direction, product), resid_gram)
        solution = solution + combine(direction, step_size)
        residual = residual - combine(product, step_size)
        if iteration + 1 < ITERS:
            weighted = apply_fsai(residual)
            next_gram = local_gram(weighted, weighted)
            precond = apply_fsai_transposed(weighted)
            conjugacy = gram_solve(resid_gram, next_gram)
            direction = precond + combine(direction, conjugacy)
            resid_gram = next_gram
    return (solution, residual)
```

```python
import functools

import jax
import jax.numpy as jnp
from jax import lax
from jax.experimental import pallas as pl
from jax.experimental.pallas import tpu as pltpu
from jax.sharding import PartitionSpec as P

MESH = pl.DeviceIdType.MESH
highest = lax.Precision.HIGHEST
GROUP_Y = 4
DEV_XC = 8
PLANE_PEERS = GROUP_Y * DEV_XC
lower_offsets = [(0, 0, -1), (0, -1, -1), (0, -1, 0), (0, -1, 1)] + [
    (-1, row_step, column_step) for row_step in (-1, 0, 1) for column_step in (-1, 0, 1)
]


def with_halo(block, sides, width):
    for axis, dim in sides:
        count = lax.axis_size(axis)
        forward = [(i, i + 1) for i in range(count - 1)]
        backward = [(target, source) for source, target in forward]
        low = lax.ppermute(
            lax.slice_in_dim(block, block.shape[dim] - width, None, axis=dim), axis, forward
        )
        high = lax.ppermute(lax.slice_in_dim(block, 0, width, axis=dim), axis, backward)
        block = jnp.concatenate([low, block, high], axis=dim)
    return block


def from_behind(value, axis, steps):
    count = lax.axis_size(axis)
    first, last = (max(0, -steps), min(count, count - steps))
    return lax.ppermute(value, axis, [(source, source + steps) for source in range(first, last)])


def block_mul(coeffs, vector):
    return jnp.stack(
        [
            coeffs[target, 0][..., None] * vector[0]
            + coeffs[target, 1][..., None] * vector[1]
            + coeffs[target, 2][..., None] * vector[2]
            for target in range(3)
        ]
    )


def block_mul_transposed(coeffs, vector):
    return jnp.stack(
        [
            coeffs[0, target][..., None] * vector[0]
            + coeffs[1, target][..., None] * vector[1]
            + coeffs[2, target][..., None] * vector[2]
            for target in range(3)
        ]
    )


def pad_columns(vector):
    return jnp.pad(vector, ((0, 0), (0, 0), (0, 0), (1, 1), (0, 0)))


def reduce_kernel(z_lo_count, z_hi_count, g_ref, out_ref, rs_buf, z_buf, send, recv, z_send, z_recv, a_send, a_recv):
    group, dev = lax.axis_index("group"), lax.axis_index("dev")
    z_lo, y = group // GROUP_Y, group % GROUP_Y
    z_hi, xc = dev // DEV_XC, dev % DEV_XC
    me = y * DEV_XC + xc
    my_z = z_hi * z_lo_count + z_lo
    z_count = z_lo_count * z_hi_count

    def plane_peer(step):
        peer = (me + step) % PLANE_PEERS
        return peer, (z_lo * GROUP_Y + peer // DEV_XC, z_hi * DEV_XC + peer % DEV_XC)

    def z_peer(step):
        peer = (my_z + step) % z_count
        return peer, (peer % z_lo_count * GROUP_Y + y, peer // z_lo_count * DEV_XC + xc)

    barrier = pltpu.get_barrier_semaphore()

    def greet(step, peer_of):
        pl.semaphore_signal(barrier, inc=1, device_id=peer_of(step)[1], device_id_type=MESH)
        return peer_of

    lax.fori_loop(1, PLANE_PEERS, lambda s, c: (greet(s, plane_peer), c)[1], 0)
    lax.fori_loop(1, z_count, lambda s, c: (greet(s, z_peer), c)[1], 0)
    pl.semaphore_wait(barrier, PLANE_PEERS - 1 + z_count - 1)

    def scatter(step):
        peer, place = plane_peer(step)
        return pltpu.make_async_remote_copy(
            src_ref=g_ref.at[peer], dst_ref=rs_buf.at[me], send_sem=send.at[step],
            recv_sem=recv.at[step], device_id=place, device_id_type=MESH,
        )

    def exchange(step):
        _, place = z_peer(step)
        return pltpu.make_async_remote_copy(
            src_ref=z_buf.at[my_z], dst_ref=z_buf.at[my_z], send_sem=z_send.at[step],
            recv_sem=z_recv.at[step], device_id=place, device_id_type=MESH,
        )

    def gather(step):
        _, place = plane_peer(step)
        return pltpu.make_async_remote_copy(
            src_ref=out_ref.at[me], dst_ref=out_ref.at[me], send_sem=a_send.at[step],
            recv_sem=a_recv.at[step], device_id=place, device_id_type=MESH,
        )

    def run(count, make, method):
        def body(step, carry):
            getattr(make(step), method)()
            return carry
        lax.fori_loop(1, count, body, 0)

    rs_buf[me] = g_ref[me]
    run(PLANE_PEERS, scatter, "start")
    run(PLANE_PEERS, scatter, "wait_recv")
    z_buf[my_z] = jnp.sum(rs_buf[...], axis=0)
    run(z_count, exchange, "start")
    run(z_count, exchange, "wait_recv")
    out_ref[me] = jnp.sum(z_buf[...], axis=0)
    run(PLANE_PEERS, gather, "start")
    run(PLANE_PEERS, gather, "wait_recv")
    run(PLANE_PEERS, scatter, "wait_send")
    run(z_count, exchange, "wait_send")
    run(PLANE_PEERS, gather, "wait_send")


def reduce_grams(grams):
    z_lo_count = lax.axis_size("group") // GROUP_Y
    z_hi_count = lax.axis_size("dev") // DEV_XC
    z_count = z_lo_count * z_hi_count
    rows = grams.shape[0] // PLANE_PEERS
    pieces = (PLANE_PEERS, rows, grams.shape[1])
    vmem = pl.BlockSpec(memory_space=pltpu.VMEM)
    total = pl.pallas_call(
        functools.partial(reduce_kernel, z_lo_count, z_hi_count),
        out_shape=jax.ShapeDtypeStruct(pieces, jnp.float32),
        in_specs=[vmem],
        out_specs=vmem,
        scratch_shapes=[
            pltpu.VMEM(pieces, jnp.float32),
            pltpu.VMEM((z_count,) + pieces[1:], jnp.float32),
        ]
        + [pltpu.SemaphoreType.DMA((PLANE_PEERS,))] * 2
        + [pltpu.SemaphoreType.DMA((z_count,))] * 2
        + [pltpu.SemaphoreType.DMA((PLANE_PEERS,))] * 2,
        compiler_params=pltpu.CompilerParams(collective_id=0, has_side_effects=True),
        name="reduce_grams",
    )(grams.reshape(pieces))
    return total.reshape(grams.shape)


def mm(left, right, dims=((1,), (0,))):
    return lax.dot_general(left, right, (dims, ((), ())), precision=highest, preferred_element_type=jnp.float32)


def invert(*matrices):
    size = matrices[0].shape[0]
    lane = lax.broadcasted_iota(jnp.int32, (size, size), 1)
    sub = lax.broadcasted_iota(jnp.int32, (size, size), 0)
    lane_row = lax.broadcasted_iota(jnp.int32, (1, size), 1)
    matrices = list(matrices)
    for k in range(size):
        for i, m in enumerate(matrices):
            inverse = 1.0 / m[k : k + 1, k : k + 1]
            row = jnp.where(lane_row == k, inverse, m[k : k + 1, :] * inverse)
            column = m[:, k : k + 1]
            swept = jnp.where(lane == k, 0.0, m) - column * row
            matrices[i] = jnp.where(sub == k, jnp.broadcast_to(row, m.shape), swept)
    return matrices


def finish_kernel(grams_ref, right_ref, d_ref, q_ref, z_ref, y_ref, solution_ref, residual_ref):
    size = grams_ref.shape[1]
    resid, energy, coupling, outer = [grams_ref[i * size : (i + 1) * size, :] for i in range(4)]
    identity = (
        lax.broadcasted_iota(jnp.int32, (size, size), 0) == lax.broadcasted_iota(jnp.int32, (size, size), 1)
    ).astype(jnp.float32)
    trans = ((0,), (0,))
    energy = 0.5 * (energy + energy.T)
    energy_inv, resid_inv = invert(energy, resid)
    step = mm(energy_inv, resid)
    shift = mm(energy, step)
    next_gram = resid - shift - shift.T + mm(step, mm(coupling, step), trans)
    grow = identity + mm(resid_inv, next_gram)
    cross = mm(grow, mm(coupling, step), trans)
    next_energy = mm(grow, mm(energy, grow), trans) - cross - cross.T + mm(step, mm(outer, step), trans)
    next_energy = 0.5 * (next_energy + next_energy.T)
    (next_inv,) = invert(next_energy)
    next_step = mm(next_inv, next_gram)
    near = step + mm(grow, next_step)
    far = mm(step, next_step)
    solution_ref[...] = mm(d_ref[...], near) - mm(z_ref[...], far)
    residual_ref[...] = right_ref[...] - mm(q_ref[...], near) + mm(y_ref[...], far)


def finish(grams, *vectors):
    shape = vectors[0].shape
    flat = [v.reshape(-1, shape[-1]) for v in vectors]
    vmem = pl.BlockSpec(memory_space=pltpu.VMEM)
    outs = pl.pallas_call(
        finish_kernel,
        out_shape=[jax.ShapeDtypeStruct(flat[0].shape, jnp.float32)] * 2,
        in_specs=[vmem] * (1 + len(flat)),
        out_specs=[vmem] * 2,
        name="finish",
    )(grams, *flat)
    return tuple(o.reshape(shape) for o in outs)


def local_gram(left_block, right_block):
    return jnp.einsum("azxyr,azxys->rs", left_block, right_block, precision=highest)


def per_device(right_side, stiff_diag, stiff_lower, fsai_diag, fsai_lower, fsai_pattern):
    local_planes = right_side.shape[1]
    local_rows = right_side.shape[2]
    line_length = right_side.shape[3]
    slot_count = stiff_lower.shape[2]
    stiff_d = stiff_diag.reshape(3, 3, local_planes, local_rows, line_length)
    fsai_d = fsai_diag.reshape(3, 3, local_planes, local_rows, line_length)
    stiff_low = stiff_lower.reshape(3, 3, slot_count, local_planes, local_rows, line_length)
    kept = fsai_pattern.astype(jnp.float32)
    fsai_low = (fsai_lower * kept[None, None]).reshape(
        3, 3, slot_count, local_planes, local_rows, line_length
    )

    def lower_window(vector):
        rimmed = with_halo(vector, (("dev", 2),), 1)
        plane_under = from_behind(rimmed[:, local_planes - 1 :], "group", 1)
        return pad_columns(jnp.concatenate([plane_under, rimmed], axis=1))

    def gather_lower(diag_blocks, low_blocks, window_data, vector):
        result = block_mul(diag_blocks, vector)
        for slot_index, (depth_step, row_step, column_step) in enumerate(lower_offsets):
            picked = window_data[
                :,
                1 + depth_step : 1 + depth_step + local_planes,
                1 + row_step : 1 + row_step + local_rows,
                1 + column_step : 1 + column_step + line_length,
            ]
            result = result + block_mul(low_blocks[:, :, slot_index], picked)
        return result

    def push_upper(low_blocks, vector):
        buffer = None
        for slot_index, (depth_step, row_step, column_step) in enumerate(lower_offsets):
            slot_term = block_mul_transposed(low_blocks[:, :, slot_index], vector)
            placed = jnp.pad(
                slot_term,
                (
                    (0, 0),
                    (1 + depth_step, -depth_step),
                    (1 + row_step, 1 - row_step),
                    (1 + column_step, 1 - column_step),
                    (0, 0),
                ),
            )
            buffer = placed if buffer is None else buffer + placed
        inner_part = buffer[:, :, :, 1 : line_length + 1]
        rim_rows = jnp.concatenate(
            [inner_part[:, :, :1], inner_part[:, :, local_rows + 1 :]], axis=2
        )
        arrived = with_halo(rim_rows, (("dev", 2),), 1)
        core_part = inner_part[:, :, 1 : local_rows + 1]
        core_part = core_part.at[:, :, :1].add(arrived[:, :, :1])
        core_part = core_part.at[:, :, local_rows - 1 :].add(arrived[:, :, 3:])
        returned = from_behind(core_part[:, :1], "group", -1)
        return core_part[:, 1:].at[:, local_planes - 1 :].add(returned)

    def apply_fsai(vector):
        return gather_lower(fsai_d, fsai_low, lower_window(vector), vector)

    def apply_fsai_transposed(vector):
        diagonal_part = block_mul_transposed(fsai_d, vector)
        upper_sum = push_upper(fsai_low, vector)
        return diagonal_part + upper_sum

    def apply_matrix(vector):
        return gather_lower(stiff_d, stiff_low, lower_window(vector), vector) + push_upper(stiff_low, vector)

    weighted = apply_fsai(right_side)
    direction = apply_fsai_transposed(weighted)
    product = apply_matrix(direction)
    image = apply_fsai(product)
    second = apply_fsai_transposed(image)
    second_product = apply_matrix(second)
    grams = jnp.concatenate(
        [
            local_gram(weighted, weighted),
            local_gram(direction, product),
            local_gram(image, image),
            local_gram(second, second_product),
        ]
    )
    return finish(reduce_grams(grams), right_side, direction, product, second, second_product)


def solution(mesh):
    return jax.shard_map(
        per_device,
        mesh=mesh,
        in_specs=(
            P(None, "group", "dev", None, None),
            P(None, None, "group", "dev"),
            P(None, None, None, "group", "dev"),
            P(None, None, "group", "dev"),
            P(None, None, None, "group", "dev"),
            P(None, "group", "dev"),
        ),
        out_specs=(P(None, "group", "dev", None, None), P(None, "group", "dev", None, None)),
        check_vma=False,
    )
```

```python
import functools

import jax
import jax.numpy as jnp
from jax import lax
from jax.experimental import pallas as pl
from jax.experimental.pallas import tpu as pltpu
from jax.sharding import PartitionSpec as P

MESH = pl.DeviceIdType.MESH
highest = lax.Precision.HIGHEST
GROUP_Y = 4
DEV_XC = 8
PLANE_PEERS = GROUP_Y * DEV_XC
lower_offsets = [(0, 0, -1), (0, -1, -1), (0, -1, 0), (0, -1, 1)] + [
    (-1, row_step, column_step) for row_step in (-1, 0, 1) for column_step in (-1, 0, 1)
]


def mm(left, right, dims=((1,), (0,))):
    return lax.dot_general(left, right, (dims, ((), ())), precision=highest, preferred_element_type=jnp.float32)


def invert(*matrices):
    size = matrices[0].shape[0]
    lane = lax.broadcasted_iota(jnp.int32, (size, size), 1)
    sub = lax.broadcasted_iota(jnp.int32, (size, size), 0)
    lane_row = lax.broadcasted_iota(jnp.int32, (1, size), 1)
    matrices = list(matrices)
    for k in range(size):
        for i, m in enumerate(matrices):
            inverse = 1.0 / m[k : k + 1, k : k + 1]
            row = jnp.where(lane_row == k, inverse, m[k : k + 1, :] * inverse)
            column = m[:, k : k + 1]
            swept = jnp.where(lane == k, 0.0, m) - column * row
            matrices[i] = jnp.where(sub == k, jnp.broadcast_to(row, m.shape), swept)
    return matrices


def finish_kernel(grams_ref, right_ref, basis_ref, solution_ref, residual_ref):
    size = grams_ref.shape[1]
    resid, energy, coupling, outer = [grams_ref[i * size : (i + 1) * size, :] for i in range(4)]
    identity = (
        lax.broadcasted_iota(jnp.int32, (size, size), 0) == lax.broadcasted_iota(jnp.int32, (size, size), 1)
    ).astype(jnp.float32)
    trans = ((0,), (0,))
    energy = 0.5 * (energy + energy.T)
    energy_inv, resid_inv = invert(energy, resid)
    step = mm(energy_inv, resid)
    shift = mm(energy, step)
    next_gram = resid - shift - shift.T + mm(step, mm(coupling, step), trans)
    grow = identity + mm(resid_inv, next_gram)
    cross = mm(grow, mm(coupling, step), trans)
    next_energy = mm(grow, mm(energy, grow), trans) - cross - cross.T + mm(step, mm(outer, step), trans)
    next_energy = 0.5 * (next_energy + next_energy.T)
    (next_inv,) = invert(next_energy)
    next_step = mm(next_inv, next_gram)
    near = step + mm(grow, next_step)
    far = mm(step, next_step)
    for c in range(right_ref.shape[0]):
        flat = (-1, size)
        d, q, z, y = [basis_ref[k, c].reshape(flat) for k in range(4)]
        block = right_ref.shape[1:]
        solution_ref[c] = (mm(d, near) - mm(z, far)).reshape(block)
        residual_ref[c] = (right_ref[c].reshape(flat) - mm(q, near) + mm(y, far)).reshape(block)


def finish(grams, right_side, basis):
    vmem = pl.BlockSpec(memory_space=pltpu.VMEM)
    return tuple(
        pl.pallas_call(
            finish_kernel,
            out_shape=[jax.ShapeDtypeStruct(right_side.shape, jnp.float32)] * 2,
            in_specs=[vmem] * 3,
            out_specs=[vmem] * 2,
            name="finish",
        )(grams, right_side, basis)
    )


EDGE = 8
CHANNELS = 8
LOWER, UPPER, BOTH = 0, 1, 2


def krylov_kernel(
    z_lo_count, z_hi_count, right_ref, coef_ref, total_ref, out_ref,
    vec, coef, grams, rs_buf, z_buf,
    halo_send, halo_recv, send, recv, z_send, z_recv, a_send, a_recv,
):
    columns = right_ref.shape[3]
    inner = pl.ds(EDGE, columns)
    group, dev = lax.axis_index("group"), lax.axis_index("dev")
    group_count, dev_count = GROUP_Y * z_lo_count, DEV_XC * z_hi_count
    z_lo, y = group // GROUP_Y, group % GROUP_Y
    z_hi, xc = dev // DEV_XC, dev % DEV_XC
    me = y * DEV_XC + xc
    my_z = z_hi * z_lo_count + z_lo
    z_count = z_lo_count * z_hi_count
    has_prev_dev, has_next_dev = dev > 0, dev < dev_count - 1
    has_prev_group, has_next_group = group > 0, group < group_count - 1
    prev_dev, next_dev = (group, dev - 1), (group, dev + 1)
    prev_group, next_group = (group - 1, dev), (group + 1, dev)

    def plane_peer(step):
        peer = (me + step) % PLANE_PEERS
        return peer, (z_lo * GROUP_Y + peer // DEV_XC, z_hi * DEV_XC + peer % DEV_XC)

    def z_peer(step):
        peer = (my_z + step) % z_count
        return peer, (peer % z_lo_count * GROUP_Y + y, peer // z_lo_count * DEV_XC + xc)

    def clear(line, carry):
        plane, row = line // 4, line % 4
        for v in range(vec.shape[0]):
            vec[v, plane, row] = jnp.zeros(vec.shape[3:], jnp.float32)
        coef[plane, row] = jnp.zeros(coef.shape[2:], jnp.float32)
        return carry

    lax.fori_loop(0, 16, clear, 0)

    def load(line, carry):
        plane, row = line // 2, line % 2
        for c in range(3):
            vec[0, plane + 1, row + 1, c, inner, :] = right_ref[c, plane, row]
        for c in range(2):
            coef[plane + 1, row + 1, c, inner, :] = coef_ref[c, plane, row]
        return carry

    lax.fori_loop(0, 4, load, 0)

    barrier = pltpu.get_barrier_semaphore()

    def greet(place):
        pl.semaphore_signal(barrier, inc=1, device_id=place, device_id_type=MESH)

    def greet_all(count, peer_of):
        def body(step, carry):
            greet(peer_of(step)[1])
            return carry
        lax.fori_loop(1, count, body, 0)

    greet_all(PLANE_PEERS, plane_peer)
    greet_all(z_count, z_peer)
    neighbours = (
        (group, (dev + dev_count - 1) % dev_count), (group, (dev + 1) % dev_count),
        ((group + group_count - 1) % group_count, dev), ((group + 1) % group_count, dev),
    )
    for place in neighbours:
        greet(place)
    pl.semaphore_wait(barrier, PLANE_PEERS - 1 + z_count - 1 + len(neighbours))

    def channel(number, kind):
        down = pl.ds(2, 1) if kind == UPPER else pl.ds(1, 2)
        up = pl.ds(1, 1) if kind == LOWER else pl.ds(1, 2)
        one, rows = (lambda i: pl.ds(i, 1)), pl.ds(1, 2)
        return [
            ((down, one(2)), (down, one(0)), next_dev, has_next_dev, has_prev_dev),
            ((up, one(1)), (up, one(3)), prev_dev, has_prev_dev, has_next_dev),
            ((one(2), rows), (one(0), rows), next_group, has_next_group, has_prev_group),
            ((one(1), rows), (one(3), rows), prev_group, has_prev_group, has_next_group),
            ((one(0), one(2)), (one(0), one(0)), next_dev, has_next_dev & has_prev_group, has_prev_dev & has_prev_group),
            ((one(0), one(1)), (one(0), one(3)), prev_dev, has_prev_dev & has_prev_group, has_next_dev & has_prev_group),
            ((one(3), one(2)), (one(3), one(0)), next_dev, has_next_dev & has_next_group, has_prev_dev & has_next_group),
            ((one(3), one(1)), (one(3), one(3)), prev_dev, has_prev_dev & has_next_group, has_next_dev & has_next_group),
        ][number]

    def halo(buf, phase, number, kind, method):
        (src_plane, src_row), (dst_plane, dst_row), place, to, come = channel(number, kind)

        @pl.when(come if method == "wait_recv" else to)
        def _():
            copy = pltpu.make_async_remote_copy(
                src_ref=buf.at[src_plane, src_row, :, inner, :],
                dst_ref=buf.at[dst_plane, dst_row, :, inner, :],
                send_sem=halo_send.at[phase, number], recv_sem=halo_recv.at[phase, number],
                device_id=place, device_id_type=MESH,
            )
            getattr(copy, method)()

    planes_of = {LOWER: (2,), UPPER: (3,), BOTH: (2, 3)}
    corners_of = {LOWER: (4, 5), UPPER: (6, 7), BOTH: (4, 5, 6, 7)}

    def send_own(buf, phase, kind):
        for number in planes_of[kind] + (0, 1):
            halo(buf, phase, number, kind, "start")

    def take_rims(buf, phase, kind):
        for number in (0, 1):
            halo(buf, phase, number, kind, "wait_recv")

    def pass_planes(buf, phase, kind):
        for number in planes_of[kind]:
            halo(buf, phase, number, kind, "wait_recv")
        for number in corners_of[kind]:
            halo(buf, phase, number, kind, "start")

    def take_corners(buf, phase, kind):
        for number in corners_of[kind]:
            halo(buf, phase, number, kind, "wait_recv")

    def settle(buf, phase, kind):
        for number in (0, 1) + planes_of[kind] + corners_of[kind]:
            halo(buf, phase, number, kind, "wait_send")

    def accumulate(acc, source, which, upper, diagonal, plane, row):
        slots = ([((0, 0, 0), None)] if diagonal else []) + list(zip(lower_offsets, range(len(lower_offsets))))
        for (a, b, c), slot in slots:
            sign = -1 if upper else 1
            at_plane, at_row = plane + 1 + sign * a, row + 1 + sign * b
            cols = pl.ds(EDGE + sign * c, columns)
            blocks = coef[at_plane, at_row, which, cols, :] if upper else coef[plane + 1, row + 1, which, inner, :]
            for j in range(3):
                value = source[at_plane, at_row, j, cols, :]
                for i in range(3):
                    entry = (j * 3 + i) if upper else (i * 3 + j)
                    lane = entry if slot is None else 9 + entry * len(lower_offsets) + slot
                    acc[i] = acc[i] + blocks[:, lane : lane + 1] * value
        return acc

    def apply(source, target, which, kind, between):
        def body(line, carry):
            row, late = line % 2, line // 2

            @pl.when(line == 2)
            def _():
                between()

            parts = {LOWER: ((False, 1 - late, True),), UPPER: ((True, late, True),), BOTH: ((False, 1 - late, True), (True, late, False))}[kind]
            for upper, plane, diagonal in parts:
                old = [target[plane + 1, row + 1, i, inner, :] for i in range(3)]
                new = accumulate(old, source, which, upper, diagonal, plane, row)
                for i in range(3):
                    target[plane + 1, row + 1, i, inner, :] = new[i]
            return carry

        lax.fori_loop(0, 4, body, 0)

    def rows_of(v):
        both = pl.ds(1, 2)
        block = vec[v, both, both, :, inner, :]
        return block.reshape(-1, block.shape[-1])

    def gram(index, left, right):
        left = rows_of(left)
        right = left if right is None else rows_of(right)
        value = mm(left, right, ((0,), (0,)))
        count = value.shape[0] // grams.shape[1]
        grams[pl.ds(index * count, count)] = value.reshape((count,) + grams.shape[1:])

    coef_phase = 6
    send_own(vec.at[0], 0, LOWER)
    send_own(coef, coef_phase, UPPER)

    def round_body(t, carry):
        v = 3 * t
        source, weighted, direction, product = [vec.at[v + k] for k in range(4)]
        f = 3 * t

        @pl.when(t == 1)
        def _():
            send_own(source, f, LOWER)
            gram(1, 2, 3)

        take_rims(source, f, LOWER)

        def planes_lower():
            pass_planes(source, f, LOWER)

            @pl.when(t == 0)
            def _():
                pass_planes(coef, coef_phase, UPPER)
            take_corners(source, f, LOWER)

        apply(source, weighted, 0, LOWER, planes_lower)

        send_own(weighted, f + 1, UPPER)
        gram(2 * t, v + 1, None)
        take_rims(weighted, f + 1, UPPER)

        @pl.when(t == 0)
        def _():
            take_rims(coef, coef_phase, UPPER)
            take_corners(coef, coef_phase, UPPER)

        def planes_upper():
            pass_planes(weighted, f + 1, UPPER)
            take_corners(weighted, f + 1, UPPER)

        apply(weighted, direction, 0, UPPER, planes_upper)

        send_own(direction, f + 2, BOTH)
        take_rims(direction, f + 2, BOTH)

        def planes_both():
            pass_planes(direction, f + 2, BOTH)
            take_corners(direction, f + 2, BOTH)

        apply(direction, product, 1, BOTH, planes_both)

        settle(source, f, LOWER)
        settle(weighted, f + 1, UPPER)
        settle(direction, f + 2, BOTH)
        return carry

    lax.fori_loop(0, 2, round_body, 0)
    settle(coef, coef_phase, UPPER)
    gram(3, 5, 6)

    def scatter(step):
        peer, place = plane_peer(step)
        return pltpu.make_async_remote_copy(
            src_ref=grams.at[peer], dst_ref=rs_buf.at[me], send_sem=send.at[step],
            recv_sem=recv.at[step], device_id=place, device_id_type=MESH,
        )

    def exchange(step):
        _, place = z_peer(step)
        return pltpu.make_async_remote_copy(
            src_ref=z_buf.at[my_z], dst_ref=z_buf.at[my_z], send_sem=z_send.at[step],
            recv_sem=z_recv.at[step], device_id=place, device_id_type=MESH,
        )

    def gather(step):
        _, place = plane_peer(step)
        return pltpu.make_async_remote_copy(
            src_ref=total_ref.at[me], dst_ref=total_ref.at[me], send_sem=a_send.at[step],
            recv_sem=a_recv.at[step], device_id=place, device_id_type=MESH,
        )

    def run(count, make, method):
        def body(step, carry):
            getattr(make(step), method)()
            return carry
        lax.fori_loop(1, count, body, 0)

    run(PLANE_PEERS, scatter, "start")
    rs_buf[me] = grams[me]

    def emit(line, carry):
        plane, row = line // 2, line % 2
        for slot, v in enumerate((2, 3, 5, 6)):
            for c in range(3):
                out_ref[slot, c, plane, row] = vec[v, plane + 1, row + 1, c, inner, :]
        return carry

    lax.fori_loop(0, 4, emit, 0)
    run(PLANE_PEERS, scatter, "wait_recv")
    z_buf[my_z] = jnp.sum(rs_buf[...], axis=0)
    run(z_count, exchange, "start")
    run(z_count, exchange, "wait_recv")
    total_ref[me] = jnp.sum(z_buf[...], axis=0)
    run(PLANE_PEERS, gather, "start")
    run(PLANE_PEERS, gather, "wait_recv")
    run(PLANE_PEERS, scatter, "wait_send")
    run(z_count, exchange, "wait_send")
    run(PLANE_PEERS, gather, "wait_send")


def krylov(right_side, coefs):
    z_lo_count = lax.axis_size("group") // GROUP_Y
    z_hi_count = lax.axis_size("dev") // DEV_XC
    z_count = z_lo_count * z_hi_count
    columns, size = right_side.shape[3:]
    pieces = (PLANE_PEERS, 4 * size // PLANE_PEERS, size)
    wide = columns + 2 * EDGE
    vmem = pl.BlockSpec(memory_space=pltpu.VMEM)
    dma = pltpu.SemaphoreType.DMA
    total, vectors = pl.pallas_call(
        functools.partial(krylov_kernel, z_lo_count, z_hi_count),
        out_shape=[
            jax.ShapeDtypeStruct(pieces, jnp.float32),
            jax.ShapeDtypeStruct((4,) + right_side.shape, jnp.float32),
        ],
        in_specs=[vmem] * 2,
        out_specs=[vmem] * 2,
        scratch_shapes=[
            pltpu.VMEM((7, 4, 4, 3, wide, size), jnp.float32),
            pltpu.VMEM((4, 4, 2, wide, size), jnp.float32),
            pltpu.VMEM(pieces, jnp.float32),
            pltpu.VMEM(pieces, jnp.float32),
            pltpu.VMEM((z_count,) + pieces[1:], jnp.float32),
            dma((7, CHANNELS)), dma((7, CHANNELS)),
            dma((PLANE_PEERS,)), dma((PLANE_PEERS,)),
            dma((z_count,)), dma((z_count,)),
            dma((PLANE_PEERS,)), dma((PLANE_PEERS,)),
        ],
        compiler_params=pltpu.CompilerParams(collective_id=0, has_side_effects=True),
        name="krylov",
    )(right_side, coefs)
    return total.reshape(4 * size, size), vectors


def per_device(right_side, stiff_diag, stiff_lower, fsai_diag, fsai_lower, fsai_pattern):
    planes, rows, columns = right_side.shape[1:4]
    kept = fsai_pattern.astype(jnp.float32)

    def by_node(diag, lower):
        entries = jnp.concatenate([diag.reshape((9,) + diag.shape[2:]), lower.reshape((-1,) + lower.shape[3:])])
        entries = jnp.pad(entries, ((0, right_side.shape[4] - entries.shape[0]), (0, 0), (0, 0)))
        return jnp.transpose(entries, (1, 2, 0)).reshape(planes, rows, columns, -1)

    coefs = jnp.stack([by_node(fsai_diag, fsai_lower * kept[None, None]), by_node(stiff_diag, stiff_lower)])
    return finish_of(right_side, krylov(right_side, coefs))


def finish_of(right_side, reduced):
    grams, basis = reduced
    return finish(grams, right_side, basis)


def solution(mesh):
    return jax.shard_map(
        per_device,
        mesh=mesh,
        in_specs=(
            P(None, "group", "dev", None, None),
            P(None, None, "group", "dev"),
            P(None, None, None, "group", "dev"),
            P(None, None, "group", "dev"),
            P(None, None, None, "group", "dev"),
            P(None, "group", "dev"),
        ),
        out_specs=(P(None, "group", "dev", None, None), P(None, "group", "dev", None, None)),
        check_vma=False,
    )
```

```python
import functools

import jax
import jax.numpy as jnp
from jax import lax
from jax.experimental import pallas as pl
from jax.experimental.pallas import tpu as pltpu
from jax.sharding import PartitionSpec as P

MESH = pl.DeviceIdType.MESH
highest = lax.Precision.HIGHEST
GROUP_Y = 4
DEV_XC = 8
PLANE_PEERS = GROUP_Y * DEV_XC
lower_offsets = [(0, 0, -1), (0, -1, -1), (0, -1, 0), (0, -1, 1)] + [
    (-1, row_step, column_step) for row_step in (-1, 0, 1) for column_step in (-1, 0, 1)
]


def mm(left, right, dims=((1,), (0,))):
    return lax.dot_general(left, right, (dims, ((), ())), precision=highest, preferred_element_type=jnp.float32)


TRANS = ((0,), (0,))


def sweep(matrix, row_id, column_id):
    def body(k, m):
        on_row, on_column = row_id == k, column_id == k
        row = jnp.sum(jnp.where(on_row, m, 0.0), axis=0, keepdims=True)
        column = jnp.sum(jnp.where(on_column, m, 0.0), axis=1, keepdims=True)
        pivot = jnp.sum(jnp.where(on_row & on_column, m, 0.0), axis=(0, 1), keepdims=True)
        row = jnp.where(on_column[:1], 1.0, row) / pivot
        swept = jnp.where(on_column, 0.0, m) - column * row
        return jnp.where(on_row, jnp.broadcast_to(row, m.shape), swept)

    return lax.fori_loop(0, matrix.shape[0], body, matrix)


def invert(scratch, *matrices):
    size = matrices[0].shape[0]
    row_id = lax.broadcasted_iota(jnp.int32, (size, size), 0)
    column_id = lax.broadcasted_iota(jnp.int32, (size, size), 1)
    eye = row_id == column_id
    identity = eye.astype(jnp.float32)
    scales, scaled = [], []
    for i, m in enumerate(matrices):
        diag = jnp.where(eye, m, 0.0)
        down = lax.rsqrt(jnp.sum(diag, axis=1, keepdims=True))
        across = lax.rsqrt(jnp.sum(diag, axis=0, keepdims=True))
        scales.append((down, across))
        unit = m * down * across
        scaled.append(unit)
        bound = jnp.max(jnp.sum(jnp.abs(unit), axis=0, keepdims=True), axis=1, keepdims=True)
        gain = 2.0 / (1.0 + bound)
        scratch[i] = gain * (2.0 * identity - gain * unit)

    def more(state):
        count, error = state
        return (error > 1e-8) & (count < 16)

    def newton(state):
        error = 0.0
        for i, unit in enumerate(scaled):
            guess = scratch[i]
            miss = identity - mm(unit, guess)
            scratch[i] = guess + mm(guess, miss)
            error = jnp.maximum(error, jnp.sum(miss * miss))
        return state[0] + 1, error

    _, error = lax.while_loop(more, newton, (0, jnp.float32(1.0)))

    @pl.when(jnp.logical_not(error <= 1e-8))
    def _():
        for i, unit in enumerate(scaled):
            scratch[i] = sweep(unit, row_id, column_id)

    return [scratch[i] * down * across for i, (down, across) in enumerate(scales)]


def finish_kernel(grams_ref, right_ref, basis_ref, solution_ref, residual_ref, scratch):
    size = grams_ref.shape[1]
    resid, energy, coupling, outer = [grams_ref[i * size : (i + 1) * size, :] for i in range(4)]
    identity = (
        lax.broadcasted_iota(jnp.int32, (size, size), 0) == lax.broadcasted_iota(jnp.int32, (size, size), 1)
    ).astype(jnp.float32)
    energy = 0.5 * (energy + energy.T)
    energy_inv, resid_inv = invert(scratch, energy, resid)
    step = mm(energy_inv, resid)
    shift = mm(energy, step)
    coupled = mm(coupling, step)
    next_gram = resid - shift - shift.T + mm(step, coupled, TRANS)
    grow = identity + mm(resid_inv, next_gram)
    cross = mm(grow, coupled, TRANS)
    next_energy = mm(grow, mm(energy, grow), TRANS) - cross - cross.T + mm(step, mm(outer, step), TRANS)
    next_energy = 0.5 * (next_energy + next_energy.T)
    (next_inv,) = invert(scratch, next_energy)
    next_step = mm(next_inv, next_gram)
    near = step + mm(grow, next_step)
    far = mm(step, next_step)
    weights = jnp.concatenate([near.T, -far.T], axis=1)
    planes, comps = basis_ref.shape[1:3]
    for p in range(planes):
        for c in range(comps):
            block = right_ref.shape[2:]
            ahead = mm(weights, jnp.concatenate([basis_ref[0, p, c], basis_ref[2, p, c]]))
            drop = mm(weights, jnp.concatenate([basis_ref[1, p, c], basis_ref[3, p, c]]))
            solution_ref[c, p] = ahead.T.reshape(block)
            residual_ref[c, p] = right_ref[c, p] - drop.T.reshape(block)


def finish(grams, right_side, basis):
    vmem = pl.BlockSpec(memory_space=pltpu.VMEM)
    return tuple(
        pl.pallas_call(
            finish_kernel,
            out_shape=[jax.ShapeDtypeStruct(right_side.shape, jnp.float32)] * 2,
            in_specs=[vmem] * 3,
            out_specs=[vmem] * 2,
            scratch_shapes=[pltpu.VMEM((2, grams.shape[1], grams.shape[1]), jnp.float32)],
            name="finish",
        )(grams, right_side, basis)
    )


CHANNELS = 8
LOWER, UPPER, BOTH = 0, 1, 2
SLOTS = len(lower_offsets)
PHASES = 6


def krylov_kernel(
    z_lo_count, z_hi_count, right_ref, coef_ref, total_ref, out_ref,
    vec, edge, rim_out, rim_in, low, high, low_out, low_in, grams, rs_buf, z_buf,
    halo_send, halo_recv, send, recv, z_send, z_recv, a_send, a_recv,
):
    size, lanes = vec.shape[3:]
    half, top, bottom = lanes // 2, pl.ds(0, size // 2), pl.ds(size // 2, size // 2)
    group, dev = lax.axis_index("group"), lax.axis_index("dev")
    group_count, dev_count = GROUP_Y * z_lo_count, DEV_XC * z_hi_count
    z_lo, y = group // GROUP_Y, group % GROUP_Y
    z_hi, xc = dev // DEV_XC, dev % DEV_XC
    me = y * DEV_XC + xc
    my_z = z_hi * z_lo_count + z_lo
    z_count = z_lo_count * z_hi_count
    has_prev_dev, has_next_dev = dev > 0, dev < dev_count - 1
    has_prev_group, has_next_group = group > 0, group < group_count - 1
    prev_dev, next_dev = (group, dev - 1), (group, dev + 1)
    prev_group, next_group = (group - 1, dev), (group + 1, dev)

    def plane_peer(step):
        peer = (me + step) % PLANE_PEERS
        return peer, (z_lo * GROUP_Y + peer // DEV_XC, z_hi * DEV_XC + peer % DEV_XC)

    def z_peer(step):
        peer = (my_z + step) % z_count
        return peer, (peer % z_lo_count * GROUP_Y + y, peer // z_lo_count * DEV_XC + xc)

    def clear(ref):
        ref[...] = jnp.zeros(ref.shape, ref.dtype)

    def clear_phases(*refs_of):
        def body(f, carry):
            for ref_of in refs_of:
                clear(ref_of(f))
            return carry
        lax.fori_loop(0, PHASES, body, 0)

    @pl.when(jnp.logical_not(has_prev_dev))
    def _():
        clear_phases(lambda f: rim_in.at[f, 0])
        clear(low_in.at[0])

    @pl.when(jnp.logical_not(has_next_dev))
    def _():
        clear_phases(lambda f: rim_in.at[f, 1])
        clear(low_in.at[1])

    @pl.when(jnp.logical_not(has_prev_group))
    def _():
        clear_phases(lambda f: rim_in.at[f, 0, 0], lambda f: rim_in.at[f, 1, 0], lambda f: vec.at[f, 0])

    @pl.when(jnp.logical_not(has_next_group))
    def _():
        clear_phases(lambda f: rim_in.at[f, 0, 3], lambda f: rim_in.at[f, 1, 3], lambda f: vec.at[f, 3])
        for k in range(2):
            clear(low_in.at[k, 2])
            clear(low.at[k, 2])

    barrier = pltpu.get_barrier_semaphore()

    def greet(place):
        pl.semaphore_signal(barrier, inc=1, device_id=place, device_id_type=MESH)

    def greet_all(count, peer_of):
        def body(step, carry):
            greet(peer_of(step)[1])
            return carry
        lax.fori_loop(1, count, body, 0)

    neighbours = (
        (group, (dev + dev_count - 1) % dev_count), (group, (dev + 1) % dev_count),
        ((group + group_count - 1) % group_count, dev), ((group + 1) % group_count, dev),
    )
    greet_all(PLANE_PEERS, plane_peer)
    greet_all(z_count, z_peer)
    for place in neighbours:
        greet(place)

    def left_of(shape):
        return lax.broadcasted_iota(jnp.int32, shape, len(shape) - 1) < half

    def swap(tile):
        return pltpu.roll(tile, half, axis=tile.ndim - 1)

    def turn(tile, step):
        return tile if step == 0 else pltpu.roll(tile, -step % lanes, axis=tile.ndim - 1)

    for p in range(2):
        for c in range(3):
            vec[0, p + 1, c] = right_ref[c, p].reshape(lanes, size).T

    left_low = left_of(low.shape[3:])
    left_half = left_of((size // 2, lanes))

    def pack_low(plane):
        low_out[0, plane] = jnp.where(left_low[None], swap(low[0, plane]), low[1, plane])
        low_out[1, plane] = jnp.where(left_low[None], low[0, plane], swap(low[1, plane]))

    for p in range(2):
        for k in range(2):
            low[k, p] = coef_ref[k, p, 1:]
        pack_low(p)
    pl.semaphore_wait(barrier, PLANE_PEERS - 1 + z_count - 1 + len(neighbours))

    def route(number):
        return [
            (next_dev, has_next_dev, has_prev_dev),
            (prev_dev, has_prev_dev, has_next_dev),
            (next_group, has_next_group, has_prev_group),
            (prev_group, has_prev_group, has_next_group),
            (next_dev, has_next_dev & has_prev_group, has_prev_dev & has_prev_group),
            (prev_dev, has_prev_dev & has_prev_group, has_next_dev & has_prev_group),
            (next_dev, has_next_dev & has_next_group, has_prev_dev & has_next_group),
            (prev_dev, has_prev_dev & has_next_group, has_next_dev & has_next_group),
        ][number]

    def move(source, target, phase, number, method):
        place, to, come = route(number)

        @pl.when(come if method == "wait_recv" else to)
        def _():
            copy = pltpu.make_async_remote_copy(
                src_ref=source, dst_ref=target,
                send_sem=halo_send.at[phase, number], recv_sem=halo_recv.at[phase, number],
                device_id=place, device_id_type=MESH,
            )
            getattr(copy, method)()

    def halo(f, number, kind, method):
        if number in (2, 3):
            source, target = (2, 0) if number == 2 else (1, 3)
            move(vec.at[f, source], vec.at[f, target], f, number, method)
            return
        side = number % 2
        if number > 3:
            planes = pl.ds(0 if number < 6 else 3, 1)
        elif side == 0:
            planes = pl.ds(2, 1) if kind == UPPER else pl.ds(1, 2)
        else:
            planes = pl.ds(1, 1) if kind == LOWER else pl.ds(1, 2)
        move(rim_out.at[f, side, planes], rim_in.at[f, side, planes], f, number, method)

    def low_halo(number, method):
        if number == 3:
            move(low.at[:, 0], low.at[:, 2], PHASES, number, method)
            return
        side = number % 2
        planes = pl.ds(2, 1) if number > 3 else (pl.ds(1, 1) if side == 0 else pl.ds(0, 2))
        move(low_out.at[side, planes], low_in.at[side, planes], PHASES, number, method)

    planes_of = {LOWER: (2,), UPPER: (3,), BOTH: (2, 3)}
    corners_of = {LOWER: (4, 5), UPPER: (6, 7), BOTH: (4, 5, 6, 7)}

    def pack(f, plane, sides=(0, 1)):
        for c in range(3):
            upper_rows, lower_rows = vec[f, plane, c, top, :], vec[f, plane, c, bottom, :]
            if 0 in sides:
                rim_out[f, 0, plane, c] = jnp.where(left_half, swap(upper_rows), lower_rows)
            if 1 in sides:
                rim_out[f, 1, plane, c] = jnp.where(left_half, upper_rows, swap(lower_rows))

    def unpack(f, plane):
        for c in range(3):
            before, after = rim_in[f, 0, plane, c], rim_in[f, 1, plane, c]
            edge[plane, c, top, :] = jnp.where(left_half, before, swap(after))
            edge[plane, c, bottom, :] = jnp.where(left_half, swap(before), after)

    def send_own(f, kind):
        for number in planes_of[kind]:
            halo(f, number, kind, "start")
        for plane in (1, 2):
            pack(f, plane)
        for number in (0, 1):
            halo(f, number, kind, "start")

    def take_rims(f, kind):
        for number in (0, 1):
            halo(f, number, kind, "wait_recv")
        for plane in (1, 2):
            unpack(f, plane)

    outer_of = {LOWER: (0,), UPPER: (3,), BOTH: (0, 3)}

    def pass_planes(f, kind):
        for number, plane in zip(planes_of[kind], outer_of[kind]):
            halo(f, number, kind, "wait_recv")
            pack(f, plane)
            for corner in (4, 5) if plane == 0 else (6, 7):
                halo(f, corner, kind, "start")

    def take_corners(f, kind):
        for number in corners_of[kind]:
            halo(f, number, kind, "wait_recv")
        for plane in outer_of[kind]:
            unpack(f, plane)

    def settle(f, kind):
        for number in (0, 1) + planes_of[kind] + corners_of[kind]:
            halo(f, number, kind, "wait_send")

    def raise_coefs(k):
        def body(p, carry):
            for slot, (a, b, c) in enumerate(lower_offsets):
                at = p - a
                base = low[k, at, slot]
                if b == -1:
                    rim = low_in[1, at, slot]
                    base = jnp.where(left_low, swap(base), swap(rim) if k == 0 else rim)
                elif b == 1:
                    rim = low_in[0, at, slot]
                    base = jnp.where(left_low, rim if k == 0 else swap(rim), swap(base))
                high[k, p, slot] = turn(base, -c)
            return carry
        lax.fori_loop(0, 2, body, 0)

    groups = {}
    for slot, (a, b, c) in enumerate(lower_offsets):
        groups.setdefault((a, b), []).append((slot, c))

    rows_count = 32
    left = left_of((rows_count, lanes))

    def accumulate(acc, v, k, upper, diagonal, plane, rows):
        sign = -1 if upper else 1
        swapped = {}
        for (a, b), slots in groups.items():
            at = plane + 1 + sign * a
            for j in range(3):
                tile = vec[v, at, j, rows, :]
                if b != 0:
                    if (a, j) not in swapped:
                        swapped[a, j] = swap(tile)
                    outside = edge[at, j, rows, :]
                    tile = (
                        jnp.where(left, outside, swapped[a, j]) if sign * b < 0
                        else jnp.where(left, swapped[a, j], outside)
                    )
                if diagonal and (a, b) == (0, 0):
                    for i in range(3):
                        entry = j * 3 + i if upper else i * 3 + j
                        acc[i] = acc[i] + coef_ref[k, plane, 0, pl.ds(entry, 1), :] * tile
                for slot, c in slots:
                    value = turn(tile, sign * c)
                    for i in range(3):
                        if upper:
                            block = high[k, plane, slot, pl.ds(j * 3 + i, 1), :]
                        else:
                            block = low[k, plane, slot, pl.ds(i * 3 + j, 1), :]
                        acc[i] = acc[i] + block * value
        return acc

    def apply(v, target, k, kind, between):
        chunks = size // rows_count

        def body(step, carry):
            late = step // chunks
            rows = pl.ds(pl.multiple_of(step % chunks * rows_count, rows_count), rows_count)

            @pl.when(step == chunks)
            def _():
                between()

            parts = {LOWER: ((False, 1 - late, True),), UPPER: ((True, late, True),), BOTH: ((False, 1 - late, True), (True, late, False))}[kind]
            for upper, plane, diagonal in parts:
                acc = [jnp.zeros((rows_count, lanes), jnp.float32)] * 3
                acc = accumulate(acc, v, k, upper, diagonal, plane, rows)
                for i in range(3):
                    if kind == BOTH:
                        acc[i] = jnp.where(late > 0, vec[target, plane + 1, i, rows, :], 0.0) + acc[i]
                    vec[target, plane + 1, i, rows, :] = acc[i]
            return carry

        lax.fori_loop(0, 2 * chunks, body, 0)

    def across(v):
        return jnp.concatenate([vec[v, p, c] for p in (1, 2) for c in range(3)], axis=1)

    def gram(index, v, w):
        one = across(v)
        value = mm(one, one if w is None else across(w), ((1,), (1,)))
        count = value.shape[0] // grams.shape[1]
        grams[pl.ds(index * count, count)] = value.reshape((count,) + grams.shape[1:])

    send_own(0, LOWER)
    for number in (3, 0, 1):
        low_halo(number, "start")

    def round_body(t, carry):
        f = 3 * t

        @pl.when(t == 1)
        def _():
            send_own(f, LOWER)
            gram(1, 2, 3)

        take_rims(f, LOWER)

        def planes_lower():
            pass_planes(f, LOWER)

            @pl.when(t == 0)
            def _():
                low_halo(3, "wait_recv")
                pack_low(2)
                for number in (6, 7):
                    low_halo(number, "start")
            take_corners(f, LOWER)

        apply(f, f + 1, 0, LOWER, planes_lower)

        send_own(f + 1, UPPER)
        gram(2 * t, f + 1, None)

        @pl.when(t == 0)
        def _():
            for number in (0, 1, 6, 7):
                low_halo(number, "wait_recv")
            raise_coefs(0)
        take_rims(f + 1, UPPER)

        def planes_upper():
            pass_planes(f + 1, UPPER)
            take_corners(f + 1, UPPER)

        apply(f + 1, f + 2, 0, UPPER, planes_upper)

        send_own(f + 2, BOTH)

        @pl.when(t == 0)
        def _():
            raise_coefs(1)
        take_rims(f + 2, BOTH)

        def planes_both():
            pass_planes(f + 2, BOTH)
            take_corners(f + 2, BOTH)

        apply(f + 2, f + 3, 1, BOTH, planes_both)

        settle(f, LOWER)
        settle(f + 1, UPPER)
        settle(f + 2, BOTH)
        return carry

    lax.fori_loop(0, 2, round_body, 0)
    for number in (3, 0, 1, 6, 7):
        low_halo(number, "wait_send")
    gram(3, 5, 6)

    def scatter(step):
        peer, place = plane_peer(step)
        return pltpu.make_async_remote_copy(
            src_ref=grams.at[peer], dst_ref=rs_buf.at[me], send_sem=send.at[step],
            recv_sem=recv.at[step], device_id=place, device_id_type=MESH,
        )

    def exchange(step):
        _, place = z_peer(step)
        return pltpu.make_async_remote_copy(
            src_ref=z_buf.at[my_z], dst_ref=z_buf.at[my_z], send_sem=z_send.at[step],
            recv_sem=z_recv.at[step], device_id=place, device_id_type=MESH,
        )

    def gather(step):
        _, place = plane_peer(step)
        return pltpu.make_async_remote_copy(
            src_ref=total_ref.at[me], dst_ref=total_ref.at[me], send_sem=a_send.at[step],
            recv_sem=a_recv.at[step], device_id=place, device_id_type=MESH,
        )

    def run(count, make, method):
        def body(step, carry):
            getattr(make(step), method)()
            return carry
        lax.fori_loop(1, count, body, 0)

    run(PLANE_PEERS, scatter, "start")
    rs_buf[me] = grams[me]
    for slot, v in enumerate((2, 3, 5, 6)):
        for p in range(2):
            out_ref[slot, p] = vec[v, p + 1]
    run(PLANE_PEERS, scatter, "wait_recv")
    z_buf[my_z] = jnp.sum(rs_buf[...], axis=0)
    run(z_count, exchange, "start")
    run(z_count, exchange, "wait_recv")
    total_ref[me] = jnp.sum(z_buf[...], axis=0)
    run(PLANE_PEERS, gather, "start")
    run(PLANE_PEERS, gather, "wait_recv")
    run(PLANE_PEERS, scatter, "wait_send")
    run(z_count, exchange, "wait_send")
    run(PLANE_PEERS, gather, "wait_send")


def krylov(right_side, coefs):
    z_lo_count = lax.axis_size("group") // GROUP_Y
    z_hi_count = lax.axis_size("dev") // DEV_XC
    z_count = z_lo_count * z_hi_count
    comps, planes, rows, columns, size = right_side.shape
    lanes = rows * columns
    pieces = (PLANE_PEERS, 4 * size // PLANE_PEERS, size)
    vmem = pl.BlockSpec(memory_space=pltpu.VMEM)
    dma = pltpu.SemaphoreType.DMA

    def array(*shape):
        return pltpu.VMEM(shape, jnp.float32)

    total, vectors = pl.pallas_call(
        functools.partial(krylov_kernel, z_lo_count, z_hi_count),
        out_shape=[
            jax.ShapeDtypeStruct(pieces, jnp.float32),
            jax.ShapeDtypeStruct((4, planes, comps, size, lanes), jnp.float32),
        ],
        in_specs=[vmem] * 2,
        out_specs=[vmem] * 2,
        scratch_shapes=[
            array(7, 4, comps, size, lanes),
            array(4, comps, size, lanes),
            array(PHASES, 2, 4, comps, size // 2, lanes),
            array(PHASES, 2, 4, comps, size // 2, lanes),
            array(2, 3, SLOTS, 9, lanes),
            array(2, 2, SLOTS, 9, lanes),
            array(2, 3, SLOTS, 9, lanes),
            array(2, 3, SLOTS, 9, lanes),
            array(*pieces),
            array(*pieces),
            array(z_count, *pieces[1:]),
            dma((PHASES + 1, CHANNELS)), dma((PHASES + 1, CHANNELS)),
            dma((PLANE_PEERS,)), dma((PLANE_PEERS,)),
            dma((z_count,)), dma((z_count,)),
            dma((PLANE_PEERS,)), dma((PLANE_PEERS,)),
        ],
        compiler_params=pltpu.CompilerParams(collective_id=0, has_side_effects=True),
        name="krylov",
    )(right_side, coefs)
    return total.reshape(4 * size, size), vectors


def per_device(right_side, stiff_diag, stiff_lower, fsai_diag, fsai_lower, fsai_pattern):
    columns = right_side.shape[3]
    lanes = stiff_diag.shape[3]
    kept = fsai_pattern.astype(jnp.float32)
    steps = jnp.array([c for _, _, c in lower_offsets])[:, None, None]
    column = jnp.arange(lanes)[None, None, :] % columns + steps
    inside = ((column >= 0) & (column < columns)).astype(jnp.float32)

    def by_plane(diag, lower):
        lower = (lower * inside).reshape((9,) + lower.shape[2:])
        entries = jnp.concatenate([diag.reshape((9, 1) + diag.shape[2:]), lower], axis=1)
        return jnp.transpose(entries, (2, 1, 0, 3))

    coefs = jnp.stack([by_plane(fsai_diag, fsai_lower * kept[None, None]), by_plane(stiff_diag, stiff_lower)])
    grams, basis = krylov(right_side, coefs)
    return finish(grams, right_side, basis)


def solution(mesh):
    return jax.shard_map(
        per_device,
        mesh=mesh,
        in_specs=(
            P(None, "group", "dev", None, None),
            P(None, None, "group", "dev"),
            P(None, None, None, "group", "dev"),
            P(None, None, "group", "dev"),
            P(None, None, None, "group", "dev"),
            P(None, "group", "dev"),
        ),
        out_specs=(P(None, "group", "dev", None, None), P(None, "group", "dev", None, None)),
        check_vma=False,
    )
```

```python
import functools

import jax
import jax.numpy as jnp
from jax import lax
from jax.experimental import pallas as pl
from jax.experimental.pallas import tpu as pltpu
from jax.sharding import PartitionSpec as P

MESH = pl.DeviceIdType.MESH
highest = lax.Precision.HIGHEST
GROUP_Y = 4
DEV_XC = 8
PLANE_PEERS = GROUP_Y * DEV_XC
lower_offsets = [(0, 0, -1), (0, -1, -1), (0, -1, 0), (0, -1, 1)] + [
    (-1, row_step, column_step) for row_step in (-1, 0, 1) for column_step in (-1, 0, 1)
]


def mm(left, right, dims=((1,), (0,))):
    return lax.dot_general(left, right, (dims, ((), ())), precision=highest, preferred_element_type=jnp.float32)


TRANS = ((0,), (0,))


def sweep(matrix, row_id, column_id):
    def body(k, m):
        on_row, on_column = row_id == k, column_id == k
        row = jnp.sum(jnp.where(on_row, m, 0.0), axis=0, keepdims=True)
        column = jnp.sum(jnp.where(on_column, m, 0.0), axis=1, keepdims=True)
        pivot = jnp.sum(jnp.where(on_row & on_column, m, 0.0), axis=(0, 1), keepdims=True)
        row = jnp.where(on_column[:1], 1.0, row) / pivot
        swept = jnp.where(on_column, 0.0, m) - column * row
        return jnp.where(on_row, jnp.broadcast_to(row, m.shape), swept)

    return lax.fori_loop(0, matrix.shape[0], body, matrix)


def invert(scratch, *matrices):
    size = matrices[0].shape[0]
    row_id = lax.broadcasted_iota(jnp.int32, (size, size), 0)
    column_id = lax.broadcasted_iota(jnp.int32, (size, size), 1)
    eye = row_id == column_id
    identity = eye.astype(jnp.float32)
    scales, scaled = [], []
    for i, m in enumerate(matrices):
        diag = jnp.where(eye, m, 0.0)
        down = lax.rsqrt(jnp.sum(diag, axis=1, keepdims=True))
        across = lax.rsqrt(jnp.sum(diag, axis=0, keepdims=True))
        scales.append((down, across))
        unit = m * down * across
        scaled.append(unit)
        bound = jnp.max(jnp.sum(jnp.abs(unit), axis=0, keepdims=True), axis=1, keepdims=True)
        gain = 2.0 / (1.0 + bound)
        scratch[i] = gain * (2.0 * identity - gain * unit)

    def more(state):
        count, error = state
        return (error > 1e-8) & (count < 16)

    def newton(state):
        error = 0.0
        for i, unit in enumerate(scaled):
            guess = scratch[i]
            miss = identity - mm(unit, guess)
            scratch[i] = guess + mm(guess, miss)
            error = jnp.maximum(error, jnp.sum(miss * miss))
        return state[0] + 1, error

    _, error = lax.while_loop(more, newton, (0, jnp.float32(1.0)))

    @pl.when(jnp.logical_not(error <= 1e-8))
    def _():
        for i, unit in enumerate(scaled):
            scratch[i] = sweep(unit, row_id, column_id)

    return [scratch[i] * down * across for i, (down, across) in enumerate(scales)]


def finish_kernel(grams_ref, right_ref, basis_ref, solution_ref, residual_ref, scratch):
    size = grams_ref.shape[1]
    resid, energy, coupling, outer = [grams_ref[i * size : (i + 1) * size, :] for i in range(4)]
    identity = (
        lax.broadcasted_iota(jnp.int32, (size, size), 0) == lax.broadcasted_iota(jnp.int32, (size, size), 1)
    ).astype(jnp.float32)
    energy = 0.5 * (energy + energy.T)
    energy_inv, resid_inv = invert(scratch, energy, resid)
    step = mm(energy_inv, resid)
    shift = mm(energy, step)
    coupled = mm(coupling, step)
    next_gram = resid - shift - shift.T + mm(step, coupled, TRANS)
    grow = identity + mm(resid_inv, next_gram)
    cross = mm(grow, coupled, TRANS)
    next_energy = mm(grow, mm(energy, grow), TRANS) - cross - cross.T + mm(step, mm(outer, step), TRANS)
    next_energy = 0.5 * (next_energy + next_energy.T)
    (next_inv,) = invert(scratch, next_energy)
    next_step = mm(next_inv, next_gram)
    near = step + mm(grow, next_step)
    far = mm(step, next_step)
    weights = jnp.concatenate([near.T, -far.T], axis=1)
    planes, comps = basis_ref.shape[1:3]
    for p in range(planes):
        for c in range(comps):
            block = right_ref.shape[2:]
            ahead = mm(weights, jnp.concatenate([basis_ref[0, p, c], basis_ref[2, p, c]]))
            drop = mm(weights, jnp.concatenate([basis_ref[1, p, c], basis_ref[3, p, c]]))
            solution_ref[c, p] = ahead.T.reshape(block)
            residual_ref[c, p] = right_ref[c, p] - drop.T.reshape(block)


def finish(grams, right_side, basis):
    vmem = pl.BlockSpec(memory_space=pltpu.VMEM)
    return tuple(
        pl.pallas_call(
            finish_kernel,
            out_shape=[jax.ShapeDtypeStruct(right_side.shape, jnp.float32)] * 2,
            in_specs=[vmem] * 3,
            out_specs=[vmem] * 2,
            scratch_shapes=[pltpu.VMEM((2, grams.shape[1], grams.shape[1]), jnp.float32)],
            name="finish",
        )(grams, right_side, basis)
    )


CHANNELS = 12
LOWER, UPPER, BOTH = 0, 1, 2
SLOTS = len(lower_offsets)
PHASES = 6


def krylov_kernel(
    z_lo_count, z_hi_count, right_ref, stiff_diag_ref, stiff_ref, fsai_diag_ref, fsai_ref, kept_ref, total_ref, out_ref,
    vec, edge, rim_out, rim_in, low, high, low_out, low_in, grams, rs_buf, z_buf,
    halo_send, halo_recv, send, recv, z_send, z_recv, a_send, a_recv,
):
    size, lanes = vec.shape[3:]
    half, top, bottom = lanes // 2, pl.ds(0, size // 2), pl.ds(size // 2, size // 2)
    group, dev = lax.axis_index("group"), lax.axis_index("dev")
    group_count, dev_count = GROUP_Y * z_lo_count, DEV_XC * z_hi_count
    z_lo, y = group // GROUP_Y, group % GROUP_Y
    z_hi, xc = dev // DEV_XC, dev % DEV_XC
    me = y * DEV_XC + xc
    my_z = z_hi * z_lo_count + z_lo
    z_count = z_lo_count * z_hi_count
    has_prev_dev, has_next_dev = dev > 0, dev < dev_count - 1
    has_prev_group, has_next_group = group > 0, group < group_count - 1
    prev_dev, next_dev = (group, dev - 1), (group, dev + 1)
    prev_group, next_group = (group - 1, dev), (group + 1, dev)

    def plane_peer(step):
        peer = (me + step) % PLANE_PEERS
        return peer, (z_lo * GROUP_Y + peer // DEV_XC, z_hi * DEV_XC + peer % DEV_XC)

    def z_peer(step):
        peer = (my_z + step) % z_count
        return peer, (peer % z_lo_count * GROUP_Y + y, peer // z_lo_count * DEV_XC + xc)

    def clear(ref):
        ref[...] = jnp.zeros(ref.shape, ref.dtype)

    def clear_phases(*refs_of):
        def body(f, carry):
            for ref_of in refs_of:
                clear(ref_of(f))
            return carry
        lax.fori_loop(0, PHASES, body, 0)

    @pl.when(jnp.logical_not(has_prev_dev))
    def _():
        clear_phases(lambda f: rim_in.at[f, 0])
        clear(low_in.at[0])

    @pl.when(jnp.logical_not(has_next_dev))
    def _():
        clear_phases(lambda f: rim_in.at[f, 1])
        clear(low_in.at[1])

    @pl.when(jnp.logical_not(has_prev_group))
    def _():
        clear_phases(lambda f: rim_in.at[f, 0, 0], lambda f: rim_in.at[f, 1, 0], lambda f: vec.at[f, 0])

    @pl.when(jnp.logical_not(has_next_group))
    def _():
        clear_phases(lambda f: rim_in.at[f, 0, 3], lambda f: rim_in.at[f, 1, 3], lambda f: vec.at[f, 3])
        for k in range(2):
            clear(low_in.at[k, 2])
            clear(low.at[k, 2])

    barrier = pltpu.get_barrier_semaphore()

    def greet(place):
        pl.semaphore_signal(barrier, inc=1, device_id=place, device_id_type=MESH)

    def greet_all(count, peer_of):
        def body(step, carry):
            greet(peer_of(step)[1])
            return carry
        lax.fori_loop(1, count, body, 0)

    neighbours = (
        (group, (dev + dev_count - 1) % dev_count), (group, (dev + 1) % dev_count),
        ((group + group_count - 1) % group_count, dev), ((group + 1) % group_count, dev),
    )
    greet_all(PLANE_PEERS, plane_peer)
    greet_all(z_count, z_peer)
    for place in neighbours:
        greet(place)

    def left_of(shape):
        return lax.broadcasted_iota(jnp.int32, shape, len(shape) - 1) < half

    def swap(tile):
        return pltpu.roll(tile, half, axis=tile.ndim - 1)

    def turn(tile, step):
        return tile if step == 0 else pltpu.roll(tile, -step % lanes, axis=tile.ndim - 1)

    for p in range(2):
        for c in range(3):
            vec[0, p + 1, c] = right_ref[c, p].reshape(lanes, size).T

    left_low = left_of(low.shape[3:])
    left_half = left_of((size // 2, lanes))

    def pack_low(plane):
        low_out[0, plane] = jnp.where(left_low[None], swap(low[0, plane]), low[1, plane])
        low_out[1, plane] = jnp.where(left_low[None], low[0, plane], swap(low[1, plane]))

    column = lax.broadcasted_iota(jnp.int32, (1, lanes), 1) % half
    inside = {-1: column > 0, 0: column >= 0, 1: column < half - 1}
    for p in range(2):
        for slot, (_, _, c) in enumerate(lower_offsets):
            kept = jnp.where(inside[c], kept_ref[slot, pl.ds(p, 1), :].astype(jnp.float32), 0.0)
            for i in range(3):
                for j in range(3):
                    entry = pl.ds(i * 3 + j, 1)
                    low[0, p, slot, entry, :] = fsai_ref[i, j, slot, pl.ds(p, 1), :] * kept
                    low[1, p, slot, entry, :] = jnp.where(inside[c], stiff_ref[i, j, slot, pl.ds(p, 1), :], 0.0)
        pack_low(p)
    pl.semaphore_wait(barrier, PLANE_PEERS - 1 + z_count - 1 + len(neighbours))

    def route(number):
        along = {
            0: (next_dev, has_next_dev, has_prev_dev),
            1: (prev_dev, has_prev_dev, has_next_dev),
            2: (next_group, has_next_group, has_prev_group),
            3: (prev_group, has_prev_group, has_next_group),
        }
        if number < 2:
            return along[number]
        if number < 8:
            return along[2 if number < 5 else 3]
        place, to, come = along[number % 2]
        given = has_prev_group if number < 10 else has_next_group
        return place, to & given, come & given

    def move(source, target, phase, number, method):
        place, to, come = route(number)

        @pl.when(come if method == "wait_recv" else to)
        def _():
            copy = pltpu.make_async_remote_copy(
                src_ref=source, dst_ref=target,
                send_sem=halo_send.at[phase, number], recv_sem=halo_recv.at[phase, number],
                device_id=place, device_id_type=MESH,
            )
            getattr(copy, method)()

    def halo_plane(f, plane, c, method):
        number, source = (2, 2) if plane == 0 else (5, 1)
        move(vec.at[f, source, c], vec.at[f, plane, c], f, number + c, method)

    def halo_rim(f, side, kind, method):
        if side == 0:
            planes = pl.ds(2, 1) if kind == UPPER else pl.ds(1, 2)
        else:
            planes = pl.ds(1, 1) if kind == LOWER else pl.ds(1, 2)
        move(rim_out.at[f, side, planes], rim_in.at[f, side, planes], f, side, method)

    def halo_corner(f, plane, side, method, comps=pl.ds(0, 3)):
        number = (8 if plane == 0 else 10) + side
        move(rim_out.at[f, side, plane, comps], rim_in.at[f, side, plane, comps], f, number, method)

    def low_halo(number, method):
        if number == 5:
            move(low.at[:, 0], low.at[:, 2], PHASES, number, method)
            return
        side = number % 2
        planes = pl.ds(2, 1) if number > 5 else (pl.ds(1, 1) if side == 0 else pl.ds(0, 2))
        move(low_out.at[side, planes], low_in.at[side, planes], PHASES, number, method)

    def pack(f, plane, c):
        upper_rows, lower_rows = vec[f, plane, c, top, :], vec[f, plane, c, bottom, :]
        rim_out[f, 0, plane, c] = jnp.where(left_half, swap(upper_rows), lower_rows)
        rim_out[f, 1, plane, c] = jnp.where(left_half, upper_rows, swap(lower_rows))

    def unpack(f, plane):
        for c in range(3):
            before, after = rim_in[f, 0, plane, c], rim_in[f, 1, plane, c]
            edge[plane, c, top, :] = jnp.where(left_half, before, swap(after))
            edge[plane, c, bottom, :] = jnp.where(left_half, swap(before), after)

    outer_of = {LOWER: (0,), UPPER: (3,), BOTH: (0, 3)}

    def send_own(f, kind):
        for c in range(3):
            for plane in outer_of[kind]:
                halo_plane(f, plane, c, "start")
        for plane in (1, 2):
            for c in range(3):
                pack(f, plane, c)
        for side in (0, 1):
            halo_rim(f, side, kind, "start")

    def pass_planes(f, kind):
        for c in range(3):
            for plane in outer_of[kind]:
                halo_plane(f, plane, c, "wait_recv")
                pack(f, plane, c)
                for side in (0, 1):
                    halo_corner(f, plane, side, "start", pl.ds(c, 1))

    def take_rims(f, kind):
        for side in (0, 1):
            halo_rim(f, side, kind, "wait_recv")
        for plane in (1, 2):
            unpack(f, plane)

    def take_corners(f, kind):
        for plane in outer_of[kind]:
            for side in (0, 1):
                halo_corner(f, plane, side, "wait_recv")
            unpack(f, plane)

    def settle(f, kind):
        for side in (0, 1):
            halo_rim(f, side, kind, "wait_send")
            for plane in outer_of[kind]:
                halo_corner(f, plane, side, "wait_send")
        for plane in outer_of[kind]:
            for c in range(3):
                halo_plane(f, plane, c, "wait_send")

    def raise_coefs(k):
        def body(p, carry):
            for slot, (a, b, c) in enumerate(lower_offsets):
                at = p - a
                base = low[k, at, slot]
                if b == -1:
                    rim = low_in[1, at, slot]
                    base = jnp.where(left_low, swap(base), swap(rim) if k == 0 else rim)
                elif b == 1:
                    rim = low_in[0, at, slot]
                    base = jnp.where(left_low, rim if k == 0 else swap(rim), swap(base))
                high[k, p, slot] = turn(base, -c)
            return carry
        lax.fori_loop(0, 2, body, 0)

    rows_count = 32
    left = left_of((rows_count, lanes))
    diags = (fsai_diag_ref, stiff_diag_ref)

    def uses_of(parts):
        uses = {}
        for part, (upper, plane, diagonal) in enumerate(parts):
            sign = -1 if upper else 1
            slots = [(None, (0, 0, 0))] if diagonal else []
            for slot, (a, b, c) in slots + list(enumerate(lower_offsets)):
                at = uses.setdefault(plane + 1 + sign * a, {}).setdefault(sign * b, {})
                at.setdefault(sign * c, []).append((part, slot))
        return uses

    def accumulate(acc, v, k, parts, rows):
        for at, by_row in sorted(uses_of(parts).items()):
            for j in range(3):
                own = vec[v, at, j, rows, :]
                swapped = swap(own) if set(by_row) != {0} else None
                for b, by_column in sorted(by_row.items()):
                    tile = own
                    if b != 0:
                        outside = edge[at, j, rows, :]
                        tile = jnp.where(left, outside, swapped) if b < 0 else jnp.where(left, swapped, outside)
                    for c, users in sorted(by_column.items()):
                        value = turn(tile, c)
                        for part, slot in users:
                            upper, plane, _ = parts[part]
                            for i in range(3):
                                row, col = (j, i) if upper else (i, j)
                                if slot is None:
                                    block = diags[k][row, col, pl.ds(plane, 1), :]
                                else:
                                    table = high if upper else low
                                    block = table[k, plane, slot, pl.ds(row * 3 + col, 1), :]
                                acc[part][i] = acc[part][i] + block * value
        return acc

    def apply(v, target, k, parts, add):
        def body(step, carry):
            rows = pl.ds(pl.multiple_of(step * rows_count, rows_count), rows_count)
            if add:
                acc = [[vec[target, plane + 1, i, rows, :] for i in range(3)] for _, plane, _ in parts]
            else:
                acc = [[jnp.zeros((rows_count, lanes), jnp.float32)] * 3 for _ in parts]
            acc = accumulate(acc, v, k, parts, rows)
            for (_, plane, _), values in zip(parts, acc):
                for i in range(3):
                    vec[target, plane + 1, i, rows, :] = values[i]
            return carry

        lax.fori_loop(0, size // rows_count, body, 0, unroll=2)

    def across(v):
        return jnp.concatenate([vec[v, p, c] for p in (1, 2) for c in range(3)], axis=1)

    def gram(index, v, w):
        one = across(v)
        value = mm(one, one if w is None else across(w), ((1,), (1,)))
        count = value.shape[0] // grams.shape[1]
        grams[pl.ds(index * count, count)] = value.reshape((count,) + grams.shape[1:])

    send_own(0, LOWER)
    for number in (5, 0, 1):
        low_halo(number, "start")

    def round_body(t, carry):
        f = 3 * t

        @pl.when(t == 1)
        def _():
            send_own(f, LOWER)
            gram(1, 2, 3)

        pass_planes(f, LOWER)

        @pl.when(t == 0)
        def _():
            low_halo(5, "wait_recv")
            pack_low(2)
            for number in (10, 11):
                low_halo(number, "start")

        take_rims(f, LOWER)
        apply(f, f + 1, 0, ((False, 1, True),), False)
        take_corners(f, LOWER)
        apply(f, f + 1, 0, ((False, 0, True),), False)

        send_own(f + 1, UPPER)
        gram(2 * t, f + 1, None)

        @pl.when(t == 0)
        def _():
            for number in (0, 1, 10, 11):
                low_halo(number, "wait_recv")
            raise_coefs(0)

        pass_planes(f + 1, UPPER)
        take_rims(f + 1, UPPER)
        apply(f + 1, f + 2, 0, ((True, 0, True),), False)
        take_corners(f + 1, UPPER)
        apply(f + 1, f + 2, 0, ((True, 1, True),), False)

        send_own(f + 2, BOTH)

        @pl.when(t == 0)
        def _():
            raise_coefs(1)

        pass_planes(f + 2, BOTH)
        take_rims(f + 2, BOTH)
        apply(f + 2, f + 3, 1, ((False, 1, True), (True, 0, False)), False)
        take_corners(f + 2, BOTH)
        apply(f + 2, f + 3, 1, ((False, 0, True), (True, 1, False)), True)

        settle(f, LOWER)
        settle(f + 1, UPPER)
        settle(f + 2, BOTH)
        return carry

    lax.fori_loop(0, 2, round_body, 0)
    for number in (5, 0, 1, 10, 11):
        low_halo(number, "wait_send")
    gram(3, 5, 6)

    def scatter(step):
        peer, place = plane_peer(step)
        return pltpu.make_async_remote_copy(
            src_ref=grams.at[peer], dst_ref=rs_buf.at[me], send_sem=send.at[step],
            recv_sem=recv.at[step], device_id=place, device_id_type=MESH,
        )

    def exchange(step):
        _, place = z_peer(step)
        return pltpu.make_async_remote_copy(
            src_ref=z_buf.at[my_z], dst_ref=z_buf.at[my_z], send_sem=z_send.at[step],
            recv_sem=z_recv.at[step], device_id=place, device_id_type=MESH,
        )

    def gather(step):
        _, place = plane_peer(step)
        return pltpu.make_async_remote_copy(
            src_ref=total_ref.at[me], dst_ref=total_ref.at[me], send_sem=a_send.at[step],
            recv_sem=a_recv.at[step], device_id=place, device_id_type=MESH,
        )

    def run(count, make, method):
        def body(step, carry):
            getattr(make(step), method)()
            return carry
        lax.fori_loop(1, count, body, 0)

    run(PLANE_PEERS, scatter, "start")
    rs_buf[me] = grams[me]
    for slot, v in enumerate((2, 3, 5, 6)):
        for p in range(2):
            out_ref[slot, p] = vec[v, p + 1]
    run(PLANE_PEERS, scatter, "wait_recv")
    z_buf[my_z] = jnp.sum(rs_buf[...], axis=0)
    run(z_count, exchange, "start")
    run(z_count, exchange, "wait_recv")
    total_ref[me] = jnp.sum(z_buf[...], axis=0)
    run(PLANE_PEERS, gather, "start")
    run(PLANE_PEERS, gather, "wait_recv")
    run(PLANE_PEERS, scatter, "wait_send")
    run(z_count, exchange, "wait_send")
    run(PLANE_PEERS, gather, "wait_send")


def krylov(right_side, *coefs):
    z_lo_count = lax.axis_size("group") // GROUP_Y
    z_hi_count = lax.axis_size("dev") // DEV_XC
    z_count = z_lo_count * z_hi_count
    comps, planes, rows, columns, size = right_side.shape
    lanes = rows * columns
    pieces = (PLANE_PEERS, 4 * size // PLANE_PEERS, size)
    vmem = pl.BlockSpec(memory_space=pltpu.VMEM)
    dma = pltpu.SemaphoreType.DMA

    def array(*shape):
        return pltpu.VMEM(shape, jnp.float32)

    total, vectors = pl.pallas_call(
        functools.partial(krylov_kernel, z_lo_count, z_hi_count),
        out_shape=[
            jax.ShapeDtypeStruct(pieces, jnp.float32),
            jax.ShapeDtypeStruct((4, planes, comps, size, lanes), jnp.float32),
        ],
        in_specs=[vmem] * (1 + len(coefs)),
        out_specs=[vmem] * 2,
        scratch_shapes=[
            array(7, 4, comps, size, lanes),
            array(4, comps, size, lanes),
            array(PHASES, 2, 4, comps, size // 2, lanes),
            array(PHASES, 2, 4, comps, size // 2, lanes),
            array(2, 3, SLOTS, 9, lanes),
            array(2, 2, SLOTS, 9, lanes),
            array(2, 3, SLOTS, 9, lanes),
            array(2, 3, SLOTS, 9, lanes),
            array(*pieces),
            array(*pieces),
            array(z_count, *pieces[1:]),
            dma((PHASES + 1, CHANNELS)), dma((PHASES + 1, CHANNELS)),
            dma((PLANE_PEERS,)), dma((PLANE_PEERS,)),
            dma((z_count,)), dma((z_count,)),
            dma((PLANE_PEERS,)), dma((PLANE_PEERS,)),
        ],
        compiler_params=pltpu.CompilerParams(collective_id=0, has_side_effects=True),
        name="krylov",
    )(right_side, *coefs)
    return total.reshape(4 * size, size), vectors


def per_device(right_side, *coefs):
    grams, basis = krylov(right_side, *coefs)
    return finish(grams, right_side, basis)


def solution(mesh):
    return jax.shard_map(
        per_device,
        mesh=mesh,
        in_specs=(
            P(None, "group", "dev", None, None),
            P(None, None, "group", "dev"),
            P(None, None, None, "group", "dev"),
            P(None, None, "group", "dev"),
            P(None, None, None, "group", "dev"),
            P(None, "group", "dev"),
        ),
        out_specs=(P(None, "group", "dev", None, None), P(None, "group", "dev", None, None)),
        check_vma=False,
    )
```

```python
import functools

import jax
import jax.numpy as jnp
from jax import lax
from jax.experimental import pallas as pl
from jax.experimental.pallas import tpu as pltpu
from jax.sharding import PartitionSpec as P

MESH = pl.DeviceIdType.MESH
highest = lax.Precision.HIGHEST
GROUP_Y = 4
DEV_XC = 8
PLANE_PEERS = GROUP_Y * DEV_XC
lower_offsets = [(0, 0, -1), (0, -1, -1), (0, -1, 0), (0, -1, 1)] + [
    (-1, row_step, column_step) for row_step in (-1, 0, 1) for column_step in (-1, 0, 1)
]


def mm(left, right, dims=((1,), (0,))):
    return lax.dot_general(left, right, (dims, ((), ())), precision=highest, preferred_element_type=jnp.float32)


TRANS = ((0,), (0,))


def sweep(matrix, row_id, column_id):
    def body(k, m):
        on_row, on_column = row_id == k, column_id == k
        row = jnp.sum(jnp.where(on_row, m, 0.0), axis=0, keepdims=True)
        column = jnp.sum(jnp.where(on_column, m, 0.0), axis=1, keepdims=True)
        pivot = jnp.sum(jnp.where(on_row & on_column, m, 0.0), axis=(0, 1), keepdims=True)
        row = jnp.where(on_column[:1], 1.0, row) / pivot
        swept = jnp.where(on_column, 0.0, m) - column * row
        return jnp.where(on_row, jnp.broadcast_to(row, m.shape), swept)

    return lax.fori_loop(0, matrix.shape[0], body, matrix)


def invert(scratch, *matrices):
    size = matrices[0].shape[0]
    row_id = lax.broadcasted_iota(jnp.int32, (size, size), 0)
    column_id = lax.broadcasted_iota(jnp.int32, (size, size), 1)
    eye = row_id == column_id
    identity = eye.astype(jnp.float32)
    scales, scaled = [], []
    for i, m in enumerate(matrices):
        diag = jnp.where(eye, m, 0.0)
        down = lax.rsqrt(jnp.sum(diag, axis=1, keepdims=True))
        across = lax.rsqrt(jnp.sum(diag, axis=0, keepdims=True))
        scales.append((down, across))
        unit = m * down * across
        scaled.append(unit)
        bound = jnp.max(jnp.sum(jnp.abs(unit), axis=0, keepdims=True), axis=1, keepdims=True)
        gain = 2.0 / (1.0 + bound)
        scratch[i] = gain * (2.0 * identity - gain * unit)

    def more(state):
        count, error = state
        return (error > 1e-8) & (count < 16)

    def newton(state):
        error = 0.0
        for i, unit in enumerate(scaled):
            guess = scratch[i]
            miss = identity - mm(unit, guess)
            scratch[i] = guess + mm(guess, miss)
            error = jnp.maximum(error, jnp.sum(miss * miss))
        return state[0] + 1, error

    _, error = lax.while_loop(more, newton, (0, jnp.float32(1.0)))

    @pl.when(jnp.logical_not(error <= 1e-8))
    def _():
        for i, unit in enumerate(scaled):
            scratch[i] = sweep(unit, row_id, column_id)

    return [scratch[i] * down * across for i, (down, across) in enumerate(scales)]


def finish_kernel(grams_ref, right_ref, basis_ref, solution_ref, residual_ref, scratch):
    size = grams_ref.shape[2]
    row_id = lax.broadcasted_iota(jnp.int32, (size, size), 0)
    column_id = lax.broadcasted_iota(jnp.int32, (size, size), 1)
    identity = (row_id == column_id).astype(jnp.float32)
    packed = grams_ref[:, :-1, :].reshape(2 * size, size)

    def split(i):
        pair, diag = packed[i * size : (i + 1) * size, :], grams_ref[i, -1:, :]
        first = jnp.where(row_id >= column_id, pair, pair.T)
        second = jnp.where(row_id < column_id, pair, pair.T)
        return first, jnp.where(row_id == column_id, diag, second)

    (resid, energy), (coupling, outer) = split(0), split(1)
    energy_inv, resid_inv = invert(scratch, energy, resid)
    step = mm(energy_inv, resid)
    shift = mm(energy, step)
    coupled = mm(coupling, step)
    next_gram = resid - shift - shift.T + mm(step, coupled, TRANS)
    grow = identity + mm(resid_inv, next_gram)
    cross = mm(grow, coupled, TRANS)
    next_energy = mm(grow, mm(energy, grow), TRANS) - cross - cross.T + mm(step, mm(outer, step), TRANS)
    next_energy = 0.5 * (next_energy + next_energy.T)
    (next_inv,) = invert(scratch, next_energy)
    next_step = mm(next_inv, next_gram)
    near = step + mm(grow, next_step)
    far = mm(step, next_step)
    weights = jnp.concatenate([near.T, -far.T], axis=1)
    planes, comps = basis_ref.shape[1:3]
    for p in range(planes):
        for c in range(comps):
            block = right_ref.shape[2:]
            ahead = mm(weights, jnp.concatenate([basis_ref[0, p, c], basis_ref[2, p, c]]))
            drop = mm(weights, jnp.concatenate([basis_ref[1, p, c], basis_ref[3, p, c]]))
            solution_ref[c, p] = ahead.T.reshape(block)
            residual_ref[c, p] = right_ref[c, p] - drop.T.reshape(block)


def finish(grams, right_side, basis):
    vmem = pl.BlockSpec(memory_space=pltpu.VMEM)
    return tuple(
        pl.pallas_call(
            finish_kernel,
            out_shape=[jax.ShapeDtypeStruct(right_side.shape, jnp.float32)] * 2,
            in_specs=[vmem] * 3,
            out_specs=[vmem] * 2,
            scratch_shapes=[pltpu.VMEM((2, grams.shape[2], grams.shape[2]), jnp.float32)],
            name="finish",
        )(grams, right_side, basis)
    )


CHANNELS = 8
LOWER, UPPER, BOTH = 0, 1, 2
SLOTS = len(lower_offsets)
PARTS = 2
PHASES = 6 * PARTS


def krylov_kernel(
    z_lo_count, z_hi_count, right_ref, stiff_diag_ref, stiff_ref, fsai_diag_ref, fsai_ref, kept_ref, total_ref, out_ref,
    vec, edge, rim_out, rim_in, low, high, low_out, low_in, mats, grams, rs_buf, z_buf,
    halo_send, halo_recv, send, recv, z_send, z_recv, a_send, a_recv,
):
    size, lanes = vec.shape[3:]
    half, top, bottom = lanes // 2, pl.ds(0, size // 2), pl.ds(size // 2, size // 2)
    group, dev = lax.axis_index("group"), lax.axis_index("dev")
    group_count, dev_count = GROUP_Y * z_lo_count, DEV_XC * z_hi_count
    z_lo, y = group // GROUP_Y, group % GROUP_Y
    z_hi, xc = dev // DEV_XC, dev % DEV_XC
    me = y * DEV_XC + xc
    my_z = z_hi * z_lo_count + z_lo
    z_count = z_lo_count * z_hi_count
    has_prev_dev, has_next_dev = dev > 0, dev < dev_count - 1
    has_prev_group, has_next_group = group > 0, group < group_count - 1
    prev_dev, next_dev = (group, dev - 1), (group, dev + 1)
    prev_group, next_group = (group - 1, dev), (group + 1, dev)

    def plane_peer(step):
        peer = (me + step) % PLANE_PEERS
        return peer, (z_lo * GROUP_Y + peer // DEV_XC, z_hi * DEV_XC + peer % DEV_XC)

    def z_peer(step):
        peer = (my_z + step) % z_count
        return peer, (peer % z_lo_count * GROUP_Y + y, peer // z_lo_count * DEV_XC + xc)

    def clear(ref):
        ref[...] = jnp.zeros(ref.shape, ref.dtype)

    def clear_phases(*refs_of):
        def body(f, carry):
            for ref_of in refs_of:
                clear(ref_of(f))
            return carry
        lax.fori_loop(0, PHASES, body, 0)

    @pl.when(jnp.logical_not(has_prev_dev))
    def _():
        clear_phases(lambda f: rim_in.at[f, 0])
        clear(low_in.at[0])

    @pl.when(jnp.logical_not(has_next_dev))
    def _():
        clear_phases(lambda f: rim_in.at[f, 1])
        clear(low_in.at[1])

    @pl.when(jnp.logical_not(has_prev_group))
    def _():
        clear_phases(lambda f: rim_in.at[f, 0, 0], lambda f: rim_in.at[f, 1, 0], lambda f: vec.at[f, 0])

    @pl.when(jnp.logical_not(has_next_group))
    def _():
        clear_phases(lambda f: rim_in.at[f, 0, 3], lambda f: rim_in.at[f, 1, 3], lambda f: vec.at[f, 3])
        for k in range(2):
            clear(low_in.at[k, 2])
            clear(low.at[k, 2])

    barrier = pltpu.get_barrier_semaphore()

    def greet(place):
        pl.semaphore_signal(barrier, inc=1, device_id=place, device_id_type=MESH)

    def greet_all(count, peer_of):
        def body(step, carry):
            greet(peer_of(step)[1])
            return carry
        lax.fori_loop(1, count, body, 0)

    neighbours = (
        (group, (dev + dev_count - 1) % dev_count), (group, (dev + 1) % dev_count),
        ((group + group_count - 1) % group_count, dev), ((group + 1) % group_count, dev),
    )
    greet_all(PLANE_PEERS, plane_peer)
    greet_all(z_count, z_peer)
    for place in neighbours:
        greet(place)

    def left_of(shape):
        return lax.broadcasted_iota(jnp.int32, shape, len(shape) - 1) < half

    def swap(tile):
        return pltpu.roll(tile, half, axis=tile.ndim - 1)

    def turn(tile, step):
        return tile if step == 0 else pltpu.roll(tile, -step % lanes, axis=tile.ndim - 1)

    for p in range(2):
        for c in range(3):
            tile = right_ref[c, p].reshape(lanes, PARTS * size).T
            for h in range(PARTS):
                vec[h, p + 1, c] = tile[h * size : (h + 1) * size]

    left_low = left_of(low.shape[3:])
    left_half = left_of((size // 2, lanes))

    def pack_low(plane):
        low_out[0, plane] = jnp.where(left_low[None], swap(low[0, plane]), low[1, plane])
        low_out[1, plane] = jnp.where(left_low[None], low[0, plane], swap(low[1, plane]))

    column = lax.broadcasted_iota(jnp.int32, (1, lanes), 1) % half
    inside = {-1: column > 0, 0: column >= 0, 1: column < half - 1}
    for p in range(2):
        for slot, (_, _, c) in enumerate(lower_offsets):
            kept = jnp.where(inside[c], kept_ref[slot, pl.ds(p, 1), :].astype(jnp.float32), 0.0)
            for i in range(3):
                for j in range(3):
                    entry = pl.ds(i * 3 + j, 1)
                    low[0, p, slot, entry, :] = fsai_ref[i, j, slot, pl.ds(p, 1), :] * kept
                    low[1, p, slot, entry, :] = jnp.where(inside[c], stiff_ref[i, j, slot, pl.ds(p, 1), :], 0.0)
        pack_low(p)
    pl.semaphore_wait(barrier, PLANE_PEERS - 1 + z_count - 1 + len(neighbours))

    def route(number):
        along = {
            0: (next_dev, has_next_dev, has_prev_dev),
            1: (prev_dev, has_prev_dev, has_next_dev),
            2: (next_group, has_next_group, has_prev_group),
            3: (prev_group, has_prev_group, has_next_group),
        }
        if number < 2:
            return along[number]
        if number < 4:
            return along[number]
        place, to, come = along[number % 2]
        given = has_prev_group if number < 6 else has_next_group
        return place, to & given, come & given

    def move(source, target, phase, number, method):
        place, to, come = route(number)

        @pl.when(come if method == "wait_recv" else to)
        def _():
            copy = pltpu.make_async_remote_copy(
                src_ref=source, dst_ref=target,
                send_sem=halo_send.at[phase, number], recv_sem=halo_recv.at[phase, number],
                device_id=place, device_id_type=MESH,
            )
            getattr(copy, method)()

    def halo_plane(f, plane, method):
        number, source = (2, 2) if plane == 0 else (3, 1)
        move(vec.at[f, source], vec.at[f, plane], f, number, method)

    def halo_rim(f, side, kind, method):
        if side == 0:
            planes = pl.ds(2, 1) if kind == UPPER else pl.ds(1, 2)
        else:
            planes = pl.ds(1, 1) if kind == LOWER else pl.ds(1, 2)
        move(rim_out.at[f, side, planes], rim_in.at[f, side, planes], f, side, method)

    def halo_corner(f, plane, side, method):
        number = (4 if plane == 0 else 6) + side
        move(rim_out.at[f, side, plane], rim_in.at[f, side, plane], f, number, method)

    def low_halo(number, method):
        if number == 3:
            move(low.at[:, 0], low.at[:, 2], PHASES, number, method)
            return
        side = number % 2
        planes = pl.ds(2, 1) if number > 3 else (pl.ds(1, 1) if side == 0 else pl.ds(0, 2))
        move(low_out.at[side, planes], low_in.at[side, planes], PHASES, number, method)

    def pack(f, plane, c):
        upper_rows, lower_rows = vec[f, plane, c, top, :], vec[f, plane, c, bottom, :]
        rim_out[f, 0, plane, c] = jnp.where(left_half, swap(upper_rows), lower_rows)
        rim_out[f, 1, plane, c] = jnp.where(left_half, upper_rows, swap(lower_rows))

    def unpack(f, plane):
        for c in range(3):
            before, after = rim_in[f, 0, plane, c], rim_in[f, 1, plane, c]
            edge[plane, c, top, :] = jnp.where(left_half, before, swap(after))
            edge[plane, c, bottom, :] = jnp.where(left_half, swap(before), after)

    outer_of = {LOWER: (0,), UPPER: (3,), BOTH: (0, 3)}

    def send_own(f, kind):
        for plane in outer_of[kind]:
            halo_plane(f, plane, "start")
        for plane in (1, 2):
            for c in range(3):
                pack(f, plane, c)
        for side in (0, 1):
            halo_rim(f, side, kind, "start")

    def pass_planes(f, kind):
        for plane in outer_of[kind]:
            halo_plane(f, plane, "wait_recv")
            for c in range(3):
                pack(f, plane, c)
            for side in (0, 1):
                halo_corner(f, plane, side, "start")

    def take_rims(f, kind):
        for side in (0, 1):
            halo_rim(f, side, kind, "wait_recv")
        for plane in (1, 2):
            unpack(f, plane)

    def take_corners(f, kind):
        for plane in outer_of[kind]:
            for side in (0, 1):
                halo_corner(f, plane, side, "wait_recv")
            unpack(f, plane)

    def settle(f, kind):
        for side in (0, 1):
            halo_rim(f, side, kind, "wait_send")
            for plane in outer_of[kind]:
                halo_corner(f, plane, side, "wait_send")
        for plane in outer_of[kind]:
            halo_plane(f, plane, "wait_send")

    def raise_coefs(k):
        def body(p, carry):
            for slot, (a, b, c) in enumerate(lower_offsets):
                at = p - a
                base = low[k, at, slot]
                if b == -1:
                    rim = low_in[1, at, slot]
                    base = jnp.where(left_low, swap(base), swap(rim) if k == 0 else rim)
                elif b == 1:
                    rim = low_in[0, at, slot]
                    base = jnp.where(left_low, rim if k == 0 else swap(rim), swap(base))
                high[k, p, slot] = turn(base, -c)
            return carry
        lax.fori_loop(0, 2, body, 0)

    rows_count = 32
    left = left_of((rows_count, lanes))
    diags = (fsai_diag_ref, stiff_diag_ref)

    def uses_of(parts):
        uses = {}
        for part, (upper, plane, diagonal) in enumerate(parts):
            sign = -1 if upper else 1
            slots = [(None, (0, 0, 0))] if diagonal else []
            for slot, (a, b, c) in slots + list(enumerate(lower_offsets)):
                at = uses.setdefault(plane + 1 + sign * a, {}).setdefault(sign * b, {})
                at.setdefault(sign * c, []).append((part, slot))
        return uses

    def accumulate(acc, v, k, parts, rows):
        for at, by_row in sorted(uses_of(parts).items()):
            for j in range(3):
                own = vec[v, at, j, rows, :]
                swapped = swap(own) if set(by_row) != {0} else None
                for b, by_column in sorted(by_row.items()):
                    tile = own
                    if b != 0:
                        outside = edge[at, j, rows, :]
                        tile = jnp.where(left, outside, swapped) if b < 0 else jnp.where(left, swapped, outside)
                    for c, users in sorted(by_column.items()):
                        value = turn(tile, c)
                        for part, slot in users:
                            upper, plane, _ = parts[part]
                            for i in range(3):
                                row, col = (j, i) if upper else (i, j)
                                if slot is None:
                                    block = diags[k][row, col, pl.ds(plane, 1), :]
                                else:
                                    table = high if upper else low
                                    block = table[k, plane, slot, pl.ds(row * 3 + col, 1), :]
                                acc[part][i] = acc[part][i] + block * value
        return acc

    def apply(v, target, k, parts, add):
        def body(step, carry):
            rows = pl.ds(pl.multiple_of(step * rows_count, rows_count), rows_count)
            if add:
                acc = [[vec[target, plane + 1, i, rows, :] for i in range(3)] for _, plane, _ in parts]
            else:
                acc = [[jnp.zeros((rows_count, lanes), jnp.float32)] * 3 for _ in parts]
            acc = accumulate(acc, v, k, parts, rows)
            for (_, plane, _), values in zip(parts, acc):
                for i in range(3):
                    vec[target, plane + 1, i, rows, :] = values[i]
            return carry

        lax.fori_loop(0, size // rows_count, body, 0)

    def across(v):
        parts = [
            jnp.concatenate([vec[PARTS * v + h, p, c] for p in (1, 2) for c in range(3)], axis=1) for h in range(PARTS)
        ]
        return jnp.concatenate(parts, axis=0)

    def gram(index, v, w):
        one = across(v)
        mats[index] = mm(one, one if w is None else across(w), ((1,), (1,)))

    def each_part(step):
        def body(h, carry):
            step(h)
            return carry
        lax.fori_loop(0, PARTS, body, 0)

    def operate(v, k, kind, then):
        early, late = {
            LOWER: (((False, 1, True),), ((False, 0, True),)),
            UPPER: (((True, 0, True),), ((True, 1, True),)),
            BOTH: (((False, 1, True), (True, 0, False)), ((False, 0, True), (True, 1, False))),
        }[kind]

        def step(h):
            f, target = PARTS * v + h, PARTS * (v + 1) + h
            take_rims(f, kind)
            apply(f, target, k, early, False)
            take_corners(f, kind)
            apply(f, target, k, late, kind == BOTH)
            then(target)

        each_part(step)

    each_part(lambda h: send_own(h, LOWER))
    for number in (3, 0, 1):
        low_halo(number, "start")

    def round_body(t, carry):
        v = 3 * t
        each_part(lambda h: pass_planes(PARTS * v + h, LOWER))

        @pl.when(t == 0)
        def _():
            low_halo(3, "wait_recv")
            pack_low(2)
            for number in (6, 7):
                low_halo(number, "start")

        operate(v, 0, LOWER, lambda f: send_own(f, UPPER))
        gram(2 * t, v + 1, None)

        @pl.when(t == 0)
        def _():
            for number in (0, 1, 6, 7):
                low_halo(number, "wait_recv")
            raise_coefs(0)

        each_part(lambda h: pass_planes(PARTS * (v + 1) + h, UPPER))
        operate(v + 1, 0, UPPER, lambda f: send_own(f, BOTH))

        @pl.when(t == 0)
        def _():
            raise_coefs(1)

        each_part(lambda h: pass_planes(PARTS * (v + 2) + h, BOTH))

        def again(f):
            @pl.when(t == 0)
            def _():
                send_own(f, LOWER)

        operate(v + 2, 1, BOTH, again)
        gram(2 * t + 1, v + 2, v + 3)

        def settle_part(h):
            settle(PARTS * v + h, LOWER)
            settle(PARTS * (v + 1) + h, UPPER)
            settle(PARTS * (v + 2) + h, BOTH)

        each_part(settle_part)
        return carry

    lax.fori_loop(0, 2, round_body, 0)
    for number in (3, 0, 1, 6, 7):
        low_halo(number, "wait_send")

    square = mats.shape[1:]
    row_id = lax.broadcasted_iota(jnp.int32, square, 0)
    column_id = lax.broadcasted_iota(jnp.int32, square, 1)
    count = square[0] // (grams.shape[1] - 1)
    grams[:, pl.ds(grams.shape[1] - 1, 1), :] = jnp.zeros((grams.shape[0], 1, square[1]), jnp.float32)
    for i in range(2):
        first, second = mats[2 * i], mats[2 * i + 1]
        pair = jnp.where(row_id >= column_id, first, second)
        grams[pl.ds(i * count, count), pl.ds(0, grams.shape[1] - 1), :] = pair.reshape(count, -1, square[1])
        diag = jnp.sum(jnp.where(row_id == column_id, second, 0.0), axis=0, keepdims=True)
        grams[i, pl.ds(grams.shape[1] - 1, 1), :] = diag

    def scatter(step):
        peer, place = plane_peer(step)
        return pltpu.make_async_remote_copy(
            src_ref=grams.at[peer], dst_ref=rs_buf.at[me], send_sem=send.at[step],
            recv_sem=recv.at[step], device_id=place, device_id_type=MESH,
        )

    def exchange(step):
        _, place = z_peer(step)
        return pltpu.make_async_remote_copy(
            src_ref=z_buf.at[my_z], dst_ref=z_buf.at[my_z], send_sem=z_send.at[step],
            recv_sem=z_recv.at[step], device_id=place, device_id_type=MESH,
        )

    def gather(step):
        _, place = plane_peer(step)
        return pltpu.make_async_remote_copy(
            src_ref=total_ref.at[me], dst_ref=total_ref.at[me], send_sem=a_send.at[step],
            recv_sem=a_recv.at[step], device_id=place, device_id_type=MESH,
        )

    def run(count, make, method):
        def body(step, carry):
            getattr(make(step), method)()
            return carry
        lax.fori_loop(1, count, body, 0)

    run(PLANE_PEERS, scatter, "start")
    rs_buf[me] = grams[me]
    for slot, v in enumerate((2, 3, 5, 6)):
        for p in range(2):
            for h in range(PARTS):
                out_ref[slot, p, :, pl.ds(h * size, size), :] = vec[PARTS * v + h, p + 1]
    run(PLANE_PEERS, scatter, "wait_recv")
    z_buf[my_z] = jnp.sum(rs_buf[...], axis=0)
    run(z_count, exchange, "start")
    run(z_count, exchange, "wait_recv")
    total_ref[me] = jnp.sum(z_buf[...], axis=0)
    run(PLANE_PEERS, gather, "start")
    run(PLANE_PEERS, gather, "wait_recv")
    run(PLANE_PEERS, scatter, "wait_send")
    run(z_count, exchange, "wait_send")
    run(PLANE_PEERS, gather, "wait_send")


def krylov(right_side, *coefs):
    z_lo_count = lax.axis_size("group") // GROUP_Y
    z_hi_count = lax.axis_size("dev") // DEV_XC
    z_count = z_lo_count * z_hi_count
    comps, planes, rows, columns, size = right_side.shape
    lanes = rows * columns
    pieces = (PLANE_PEERS, 2 * size // PLANE_PEERS + 1, size)
    part = size // PARTS
    vmem = pl.BlockSpec(memory_space=pltpu.VMEM)
    dma = pltpu.SemaphoreType.DMA

    def array(*shape):
        return pltpu.VMEM(shape, jnp.float32)

    total, vectors = pl.pallas_call(
        functools.partial(krylov_kernel, z_lo_count, z_hi_count),
        out_shape=[
            jax.ShapeDtypeStruct(pieces, jnp.float32),
            jax.ShapeDtypeStruct((4, planes, comps, size, lanes), jnp.float32),
        ],
        in_specs=[vmem] * (1 + len(coefs)),
        out_specs=[vmem] * 2,
        scratch_shapes=[
            array(7 * PARTS, 4, comps, part, lanes),
            array(4, comps, part, lanes),
            array(PHASES, 2, 4, comps, part // 2, lanes),
            array(PHASES, 2, 4, comps, part // 2, lanes),
            array(2, 3, SLOTS, 9, lanes),
            array(2, 2, SLOTS, 9, lanes),
            array(2, 3, SLOTS, 9, lanes),
            array(2, 3, SLOTS, 9, lanes),
            array(4, size, size),
            array(*pieces),
            array(*pieces),
            array(z_count, *pieces[1:]),
            dma((PHASES + 1, CHANNELS)), dma((PHASES + 1, CHANNELS)),
            dma((PLANE_PEERS,)), dma((PLANE_PEERS,)),
            dma((z_count,)), dma((z_count,)),
            dma((PLANE_PEERS,)), dma((PLANE_PEERS,)),
        ],
        compiler_params=pltpu.CompilerParams(collective_id=0, has_side_effects=True),
        name="krylov",
    )(right_side, *coefs)
    return total, vectors


def per_device(right_side, *coefs):
    grams, basis = krylov(right_side, *coefs)
    return finish(grams, right_side, basis)


def solution(mesh):
    return jax.shard_map(
        per_device,
        mesh=mesh,
        in_specs=(
            P(None, "group", "dev", None, None),
            P(None, None, "group", "dev"),
            P(None, None, None, "group", "dev"),
            P(None, None, "group", "dev"),
            P(None, None, None, "group", "dev"),
            P(None, "group", "dev"),
        ),
        out_specs=(P(None, "group", "dev", None, None), P(None, "group", "dev", None, None)),
        check_vma=False,
    )
```

```python
import functools

import jax
import jax.numpy as jnp
from jax import lax
from jax.experimental import pallas as pl
from jax.experimental.pallas import tpu as pltpu
from jax.sharding import PartitionSpec as P

MESH = pl.DeviceIdType.MESH
highest = lax.Precision.HIGHEST
GROUP_Y = 4
DEV_XC = 8
PLANE_PEERS = GROUP_Y * DEV_XC
lower_offsets = [(0, 0, -1), (0, -1, -1), (0, -1, 0), (0, -1, 1)] + [
    (-1, row_step, column_step) for row_step in (-1, 0, 1) for column_step in (-1, 0, 1)
]


def mm(left, right, dims=((1,), (0,))):
    return lax.dot_general(left, right, (dims, ((), ())), precision=highest, preferred_element_type=jnp.float32)


TRANS = ((0,), (0,))


def sweep(matrix, row_id, column_id):
    def body(k, m):
        on_row, on_column = row_id == k, column_id == k
        row = jnp.sum(jnp.where(on_row, m, 0.0), axis=0, keepdims=True)
        column = jnp.sum(jnp.where(on_column, m, 0.0), axis=1, keepdims=True)
        pivot = jnp.sum(jnp.where(on_row & on_column, m, 0.0), axis=(0, 1), keepdims=True)
        row = jnp.where(on_column[:1], 1.0, row) / pivot
        swept = jnp.where(on_column, 0.0, m) - column * row
        return jnp.where(on_row, jnp.broadcast_to(row, m.shape), swept)

    return lax.fori_loop(0, matrix.shape[0], body, matrix)


def invert(scratch, *matrices):
    size = matrices[0].shape[0]
    row_id = lax.broadcasted_iota(jnp.int32, (size, size), 0)
    column_id = lax.broadcasted_iota(jnp.int32, (size, size), 1)
    eye = row_id == column_id
    identity = eye.astype(jnp.float32)
    scales, scaled = [], []
    for i, m in enumerate(matrices):
        diag = jnp.where(eye, m, 0.0)
        down = lax.rsqrt(jnp.sum(diag, axis=1, keepdims=True))
        across = lax.rsqrt(jnp.sum(diag, axis=0, keepdims=True))
        scales.append((down, across))
        unit = m * down * across
        scaled.append(unit)
        bound = jnp.max(jnp.sum(jnp.abs(unit), axis=0, keepdims=True), axis=1, keepdims=True)
        gain = 2.0 / (1.0 + bound)
        scratch[i] = gain * (2.0 * identity - gain * unit)

    def more(state):
        count, error = state
        return (error > 1e-8) & (count < 16)

    def newton(state):
        error = 0.0
        for i, unit in enumerate(scaled):
            guess = scratch[i]
            miss = identity - mm(unit, guess)
            scratch[i] = guess + mm(guess, miss)
            error = jnp.maximum(error, jnp.sum(miss * miss))
        return state[0] + 1, error

    _, error = lax.while_loop(more, newton, (0, jnp.float32(1.0)))

    @pl.when(jnp.logical_not(error <= 1e-8))
    def _():
        for i, unit in enumerate(scaled):
            scratch[i] = sweep(unit, row_id, column_id)

    return [scratch[i] * down * across for i, (down, across) in enumerate(scales)]


def finish_kernel(
    grams_ref, right_hbm, basis_hbm, solution_hbm, residual_hbm, scratch, right_ref, basis_ref, solution_ref, residual_ref,
    in_sem, out_sem,
):
    loads = [
        pltpu.make_async_copy(basis_hbm, basis_ref, in_sem.at[0]),
        pltpu.make_async_copy(right_hbm, right_ref, in_sem.at[1]),
    ]
    for load in loads:
        load.start()
    size = grams_ref.shape[2]
    row_id = lax.broadcasted_iota(jnp.int32, (size, size), 0)
    column_id = lax.broadcasted_iota(jnp.int32, (size, size), 1)
    identity = (row_id == column_id).astype(jnp.float32)
    packed = grams_ref[:, :-1, :].reshape(2 * size, size)

    def split(i):
        pair, diag = packed[i * size : (i + 1) * size, :], grams_ref[i, -1:, :]
        first = jnp.where(row_id >= column_id, pair, pair.T)
        second = jnp.where(row_id < column_id, pair, pair.T)
        return first, jnp.where(row_id == column_id, diag, second)

    (resid, energy), (coupling, outer) = split(0), split(1)
    energy_inv, resid_inv = invert(scratch, energy, resid)
    step = mm(energy_inv, resid)
    shift = mm(energy, step)
    coupled = mm(coupling, step)
    next_gram = resid - shift - shift.T + mm(step, coupled, TRANS)
    grow = identity + mm(resid_inv, next_gram)
    cross = mm(grow, coupled, TRANS)
    next_energy = mm(grow, mm(energy, grow), TRANS) - cross - cross.T + mm(step, mm(outer, step), TRANS)
    next_energy = 0.5 * (next_energy + next_energy.T)
    (next_inv,) = invert(scratch, next_energy)
    next_step = mm(next_inv, next_gram)
    near = step + mm(grow, next_step)
    far = mm(step, next_step)
    weights = jnp.concatenate([near.T, -far.T], axis=1)
    for load in loads:
        load.wait()
    parts, planes, comps = basis_ref.shape[1:4]
    stores = []
    for c in range(comps):
        for p in range(planes):
            block = right_ref.shape[2:]

            def pair(one, other):
                return jnp.concatenate([basis_ref[slot, h, p, c] for slot in (one, other) for h in range(parts)])

            solution_ref[c, p] = mm(weights, pair(0, 2)).T.reshape(block)
            residual_ref[c, p] = right_ref[c, p] - mm(weights, pair(1, 3)).T.reshape(block)
        for k, (source, target) in enumerate(((solution_ref, solution_hbm), (residual_ref, residual_hbm))):
            stores.append(pltpu.make_async_copy(source.at[c], target.at[c], out_sem.at[k, c]))
            stores[-1].start()
    for store in stores:
        store.wait()


def finish(grams, right_side, basis):
    vmem, whole = pl.BlockSpec(memory_space=pltpu.VMEM), pl.BlockSpec(memory_space=pl.ANY)
    size = grams.shape[2]
    scratch_of = [(2, size, size), right_side.shape, basis.shape, right_side.shape, right_side.shape]
    return tuple(
        pl.pallas_call(
            finish_kernel,
            out_shape=[jax.ShapeDtypeStruct(right_side.shape, jnp.float32)] * 2,
            in_specs=[vmem, whole, whole],
            out_specs=[whole] * 2,
            scratch_shapes=[pltpu.VMEM(shape, jnp.float32) for shape in scratch_of]
            + [pltpu.SemaphoreType.DMA((2,)), pltpu.SemaphoreType.DMA((2, right_side.shape[0]))],
            name="finish",
        )(grams, right_side, basis)
    )


CHANNELS = 12
LOWER, UPPER, BOTH = 0, 1, 2
SLOTS = len(lower_offsets)
PARTS = 2
PHASES = 6 * PARTS


def krylov_kernel(
    z_lo_count, z_hi_count, right_ref, stiff_diag_ref, stiff_ref, fsai_diag_ref, fsai_ref, kept_ref, total_ref, out_ref,
    vec, edge, rim_out, rim_in, low, high, low_out, low_in, mats, grams, rs_buf, z_buf,
    halo_send, halo_recv, send, recv, z_send, z_recv, a_send, a_recv, out_sem,
):
    size, lanes = vec.shape[3:]
    half, top, bottom = lanes // 2, pl.ds(0, size // 2), pl.ds(size // 2, size // 2)
    group, dev = lax.axis_index("group"), lax.axis_index("dev")
    group_count, dev_count = GROUP_Y * z_lo_count, DEV_XC * z_hi_count
    z_lo, y = group // GROUP_Y, group % GROUP_Y
    z_hi, xc = dev // DEV_XC, dev % DEV_XC
    me = y * DEV_XC + xc
    my_z = z_hi * z_lo_count + z_lo
    z_count = z_lo_count * z_hi_count
    has_prev_dev, has_next_dev = dev > 0, dev < dev_count - 1
    has_prev_group, has_next_group = group > 0, group < group_count - 1
    near_prev, near_next = dev % DEV_XC > 0, dev % DEV_XC < DEV_XC - 1
    prev_dev, next_dev = (group, dev - 1), (group, dev + 1)
    prev_group, next_group = (group - 1, dev), (group + 1, dev)

    def plane_peer(step):
        peer = (me + step) % PLANE_PEERS
        return peer, (z_lo * GROUP_Y + peer // DEV_XC, z_hi * DEV_XC + peer % DEV_XC)

    def z_peer(step):
        peer = (my_z + step) % z_count
        return peer, (peer % z_lo_count * GROUP_Y + y, peer // z_lo_count * DEV_XC + xc)

    def clear(ref):
        ref[...] = jnp.zeros(ref.shape, ref.dtype)

    def clear_phases(*refs_of):
        def body(f, carry):
            for ref_of in refs_of:
                clear(ref_of(f))
            return carry
        lax.fori_loop(0, PHASES, body, 0)

    @pl.when(jnp.logical_not(has_prev_dev))
    def _():
        clear_phases(lambda f: rim_in.at[f, 0])
        clear(low_in.at[0])

    @pl.when(jnp.logical_not(has_next_dev))
    def _():
        clear_phases(lambda f: rim_in.at[f, 1])
        clear(low_in.at[1])

    @pl.when(jnp.logical_not(has_prev_group))
    def _():
        clear_phases(lambda f: rim_in.at[f, 0, 0], lambda f: rim_in.at[f, 1, 0], lambda f: vec.at[f, 0])

    @pl.when(jnp.logical_not(has_next_group))
    def _():
        clear_phases(lambda f: rim_in.at[f, 0, 3], lambda f: rim_in.at[f, 1, 3], lambda f: vec.at[f, 3])
        for k in range(2):
            clear(low_in.at[k, 2])
            clear(low.at[k, 2])

    barrier = pltpu.get_barrier_semaphore()

    def greet(place):
        pl.semaphore_signal(barrier, inc=1, device_id=place, device_id_type=MESH)

    def greet_all(count, peer_of):
        def body(step, carry):
            greet(peer_of(step)[1])
            return carry
        lax.fori_loop(1, count, body, 0)

    neighbours = (
        (group, (dev + dev_count - 1) % dev_count), (group, (dev + 1) % dev_count),
        ((group + group_count - 1) % group_count, dev), ((group + 1) % group_count, dev),
    )
    greet_all(PLANE_PEERS, plane_peer)
    greet_all(z_count, z_peer)
    for place in neighbours:
        greet(place)

    def left_of(shape):
        return lax.broadcasted_iota(jnp.int32, shape, len(shape) - 1) < half

    def swap(tile):
        return pltpu.roll(tile, half, axis=tile.ndim - 1)

    def turn(tile, step):
        return tile if step == 0 else pltpu.roll(tile, -step % lanes, axis=tile.ndim - 1)

    for p in range(2):
        for c in range(3):
            tile = right_ref[c, p].reshape(lanes, PARTS * size).T
            for h in range(PARTS):
                vec[h, p + 1, c] = tile[h * size : (h + 1) * size]

    left_low = left_of(low.shape[3:])
    left_half = left_of((size // 2, lanes))

    def pack_low(plane):
        low_out[0, plane] = jnp.where(left_low[None], swap(low[0, plane]), low[1, plane])
        low_out[1, plane] = jnp.where(left_low[None], low[0, plane], swap(low[1, plane]))

    column = lax.broadcasted_iota(jnp.int32, (1, lanes), 1) % half
    inside = {-1: column > 0, 0: column >= 0, 1: column < half - 1}
    for p in range(2):
        for slot, (_, _, c) in enumerate(lower_offsets):
            kept = jnp.where(inside[c], kept_ref[slot, pl.ds(p, 1), :].astype(jnp.float32), 0.0)
            for i in range(3):
                for j in range(3):
                    entry = pl.ds(i * 3 + j, 1)
                    low[0, p, slot, entry, :] = fsai_ref[i, j, slot, pl.ds(p, 1), :] * kept
                    low[1, p, slot, entry, :] = jnp.where(inside[c], stiff_ref[i, j, slot, pl.ds(p, 1), :], 0.0)
        pack_low(p)
    pl.semaphore_wait(barrier, PLANE_PEERS - 1 + z_count - 1 + len(neighbours))

    def route(number, own_way):
        along = {
            0: (next_dev, has_next_dev, has_prev_dev),
            1: (prev_dev, has_prev_dev, has_next_dev),
            2: (next_group, has_next_group, has_prev_group),
            3: (prev_group, has_prev_group, has_next_group),
        }
        if number < 2:
            return along[number]
        if number < 4:
            return along[number]
        place, to, come = along[number % 2]
        given = has_prev_group if number < 6 else has_next_group
        if own_way:
            to = to & (near_next if number % 2 == 0 else near_prev)
        return place, to & given, come & given

    def move(source, target, phase, number, method, own_way=False):
        place, to, come = route(number, own_way)

        @pl.when(come if method == "wait_recv" else to)
        def _():
            copy = pltpu.make_async_remote_copy(
                src_ref=source, dst_ref=target,
                send_sem=halo_send.at[phase, number], recv_sem=halo_recv.at[phase, number],
                device_id=place, device_id_type=MESH,
            )
            getattr(copy, method)()

    def halo_plane(f, plane, method):
        number, source = (2, 2) if plane == 0 else (3, 1)
        move(vec.at[f, source], vec.at[f, plane], f, number, method)

    def halo_rim(f, side, method):
        move(rim_out.at[f, side, pl.ds(1, 2)], rim_in.at[f, side, pl.ds(1, 2)], f, side, method)

    def halo_corner(f, plane, side, method):
        number = (4 if plane == 0 else 6) + side
        move(rim_out.at[f, side, plane], rim_in.at[f, side, plane], f, number, method, True)

    def far_corner(f, plane, side, method):
        place, exists = (next_group, has_next_group) if plane == 0 else (prev_group, has_prev_group)
        far = has_prev_dev & jnp.logical_not(near_prev) if side == 0 else has_next_dev & jnp.logical_not(near_next)
        number = (4 if plane == 0 else 6) + side

        @pl.when(exists & far)
        def _():
            copy = pltpu.make_async_remote_copy(
                src_ref=rim_in.at[f, side, 2 if plane == 0 else 1], dst_ref=rim_in.at[f, side, plane],
                send_sem=halo_send.at[f, number + 4], recv_sem=halo_recv.at[f, number],
                device_id=place, device_id_type=MESH,
            )
            getattr(copy, method)()

    def low_halo(number, method):
        if number == 3:
            move(low.at[:, 0], low.at[:, 2], PHASES, number, method)
            return
        side = number % 2
        planes = pl.ds(2, 1) if number > 3 else (pl.ds(1, 1) if side == 0 else pl.ds(0, 2))
        move(low_out.at[side, planes], low_in.at[side, planes], PHASES, number, method)

    def pack(f, plane, c):
        upper_rows, lower_rows = vec[f, plane, c, top, :], vec[f, plane, c, bottom, :]
        rim_out[f, 0, plane, c] = jnp.where(left_half, swap(upper_rows), lower_rows)
        rim_out[f, 1, plane, c] = jnp.where(left_half, upper_rows, swap(lower_rows))

    def unpack(f, plane):
        for c in range(3):
            before, after = rim_in[f, 0, plane, c], rim_in[f, 1, plane, c]
            edge[plane, c, top, :] = jnp.where(left_half, before, swap(after))
            edge[plane, c, bottom, :] = jnp.where(left_half, swap(before), after)

    outer_of = {LOWER: (0,), UPPER: (3,), BOTH: (0, 3)}

    def send_own(f, kind):
        for plane in outer_of[kind]:
            halo_plane(f, plane, "start")
        for plane in (1, 2):
            for c in range(3):
                pack(f, plane, c)
        for side in (0, 1):
            halo_rim(f, side, "start")

    def pass_planes(f, kind):
        for plane in outer_of[kind]:
            halo_plane(f, plane, "wait_recv")
            for c in range(3):
                pack(f, plane, c)
            for side in (0, 1):
                halo_corner(f, plane, side, "start")
        for side in (0, 1):
            halo_rim(f, side, "wait_recv")
            for plane in outer_of[kind]:
                far_corner(f, plane, side, "start")

    def take_rims(f):
        for plane in (1, 2):
            unpack(f, plane)

    def take_corners(f, kind):
        for plane in outer_of[kind]:
            for side in (0, 1):
                halo_corner(f, plane, side, "wait_recv")
            unpack(f, plane)

    def settle(f, kind):
        for side in (0, 1):
            halo_rim(f, side, "wait_send")
            for plane in outer_of[kind]:
                halo_corner(f, plane, side, "wait_send")
                far_corner(f, plane, side, "wait_send")
        for plane in outer_of[kind]:
            halo_plane(f, plane, "wait_send")

    def raise_coefs(k):
        def body(p, carry):
            for slot, (a, b, c) in enumerate(lower_offsets):
                at = p - a
                base = low[k, at, slot]
                if b == -1:
                    rim = low_in[1, at, slot]
                    base = jnp.where(left_low, swap(base), swap(rim) if k == 0 else rim)
                elif b == 1:
                    rim = low_in[0, at, slot]
                    base = jnp.where(left_low, rim if k == 0 else swap(rim), swap(base))
                high[k, p, slot] = turn(base, -c)
            return carry
        lax.fori_loop(0, 2, body, 0)

    rows_count = 32
    left = left_of((rows_count, lanes))
    diags = (fsai_diag_ref, stiff_diag_ref)

    def uses_of(parts):
        uses = {}
        for part, (upper, plane, diagonal) in enumerate(parts):
            sign = -1 if upper else 1
            slots = [(None, (0, 0, 0))] if diagonal else []
            for slot, (a, b, c) in slots + list(enumerate(lower_offsets)):
                at = uses.setdefault(plane + 1 + sign * a, {}).setdefault(sign * b, {})
                at.setdefault(sign * c, []).append((part, slot))
        return uses

    def accumulate(acc, v, k, parts, rows):
        for at, by_row in sorted(uses_of(parts).items()):
            for j in range(3):
                own = vec[v, at, j, rows, :]
                swapped = swap(own) if set(by_row) != {0} else None
                for b, by_column in sorted(by_row.items()):
                    tile = own
                    if b != 0:
                        outside = edge[at, j, rows, :]
                        tile = jnp.where(left, outside, swapped) if b < 0 else jnp.where(left, swapped, outside)
                    for c, users in sorted(by_column.items()):
                        value = turn(tile, c)
                        for part, slot in users:
                            upper, plane, _ = parts[part]
                            for i in range(3):
                                row, col = (j, i) if upper else (i, j)
                                if slot is None:
                                    block = diags[k][row, col, pl.ds(plane, 1), :]
                                else:
                                    table = high if upper else low
                                    block = table[k, plane, slot, pl.ds(row * 3 + col, 1), :]
                                acc[part][i] = acc[part][i] + block * value
        return acc

    def apply(v, target, k, parts, add):
        def body(step, carry):
            rows = pl.ds(pl.multiple_of(step * rows_count, rows_count), rows_count)
            if add:
                acc = [[vec[target, plane + 1, i, rows, :] for i in range(3)] for _, plane, _ in parts]
            else:
                acc = [[jnp.zeros((rows_count, lanes), jnp.float32)] * 3 for _ in parts]
            acc = accumulate(acc, v, k, parts, rows)
            for (_, plane, _), values in zip(parts, acc):
                for i in range(3):
                    vec[target, plane + 1, i, rows, :] = values[i]
            return carry

        lax.fori_loop(0, size // rows_count, body, 0)

    def across(v):
        parts = [
            jnp.concatenate([vec[PARTS * v + h, p, c] for p in (1, 2) for c in range(3)], axis=1) for h in range(PARTS)
        ]
        return jnp.concatenate(parts, axis=0)

    def gram(index, v, w):
        one = across(v)
        mats[index] = mm(one, one if w is None else across(w), ((1,), (1,)))

    def emit(slot, v):
        return pltpu.make_async_copy(vec.at[pl.ds(PARTS * v, PARTS), pl.ds(1, 2)], out_ref.at[slot], out_sem.at[slot])

    def each_part(step):
        def body(h, carry):
            step(h)
            return carry
        lax.fori_loop(0, PARTS, body, 0)

    def operate(v, k, kind, then):
        early, late = {
            LOWER: (((False, 1, True),), ((False, 0, True),)),
            UPPER: (((True, 0, True),), ((True, 1, True),)),
            BOTH: (((False, 1, True), (True, 0, False)), ((False, 0, True), (True, 1, False))),
        }[kind]

        def step(h):
            f, target = PARTS * v + h, PARTS * (v + 1) + h
            take_rims(f)
            apply(f, target, k, early, False)
            take_corners(f, kind)
            apply(f, target, k, late, kind == BOTH)
            then(target)

        each_part(step)

    each_part(lambda h: send_own(h, LOWER))
    for number in (3, 0, 1):
        low_halo(number, "start")

    def round_body(t, carry):
        v = 3 * t
        each_part(lambda h: pass_planes(PARTS * v + h, LOWER))

        @pl.when(t == 0)
        def _():
            low_halo(3, "wait_recv")
            pack_low(2)
            for number in (6, 7):
                low_halo(number, "start")

        operate(v, 0, LOWER, lambda f: send_own(f, UPPER))
        gram(2 * t, v + 1, None)

        @pl.when(t == 0)
        def _():
            for number in (0, 1, 6, 7):
                low_halo(number, "wait_recv")
            raise_coefs(0)

        each_part(lambda h: pass_planes(PARTS * (v + 1) + h, UPPER))
        operate(v + 1, 0, UPPER, lambda f: send_own(f, BOTH))
        emit(2 * t, v + 2).start()

        @pl.when(t == 0)
        def _():
            raise_coefs(1)

        each_part(lambda h: pass_planes(PARTS * (v + 2) + h, BOTH))

        def again(f):
            @pl.when(t == 0)
            def _():
                send_own(f, LOWER)

        operate(v + 2, 1, BOTH, again)
        emit(2 * t + 1, v + 3).start()
        gram(2 * t + 1, v + 2, v + 3)

        def settle_part(h):
            settle(PARTS * v + h, LOWER)
            settle(PARTS * (v + 1) + h, UPPER)
            settle(PARTS * (v + 2) + h, BOTH)

        each_part(settle_part)
        return carry

    lax.fori_loop(0, 2, round_body, 0)
    for number in (3, 0, 1, 6, 7):
        low_halo(number, "wait_send")

    square = mats.shape[1:]
    row_id = lax.broadcasted_iota(jnp.int32, square, 0)
    column_id = lax.broadcasted_iota(jnp.int32, square, 1)
    count = square[0] // (grams.shape[1] - 1)
    grams[:, pl.ds(grams.shape[1] - 1, 1), :] = jnp.zeros((grams.shape[0], 1, square[1]), jnp.float32)
    for i in range(2):
        first, second = mats[2 * i], mats[2 * i + 1]
        pair = jnp.where(row_id >= column_id, first, second)
        grams[pl.ds(i * count, count), pl.ds(0, grams.shape[1] - 1), :] = pair.reshape(count, -1, square[1])
        diag = jnp.sum(jnp.where(row_id == column_id, second, 0.0), axis=0, keepdims=True)
        grams[i, pl.ds(grams.shape[1] - 1, 1), :] = diag

    def scatter(step):
        peer, place = plane_peer(step)
        return pltpu.make_async_remote_copy(
            src_ref=grams.at[peer], dst_ref=rs_buf.at[me], send_sem=send.at[step],
            recv_sem=recv.at[step], device_id=place, device_id_type=MESH,
        )

    def exchange(step):
        _, place = z_peer(step)
        return pltpu.make_async_remote_copy(
            src_ref=z_buf.at[my_z], dst_ref=z_buf.at[my_z], send_sem=z_send.at[step],
            recv_sem=z_recv.at[step], device_id=place, device_id_type=MESH,
        )

    def gather(step):
        _, place = plane_peer(step)
        return pltpu.make_async_remote_copy(
            src_ref=total_ref.at[me], dst_ref=total_ref.at[me], send_sem=a_send.at[step],
            recv_sem=a_recv.at[step], device_id=place, device_id_type=MESH,
        )

    def run(count, make, method):
        def body(step, carry):
            getattr(make(step), method)()
            return carry
        lax.fori_loop(1, count, body, 0)

    run(PLANE_PEERS, scatter, "start")
    rs_buf[me] = grams[me]
    run(PLANE_PEERS, scatter, "wait_recv")
    z_buf[my_z] = jnp.sum(rs_buf[...], axis=0)
    run(z_count, exchange, "start")
    run(z_count, exchange, "wait_recv")
    total_ref[me] = jnp.sum(z_buf[...], axis=0)
    run(PLANE_PEERS, gather, "start")
    run(PLANE_PEERS, gather, "wait_recv")
    run(PLANE_PEERS, scatter, "wait_send")
    run(z_count, exchange, "wait_send")
    run(PLANE_PEERS, gather, "wait_send")
    for slot, v in enumerate((2, 3, 5, 6)):
        emit(slot, v).wait()


def krylov(right_side, *coefs):
    z_lo_count = lax.axis_size("group") // GROUP_Y
    z_hi_count = lax.axis_size("dev") // DEV_XC
    z_count = z_lo_count * z_hi_count
    comps, planes, rows, columns, size = right_side.shape
    lanes = rows * columns
    pieces = (PLANE_PEERS, 2 * size // PLANE_PEERS + 1, size)
    part = size // PARTS
    vmem = pl.BlockSpec(memory_space=pltpu.VMEM)
    dma = pltpu.SemaphoreType.DMA

    def array(*shape):
        return pltpu.VMEM(shape, jnp.float32)

    total, vectors = pl.pallas_call(
        functools.partial(krylov_kernel, z_lo_count, z_hi_count),
        out_shape=[
            jax.ShapeDtypeStruct(pieces, jnp.float32),
            jax.ShapeDtypeStruct((4, PARTS, planes, comps, part, lanes), jnp.float32),
        ],
        in_specs=[vmem] * (1 + len(coefs)),
        out_specs=[vmem, pl.BlockSpec(memory_space=pl.ANY)],
        scratch_shapes=[
            array(7 * PARTS, 4, comps, part, lanes),
            array(4, comps, part, lanes),
            array(PHASES, 2, 4, comps, part // 2, lanes),
            array(PHASES, 2, 4, comps, part // 2, lanes),
            array(2, 3, SLOTS, 9, lanes),
            array(2, 2, SLOTS, 9, lanes),
            array(2, 3, SLOTS, 9, lanes),
            array(2, 3, SLOTS, 9, lanes),
            array(4, size, size),
            array(*pieces),
            array(*pieces),
            array(z_count, *pieces[1:]),
            dma((PHASES + 1, CHANNELS)), dma((PHASES + 1, CHANNELS)),
            dma((PLANE_PEERS,)), dma((PLANE_PEERS,)),
            dma((z_count,)), dma((z_count,)),
            dma((PLANE_PEERS,)), dma((PLANE_PEERS,)),
            dma((4,)),
        ],
        compiler_params=pltpu.CompilerParams(collective_id=0, has_side_effects=True),
        name="krylov",
    )(right_side, *coefs)
    return total, vectors


def per_device(right_side, *coefs):
    grams, basis = krylov(right_side, *coefs)
    return finish(grams, right_side, basis)


def solution(mesh):
    return jax.shard_map(
        per_device,
        mesh=mesh,
        in_specs=(
            P(None, "group", "dev", None, None),
            P(None, None, "group", "dev"),
            P(None, None, None, "group", "dev"),
            P(None, None, "group", "dev"),
            P(None, None, None, "group", "dev"),
            P(None, "group", "dev"),
        ),
        out_specs=(P(None, "group", "dev", None, None), P(None, "group", "dev", None, None)),
        check_vma=False,
    )
```

```python
import functools

import jax
import jax.numpy as jnp
from jax import lax
from jax.experimental import pallas as pl
from jax.experimental.pallas import tpu as pltpu
from jax.sharding import PartitionSpec as P

MESH = pl.DeviceIdType.MESH
highest = lax.Precision.HIGHEST
GROUP_Y = 4
DEV_XC = 8
PLANE_PEERS = GROUP_Y * DEV_XC
lower_offsets = [(0, 0, -1), (0, -1, -1), (0, -1, 0), (0, -1, 1)] + [
    (-1, row_step, column_step) for row_step in (-1, 0, 1) for column_step in (-1, 0, 1)
]


def mm(left, right, dims=((1,), (0,))):
    return lax.dot_general(left, right, (dims, ((), ())), precision=highest, preferred_element_type=jnp.float32)


TRANS = ((0,), (0,))


def halves(value):
    high = value.astype(jnp.bfloat16)
    return high, (value - high.astype(jnp.float32)).astype(jnp.bfloat16)


def mm_halves(left, right):
    (a, b), (c, d) = left, halves(right)
    return sum(jnp.dot(x, y, preferred_element_type=jnp.float32) for x, y in ((a, d), (b, c), (a, c)))


def sweep(matrix, row_id, column_id):
    def body(k, m):
        on_row, on_column = row_id == k, column_id == k
        row = jnp.sum(jnp.where(on_row, m, 0.0), axis=0, keepdims=True)
        column = jnp.sum(jnp.where(on_column, m, 0.0), axis=1, keepdims=True)
        pivot = jnp.sum(jnp.where(on_row & on_column, m, 0.0), axis=(0, 1), keepdims=True)
        row = jnp.where(on_column[:1], 1.0, row) / pivot
        swept = jnp.where(on_column, 0.0, m) - column * row
        return jnp.where(on_row, jnp.broadcast_to(row, m.shape), swept)

    return lax.fori_loop(0, matrix.shape[0], body, matrix)


def invert(scratch, *matrices):
    size = matrices[0].shape[0]
    row_id = lax.broadcasted_iota(jnp.int32, (size, size), 0)
    column_id = lax.broadcasted_iota(jnp.int32, (size, size), 1)
    eye = row_id == column_id
    identity = eye.astype(jnp.float32)
    scales, scaled = [], []
    for i, m in enumerate(matrices):
        diag = jnp.where(eye, m, 0.0)
        down = lax.rsqrt(jnp.sum(diag, axis=1, keepdims=True))
        across = lax.rsqrt(jnp.sum(diag, axis=0, keepdims=True))
        scales.append((down, across))
        unit = m * down * across
        scaled.append(unit)
        bound = jnp.max(jnp.sum(jnp.abs(unit), axis=0, keepdims=True), axis=1, keepdims=True)
        gain = 2.0 / (1.0 + bound)
        scratch[i] = gain * (2.0 * identity - gain * unit)

    def more(state):
        count, error = state
        return (error > 1e-8) & (count < 16)

    def newton(state):
        error = 0.0
        for i, unit in enumerate(scaled):
            guess = scratch[i]
            miss = identity - mm(unit, guess)
            scratch[i] = guess + mm(guess, miss)
            error = jnp.maximum(error, jnp.sum(miss * miss))
        return state[0] + 1, error

    _, error = lax.while_loop(more, newton, (0, jnp.float32(1.0)))

    @pl.when(jnp.logical_not(error <= 1e-8))
    def _():
        for i, unit in enumerate(scaled):
            scratch[i] = sweep(unit, row_id, column_id)

    return [scratch[i] * down * across for i, (down, across) in enumerate(scales)]


def finish_kernel(
    grams_ref, right_hbm, basis_hbm, solution_hbm, residual_hbm, scratch, right_ref, basis_ref, solution_ref, residual_ref,
    in_sem, out_sem,
):
    loads = [
        pltpu.make_async_copy(basis_hbm, basis_ref, in_sem.at[0]),
        pltpu.make_async_copy(right_hbm, right_ref, in_sem.at[1]),
    ]
    for load in loads:
        load.start()
    size = grams_ref.shape[2]
    row_id = lax.broadcasted_iota(jnp.int32, (size, size), 0)
    column_id = lax.broadcasted_iota(jnp.int32, (size, size), 1)
    identity = (row_id == column_id).astype(jnp.float32)
    packed = grams_ref[:, :-1, :].reshape(2 * size, size)

    def split(i):
        pair, diag = packed[i * size : (i + 1) * size, :], grams_ref[i, -1:, :]
        first = jnp.where(row_id >= column_id, pair, pair.T)
        second = jnp.where(row_id < column_id, pair, pair.T)
        return first, jnp.where(row_id == column_id, diag, second)

    (resid, energy), (coupling, outer) = split(0), split(1)
    energy_inv, resid_inv = invert(scratch, energy, resid)
    step = mm(energy_inv, resid)
    shift = mm(energy, step)
    coupled = mm(coupling, step)
    next_gram = resid - shift - shift.T + mm(step, coupled, TRANS)
    grow = identity + mm(resid_inv, next_gram)
    cross = mm(grow, coupled, TRANS)
    next_energy = mm(grow, mm(energy, grow), TRANS) - cross - cross.T + mm(step, mm(outer, step), TRANS)
    next_energy = 0.5 * (next_energy + next_energy.T)
    (next_inv,) = invert(scratch, next_energy)
    next_step = mm(next_inv, next_gram)
    near = step + mm(grow, next_step)
    far = mm(step, next_step)
    weights = halves(jnp.concatenate([near.T, -far.T], axis=1))
    for load in loads:
        load.wait()
    parts, planes, comps = basis_ref.shape[1:4]
    stores = []
    for c in range(comps):
        for p in range(planes):
            block = right_ref.shape[2:]

            def pair(one, other):
                return jnp.concatenate([basis_ref[slot, h, p, c] for slot in (one, other) for h in range(parts)])

            solution_ref[c, p] = mm_halves(weights, pair(0, 2)).T.reshape(block)
            residual_ref[c, p] = right_ref[c, p] - mm_halves(weights, pair(1, 3)).T.reshape(block)
        for k, (source, target) in enumerate(((solution_ref, solution_hbm), (residual_ref, residual_hbm))):
            stores.append(pltpu.make_async_copy(source.at[c], target.at[c], out_sem.at[k, c]))
            stores[-1].start()
    for store in stores:
        store.wait()


def finish(grams, right_side, basis):
    vmem, whole = pl.BlockSpec(memory_space=pltpu.VMEM), pl.BlockSpec(memory_space=pl.ANY)
    size = grams.shape[2]
    scratch_of = [(2, size, size), right_side.shape, basis.shape, right_side.shape, right_side.shape]
    return tuple(
        pl.pallas_call(
            finish_kernel,
            out_shape=[jax.ShapeDtypeStruct(right_side.shape, jnp.float32)] * 2,
            in_specs=[vmem, whole, whole],
            out_specs=[whole] * 2,
            scratch_shapes=[pltpu.VMEM(shape, jnp.float32) for shape in scratch_of]
            + [pltpu.SemaphoreType.DMA((2,)), pltpu.SemaphoreType.DMA((2, right_side.shape[0]))],
            name="finish",
        )(grams, right_side, basis)
    )


CHANNELS = 12
LOWER, UPPER, BOTH = 0, 1, 2
SLOTS = len(lower_offsets)
PARTS = 4
PHASES = 6 * PARTS


def krylov_kernel(
    z_lo_count, z_hi_count, right_ref, stiff_diag_ref, stiff_ref, fsai_diag_ref, fsai_ref, kept_ref, total_ref, out_ref,
    vec, edge, rim_out, rim_in, low, high, low_out, low_in, mats, grams, rs_buf, z_buf,
    halo_send, halo_recv, send, recv, z_send, z_recv, a_send, a_recv, out_sem,
):
    size, lanes = vec.shape[3:]
    half, top, bottom = lanes // 2, pl.ds(0, size // 2), pl.ds(size // 2, size // 2)
    group, dev = lax.axis_index("group"), lax.axis_index("dev")
    group_count, dev_count = GROUP_Y * z_lo_count, DEV_XC * z_hi_count
    z_lo, y = group // GROUP_Y, group % GROUP_Y
    z_hi, xc = dev // DEV_XC, dev % DEV_XC
    me = y * DEV_XC + xc
    my_z = z_hi * z_lo_count + z_lo
    z_count = z_lo_count * z_hi_count
    has_prev_dev, has_next_dev = dev > 0, dev < dev_count - 1
    has_prev_group, has_next_group = group > 0, group < group_count - 1
    near_prev, near_next = dev % DEV_XC > 0, dev % DEV_XC < DEV_XC - 1
    prev_dev, next_dev = (group, dev - 1), (group, dev + 1)
    prev_group, next_group = (group - 1, dev), (group + 1, dev)

    def plane_peer(step):
        peer = (me + step) % PLANE_PEERS
        return peer, (z_lo * GROUP_Y + peer // DEV_XC, z_hi * DEV_XC + peer % DEV_XC)

    def z_peer(step):
        peer = (my_z + step) % z_count
        return peer, (peer % z_lo_count * GROUP_Y + y, peer // z_lo_count * DEV_XC + xc)

    def clear(ref):
        ref[...] = jnp.zeros(ref.shape, ref.dtype)

    def clear_phases(*refs_of):
        def body(f, carry):
            for ref_of in refs_of:
                clear(ref_of(f))
            return carry
        lax.fori_loop(0, PHASES, body, 0)

    @pl.when(jnp.logical_not(has_prev_dev))
    def _():
        clear_phases(lambda f: rim_in.at[f, 0])
        clear(low_in.at[0])

    @pl.when(jnp.logical_not(has_next_dev))
    def _():
        clear_phases(lambda f: rim_in.at[f, 1])
        clear(low_in.at[1])

    @pl.when(jnp.logical_not(has_prev_group))
    def _():
        clear_phases(lambda f: rim_in.at[f, 0, 0], lambda f: rim_in.at[f, 1, 0], lambda f: vec.at[f, 0])

    @pl.when(jnp.logical_not(has_next_group))
    def _():
        clear_phases(lambda f: rim_in.at[f, 0, 3], lambda f: rim_in.at[f, 1, 3], lambda f: vec.at[f, 3])
        for k in range(2):
            clear(low_in.at[k, 2])
            clear(low.at[k, 2])

    barrier = pltpu.get_barrier_semaphore()

    def greet(place):
        pl.semaphore_signal(barrier, inc=1, device_id=place, device_id_type=MESH)

    def greet_all(count, peer_of):
        def body(step, carry):
            greet(peer_of(step)[1])
            return carry
        lax.fori_loop(1, count, body, 0)

    around = [(1, 0), (dev_count - 1, 0), (0, 1), (0, group_count - 1)]
    around += [(a, b) for a in (1, dev_count - 1) for b in (1, group_count - 1)]
    neighbours = [((group + b) % group_count, (dev + a) % dev_count) for a, b in around]
    greet_all(PLANE_PEERS, plane_peer)
    greet_all(z_count, z_peer)
    for place in neighbours:
        greet(place)

    def left_of(shape):
        return lax.broadcasted_iota(jnp.int32, shape, len(shape) - 1) < half

    def swap(tile):
        return pltpu.roll(tile, half, axis=tile.ndim - 1)

    def turn(tile, step):
        return tile if step == 0 else pltpu.roll(tile, -step % lanes, axis=tile.ndim - 1)

    for p in range(2):
        for c in range(3):
            tile = right_ref[c, p].reshape(lanes, PARTS * size).T
            for h in range(PARTS):
                vec[h, p + 1, c] = tile[h * size : (h + 1) * size]

    left_low = left_of(low.shape[3:])
    left_half = left_of((size // 2, lanes))

    def pack_low(plane):
        low_out[0, plane] = jnp.where(left_low[None], swap(low[0, plane]), low[1, plane])
        low_out[1, plane] = jnp.where(left_low[None], low[0, plane], swap(low[1, plane]))

    column = lax.broadcasted_iota(jnp.int32, (1, lanes), 1) % half
    inside = {-1: column > 0, 0: column >= 0, 1: column < half - 1}
    for p in range(2):
        for slot, (_, _, c) in enumerate(lower_offsets):
            kept = jnp.where(inside[c], kept_ref[slot, pl.ds(p, 1), :].astype(jnp.float32), 0.0)
            for i in range(3):
                for j in range(3):
                    entry = pl.ds(i * 3 + j, 1)
                    low[0, p, slot, entry, :] = fsai_ref[i, j, slot, pl.ds(p, 1), :] * kept
                    low[1, p, slot, entry, :] = jnp.where(inside[c], stiff_ref[i, j, slot, pl.ds(p, 1), :], 0.0)
        pack_low(p)
    pl.semaphore_wait(barrier, PLANE_PEERS - 1 + z_count - 1 + len(neighbours))

    def route(number, own_way):
        along = {
            0: (next_dev, has_next_dev, has_prev_dev),
            1: (prev_dev, has_prev_dev, has_next_dev),
            2: (next_group, has_next_group, has_prev_group),
            3: (prev_group, has_prev_group, has_next_group),
        }
        if number < 2:
            return along[number]
        if number < 4:
            return along[number]
        place, to, come = along[number % 2]
        given = has_prev_group if number < 6 else has_next_group
        if own_way:
            to = to & (near_next if number % 2 == 0 else near_prev)
        return place, to & given, come & given

    def move(source, target, phase, number, method, own_way=False):
        place, to, come = route(number, own_way)

        @pl.when(come if method == "wait_recv" else to)
        def _():
            copy = pltpu.make_async_remote_copy(
                src_ref=source, dst_ref=target,
                send_sem=halo_send.at[phase, number], recv_sem=halo_recv.at[phase, number],
                device_id=place, device_id_type=MESH,
            )
            getattr(copy, method)()

    def halo_plane(f, plane, method):
        number, source = (2, 2) if plane == 0 else (3, 1)
        move(vec.at[f, source], vec.at[f, plane], f, number, method)

    def halo_rim(f, side, kind, method):
        if side == 0:
            planes = pl.ds(2, 1) if kind == UPPER else pl.ds(1, 2)
        else:
            planes = pl.ds(1, 1) if kind == LOWER else pl.ds(1, 2)
        move(rim_out.at[f, side, planes], rim_in.at[f, side, planes], f, side, method)

    def halo_corner(f, plane, side, method):
        number = (4 if plane == 0 else 6) + side
        move(rim_out.at[f, side, plane], rim_in.at[f, side, plane], f, number, method, True)

    def far_corner(f, plane, side, method):
        ahead, on = (1, has_next_group) if plane == 0 else (-1, has_prev_group)
        far = has_next_dev & jnp.logical_not(near_next) if side == 0 else has_prev_dev & jnp.logical_not(near_prev)
        number = (4 if plane == 0 else 6) + side

        @pl.when(on & far)
        def _():
            copy = pltpu.make_async_remote_copy(
                src_ref=rim_out.at[f, side, 2 if plane == 0 else 1], dst_ref=rim_in.at[f, side, plane],
                send_sem=halo_send.at[f, number + 4], recv_sem=halo_recv.at[f, number],
                device_id=(group + ahead, dev + (1 if side == 0 else -1)), device_id_type=MESH,
            )
            getattr(copy, method)()

    def low_halo(number, method):
        if number == 3:
            move(low.at[:, 0], low.at[:, 2], PHASES, number, method)
            return
        side = number % 2
        planes = pl.ds(2, 1) if number > 3 else (pl.ds(1, 1) if side == 0 else pl.ds(0, 2))
        move(low_out.at[side, planes], low_in.at[side, planes], PHASES, number, method)

    def pack(f, plane, c):
        upper_rows, lower_rows = vec[f, plane, c, top, :], vec[f, plane, c, bottom, :]
        rim_out[f, 0, plane, c] = jnp.where(left_half, swap(upper_rows), lower_rows)
        rim_out[f, 1, plane, c] = jnp.where(left_half, upper_rows, swap(lower_rows))

    def unpack(f, plane):
        for c in range(3):
            before, after = rim_in[f, 0, plane, c], rim_in[f, 1, plane, c]
            edge[plane, c, top, :] = jnp.where(left_half, before, swap(after))
            edge[plane, c, bottom, :] = jnp.where(left_half, swap(before), after)

    outer_of = {LOWER: (0,), UPPER: (3,), BOTH: (0, 3)}

    def send_own(f, kind):
        for plane in outer_of[kind]:
            halo_plane(f, plane, "start")
        for plane in (1, 2):
            for c in range(3):
                pack(f, plane, c)
        for side in (0, 1):
            halo_rim(f, side, kind, "start")
            for plane in outer_of[kind]:
                far_corner(f, plane, side, "start")

    def pass_planes(f, kind):
        for plane in outer_of[kind]:
            halo_plane(f, plane, "wait_recv")
            for c in range(3):
                pack(f, plane, c)
            for side in (0, 1):
                halo_corner(f, plane, side, "start")

    def take_rims(f, kind):
        for side in (0, 1):
            halo_rim(f, side, kind, "wait_recv")
        for plane in (1, 2):
            unpack(f, plane)

    def take_corners(f, kind):
        for plane in outer_of[kind]:
            for side in (0, 1):
                halo_corner(f, plane, side, "wait_recv")
            unpack(f, plane)

    def settle(f, kind):
        for side in (0, 1):
            halo_rim(f, side, kind, "wait_send")
            for plane in outer_of[kind]:
                halo_corner(f, plane, side, "wait_send")
                far_corner(f, plane, side, "wait_send")
        for plane in outer_of[kind]:
            halo_plane(f, plane, "wait_send")

    def raise_coefs(k):
        def body(p, carry):
            for slot, (a, b, c) in enumerate(lower_offsets):
                at = p - a
                base = low[k, at, slot]
                if b == -1:
                    rim = low_in[1, at, slot]
                    base = jnp.where(left_low, swap(base), swap(rim) if k == 0 else rim)
                elif b == 1:
                    rim = low_in[0, at, slot]
                    base = jnp.where(left_low, rim if k == 0 else swap(rim), swap(base))
                high[k, p, slot] = turn(base, -c)
            return carry
        lax.fori_loop(0, 2, body, 0)

    rows_count = 32
    left = left_of((rows_count, lanes))
    diags = (fsai_diag_ref, stiff_diag_ref)

    def uses_of(parts):
        uses = {}
        for part, (upper, plane, diagonal) in enumerate(parts):
            sign = -1 if upper else 1
            slots = [(None, (0, 0, 0))] if diagonal else []
            for slot, (a, b, c) in slots + list(enumerate(lower_offsets)):
                at = uses.setdefault(plane + 1 + sign * a, {}).setdefault(sign * b, {})
                at.setdefault(sign * c, []).append((part, slot))
        return uses

    def accumulate(acc, v, k, parts, rows):
        for at, by_row in sorted(uses_of(parts).items()):
            for j in range(3):
                own = vec[v, at, j, rows, :]
                swapped = swap(own) if set(by_row) != {0} else None
                for b, by_column in sorted(by_row.items()):
                    tile = own
                    if b != 0:
                        outside = edge[at, j, rows, :]
                        tile = jnp.where(left, outside, swapped) if b < 0 else jnp.where(left, swapped, outside)
                    for c, users in sorted(by_column.items()):
                        value = turn(tile, c)
                        for part, slot in users:
                            upper, plane, _ = parts[part]
                            for i in range(3):
                                row, col = (j, i) if upper else (i, j)
                                if slot is None:
                                    block = diags[k][row, col, pl.ds(plane, 1), :]
                                else:
                                    table = high if upper else low
                                    block = table[k, plane, slot, pl.ds(row * 3 + col, 1), :]
                                acc[part][i] = acc[part][i] + block * value
        return acc

    def apply(v, target, k, parts, add):
        def body(step, carry):
            rows = pl.ds(pl.multiple_of(step * rows_count, rows_count), rows_count)
            if add:
                acc = [[vec[target, plane + 1, i, rows, :] for i in range(3)] for _, plane, _ in parts]
            else:
                acc = [[jnp.zeros((rows_count, lanes), jnp.float32)] * 3 for _ in parts]
            acc = accumulate(acc, v, k, parts, rows)
            for (_, plane, _), values in zip(parts, acc):
                for i in range(3):
                    vec[target, plane + 1, i, rows, :] = values[i]
            return carry

        lax.fori_loop(0, size // rows_count, body, 0)

    def across(v):
        parts = [
            jnp.concatenate([vec[PARTS * v + h, p, c] for p in (1, 2) for c in range(3)], axis=1) for h in range(PARTS)
        ]
        return jnp.concatenate(parts, axis=0)

    def gram(index, v, w):
        one = across(v)
        mats[index] = mm(one, one if w is None else across(w), ((1,), (1,)))

    def emit(slot, v):
        return pltpu.make_async_copy(vec.at[pl.ds(PARTS * v, PARTS), pl.ds(1, 2)], out_ref.at[slot], out_sem.at[slot])

    def each_part(step):
        def body(h, carry):
            step(h)
            return carry
        lax.fori_loop(0, PARTS, body, 0)

    def operate(v, k, kind, then):
        early, late = {
            LOWER: (((False, 1, True),), ((False, 0, True),)),
            UPPER: (((True, 0, True),), ((True, 1, True),)),
            BOTH: (((False, 1, True), (True, 0, False)), ((False, 0, True), (True, 1, False))),
        }[kind]

        def step(h):
            f, target = PARTS * v + h, PARTS * (v + 1) + h

            @pl.when(h < PARTS - 1)
            def _():
                pass_planes(f + 1, kind)

            take_rims(f, kind)
            apply(f, target, k, early, False)
            take_corners(f, kind)
            apply(f, target, k, late, kind == BOTH)
            then(target)

        each_part(step)

    each_part(lambda h: send_own(h, LOWER))
    for number in (3, 0, 1):
        low_halo(number, "start")

    def round_body(t, carry):
        v = 3 * t
        pass_planes(PARTS * v, LOWER)

        @pl.when(t == 0)
        def _():
            low_halo(3, "wait_recv")
            pack_low(2)
            for number in (6, 7):
                low_halo(number, "start")

        operate(v, 0, LOWER, lambda f: send_own(f, UPPER))
        gram(2 * t, v + 1, None)

        @pl.when(t == 0)
        def _():
            for number in (0, 1, 6, 7):
                low_halo(number, "wait_recv")
            raise_coefs(0)

        pass_planes(PARTS * (v + 1), UPPER)
        operate(v + 1, 0, UPPER, lambda f: send_own(f, BOTH))
        emit(2 * t, v + 2).start()

        @pl.when(t == 0)
        def _():
            raise_coefs(1)

        pass_planes(PARTS * (v + 2), BOTH)

        def again(f):
            @pl.when(t == 0)
            def _():
                send_own(f, LOWER)

        operate(v + 2, 1, BOTH, again)
        emit(2 * t + 1, v + 3).start()
        gram(2 * t + 1, v + 2, v + 3)
        return carry

    lax.fori_loop(0, 2, round_body, 0)
    square = mats.shape[1:]
    row_id = lax.broadcasted_iota(jnp.int32, square, 0)
    column_id = lax.broadcasted_iota(jnp.int32, square, 1)
    count = square[0] // (grams.shape[1] - 1)
    grams[:, pl.ds(grams.shape[1] - 1, 1), :] = jnp.zeros((grams.shape[0], 1, square[1]), jnp.float32)
    for i in range(2):
        first, second = mats[2 * i], mats[2 * i + 1]
        pair = jnp.where(row_id >= column_id, first, second)
        grams[pl.ds(i * count, count), pl.ds(0, grams.shape[1] - 1), :] = pair.reshape(count, -1, square[1])
        diag = jnp.sum(jnp.where(row_id == column_id, second, 0.0), axis=0, keepdims=True)
        grams[i, pl.ds(grams.shape[1] - 1, 1), :] = diag

    def scatter(step):
        peer, place = plane_peer(step)
        return pltpu.make_async_remote_copy(
            src_ref=grams.at[peer], dst_ref=rs_buf.at[me], send_sem=send.at[step],
            recv_sem=recv.at[step], device_id=place, device_id_type=MESH,
        )

    def exchange(step):
        _, place = z_peer(step)
        return pltpu.make_async_remote_copy(
            src_ref=z_buf.at[my_z], dst_ref=z_buf.at[my_z], send_sem=z_send.at[step],
            recv_sem=z_recv.at[step], device_id=place, device_id_type=MESH,
        )

    def gather(step):
        _, place = plane_peer(step)
        return pltpu.make_async_remote_copy(
            src_ref=total_ref.at[me], dst_ref=total_ref.at[me], send_sem=a_send.at[step],
            recv_sem=a_recv.at[step], device_id=place, device_id_type=MESH,
        )

    def run(count, make, method):
        def body(step, carry):
            getattr(make(step), method)()
            return carry
        lax.fori_loop(1, count, body, 0)

    run(PLANE_PEERS, scatter, "start")
    rs_buf[me] = grams[me]

    def settle_round(t, carry):
        def settle_part(h):
            for k, kind in enumerate((LOWER, UPPER, BOTH)):
                settle(PARTS * (3 * t + k) + h, kind)

        each_part(settle_part)
        return carry

    lax.fori_loop(0, 2, settle_round, 0)
    for number in (3, 0, 1, 6, 7):
        low_halo(number, "wait_send")
    run(PLANE_PEERS, scatter, "wait_recv")
    z_buf[my_z] = jnp.sum(rs_buf[...], axis=0)
    run(z_count, exchange, "start")
    run(PLANE_PEERS, scatter, "wait_send")
    run(z_count, exchange, "wait_recv")
    total_ref[me] = jnp.sum(z_buf[...], axis=0)
    run(PLANE_PEERS, gather, "start")
    run(z_count, exchange, "wait_send")
    for slot, v in enumerate((2, 3, 5, 6)):
        emit(slot, v).wait()
    run(PLANE_PEERS, gather, "wait_recv")
    run(PLANE_PEERS, gather, "wait_send")


def krylov(right_side, *coefs):
    z_lo_count = lax.axis_size("group") // GROUP_Y
    z_hi_count = lax.axis_size("dev") // DEV_XC
    z_count = z_lo_count * z_hi_count
    comps, planes, rows, columns, size = right_side.shape
    lanes = rows * columns
    pieces = (PLANE_PEERS, 2 * size // PLANE_PEERS + 1, size)
    part = size // PARTS
    vmem = pl.BlockSpec(memory_space=pltpu.VMEM)
    dma = pltpu.SemaphoreType.DMA

    def array(*shape):
        return pltpu.VMEM(shape, jnp.float32)

    total, vectors = pl.pallas_call(
        functools.partial(krylov_kernel, z_lo_count, z_hi_count),
        out_shape=[
            jax.ShapeDtypeStruct(pieces, jnp.float32),
            jax.ShapeDtypeStruct((4, PARTS, planes, comps, part, lanes), jnp.float32),
        ],
        in_specs=[vmem] * (1 + len(coefs)),
        out_specs=[vmem, pl.BlockSpec(memory_space=pl.ANY)],
        scratch_shapes=[
            array(7 * PARTS, 4, comps, part, lanes),
            array(4, comps, part, lanes),
            array(PHASES, 2, 4, comps, part // 2, lanes),
            array(PHASES, 2, 4, comps, part // 2, lanes),
            array(2, 3, SLOTS, 9, lanes),
            array(2, 2, SLOTS, 9, lanes),
            array(2, 3, SLOTS, 9, lanes),
            array(2, 3, SLOTS, 9, lanes),
            array(4, size, size),
            array(*pieces),
            array(*pieces),
            array(z_count, *pieces[1:]),
            dma((PHASES + 1, CHANNELS)), dma((PHASES + 1, CHANNELS)),
            dma((PLANE_PEERS,)), dma((PLANE_PEERS,)),
            dma((z_count,)), dma((z_count,)),
            dma((PLANE_PEERS,)), dma((PLANE_PEERS,)),
            dma((4,)),
        ],
        compiler_params=pltpu.CompilerParams(collective_id=0, has_side_effects=True),
        name="krylov",
    )(right_side, *coefs)
    return total, vectors


def per_device(right_side, *coefs):
    grams, basis = krylov(right_side, *coefs)
    return finish(grams, right_side, basis)


def solution(mesh):
    return jax.shard_map(
        per_device,
        mesh=mesh,
        in_specs=(
            P(None, "group", "dev", None, None),
            P(None, None, "group", "dev"),
            P(None, None, None, "group", "dev"),
            P(None, None, "group", "dev"),
            P(None, None, None, "group", "dev"),
            P(None, "group", "dev"),
        ),
        out_specs=(P(None, "group", "dev", None, None), P(None, "group", "dev", None, None)),
        check_vma=False,
    )
```

```python
import functools

import jax
import jax.numpy as jnp
from jax import lax
from jax.experimental import pallas as pl
from jax.experimental.pallas import tpu as pltpu
from jax.sharding import PartitionSpec as P

MESH = pl.DeviceIdType.MESH
highest = lax.Precision.HIGHEST
GROUP_Y = 4
DEV_XC = 8
PLANE_PEERS = GROUP_Y * DEV_XC
lower_offsets = [(0, 0, -1), (0, -1, -1), (0, -1, 0), (0, -1, 1)] + [
    (-1, row_step, column_step) for row_step in (-1, 0, 1) for column_step in (-1, 0, 1)
]


def mm(left, right, dims=((1,), (0,))):
    return lax.dot_general(left, right, (dims, ((), ())), precision=highest, preferred_element_type=jnp.float32)


TRANS = ((0,), (0,))


def halves(value):
    high = value.astype(jnp.bfloat16)
    return high, (value - high.astype(jnp.float32)).astype(jnp.bfloat16)


def mm_halves(left, right):
    (a, b), (c, d) = left, halves(right)
    return sum(jnp.dot(x, y, preferred_element_type=jnp.float32) for x, y in ((a, d), (b, c), (a, c)))


def sweep(matrix, row_id, column_id):
    def body(k, m):
        on_row, on_column = row_id == k, column_id == k
        row = jnp.sum(jnp.where(on_row, m, 0.0), axis=0, keepdims=True)
        column = jnp.sum(jnp.where(on_column, m, 0.0), axis=1, keepdims=True)
        pivot = jnp.sum(jnp.where(on_row & on_column, m, 0.0), axis=(0, 1), keepdims=True)
        row = jnp.where(on_column[:1], 1.0, row) / pivot
        swept = jnp.where(on_column, 0.0, m) - column * row
        return jnp.where(on_row, jnp.broadcast_to(row, m.shape), swept)

    return lax.fori_loop(0, matrix.shape[0], body, matrix)


def invert(scratch, *matrices):
    size = matrices[0].shape[0]
    row_id = lax.broadcasted_iota(jnp.int32, (size, size), 0)
    column_id = lax.broadcasted_iota(jnp.int32, (size, size), 1)
    eye = row_id == column_id
    identity = eye.astype(jnp.float32)
    scales, scaled = [], []
    for i, m in enumerate(matrices):
        diag = jnp.where(eye, m, 0.0)
        down = lax.rsqrt(jnp.sum(diag, axis=1, keepdims=True))
        across = lax.rsqrt(jnp.sum(diag, axis=0, keepdims=True))
        scales.append((down, across))
        unit = m * down * across
        scaled.append(unit)
        bound = jnp.max(jnp.sum(jnp.abs(unit), axis=0, keepdims=True), axis=1, keepdims=True)
        gain = 2.0 / (1.0 + bound)
        scratch[i] = gain * (2.0 * identity - gain * unit)

    def more(state):
        count, error = state
        return (error > 1e-7) & (count < 16)

    def newton(state):
        error = 0.0
        for i, unit in enumerate(scaled):
            guess = scratch[i]
            miss = identity - mm(unit, guess)
            scratch[i] = guess + mm_halves(halves(guess), miss)
            error = jnp.maximum(error, jnp.sum(miss * miss))
        return state[0] + 1, error

    _, error = lax.while_loop(more, newton, (0, jnp.float32(1.0)))

    @pl.when(jnp.logical_not(error <= 1e-7))
    def _():
        for i, unit in enumerate(scaled):
            scratch[i] = sweep(unit, row_id, column_id)

    return [scratch[i] * down * across for i, (down, across) in enumerate(scales)]


def finish_kernel(
    grams_ref, right_hbm, basis_hbm, solution_hbm, residual_hbm, scratch, right_ref, basis_ref, solution_ref, residual_ref,
    in_sem, out_sem,
):
    loads = [
        pltpu.make_async_copy(basis_hbm, basis_ref, in_sem.at[0]),
        pltpu.make_async_copy(right_hbm, right_ref, in_sem.at[1]),
    ]
    for load in loads:
        load.start()
    size = grams_ref.shape[2]
    row_id = lax.broadcasted_iota(jnp.int32, (size, size), 0)
    column_id = lax.broadcasted_iota(jnp.int32, (size, size), 1)
    identity = (row_id == column_id).astype(jnp.float32)
    packed = grams_ref[:, :-1, :].reshape(2 * size, size)

    def split(i):
        pair, diag = packed[i * size : (i + 1) * size, :], grams_ref[i, -1:, :]
        first = jnp.where(row_id >= column_id, pair, pair.T)
        second = jnp.where(row_id < column_id, pair, pair.T)
        return first, jnp.where(row_id == column_id, diag, second)

    (resid, energy), (coupling, outer) = split(0), split(1)
    energy_inv, resid_inv = invert(scratch, energy, resid)
    step = mm(energy_inv, resid)
    shift = mm(energy, step)
    coupled = mm(coupling, step)
    next_gram = resid - shift - shift.T + mm(step, coupled, TRANS)
    grow = identity + mm(resid_inv, next_gram)
    cross = mm(grow, coupled, TRANS)
    next_energy = mm(grow, mm(energy, grow), TRANS) - cross - cross.T + mm(step, mm(outer, step), TRANS)
    next_energy = 0.5 * (next_energy + next_energy.T)
    (next_inv,) = invert(scratch, next_energy)
    next_step = mm(next_inv, next_gram)
    near = step + mm(grow, next_step)
    far = mm(step, next_step)
    weights = halves(jnp.concatenate([near.T, -far.T], axis=1))
    for load in loads:
        load.wait()
    parts, planes, comps = basis_ref.shape[1:4]
    stores = []
    for c in range(comps):
        for p in range(planes):
            block = right_ref.shape[2:]

            def pair(one, other):
                return jnp.concatenate([basis_ref[slot, h, p, c] for slot in (one, other) for h in range(parts)])

            solution_ref[c, p] = mm_halves(weights, pair(0, 2)).T.reshape(block)
            residual_ref[c, p] = right_ref[c, p] - mm_halves(weights, pair(1, 3)).T.reshape(block)
        for k, (source, target) in enumerate(((solution_ref, solution_hbm), (residual_ref, residual_hbm))):
            stores.append(pltpu.make_async_copy(source.at[c], target.at[c], out_sem.at[k, c]))
            stores[-1].start()
    for store in stores:
        store.wait()


def finish(grams, right_side, basis):
    vmem, whole = pl.BlockSpec(memory_space=pltpu.VMEM), pl.BlockSpec(memory_space=pl.ANY)
    size = grams.shape[2]
    scratch_of = [(2, size, size), right_side.shape, basis.shape, right_side.shape, right_side.shape]
    return tuple(
        pl.pallas_call(
            finish_kernel,
            out_shape=[jax.ShapeDtypeStruct(right_side.shape, jnp.float32)] * 2,
            in_specs=[vmem, whole, whole],
            out_specs=[whole] * 2,
            scratch_shapes=[pltpu.VMEM(shape, jnp.float32) for shape in scratch_of]
            + [pltpu.SemaphoreType.DMA((2,)), pltpu.SemaphoreType.DMA((2, right_side.shape[0]))],
            name="finish",
        )(grams, right_side, basis)
    )


CHANNELS = 12
LOWER, UPPER, BOTH = 0, 1, 2
SLOTS = len(lower_offsets)
PARTS = 4
PHASES = 6 * PARTS


def krylov_kernel(
    z_lo_count, z_hi_count, right_ref, stiff_diag_ref, stiff_ref, fsai_diag_ref, fsai_ref, kept_ref, total_ref, out_ref,
    vec, edge, rim_out, rim_in, low, high, low_out, low_in, mats, grams, rs_buf, z_buf,
    halo_send, halo_recv, send, recv, z_send, z_recv, a_send, a_recv, out_sem,
):
    size, lanes = vec.shape[3:]
    half, top, bottom = lanes // 2, pl.ds(0, size // 2), pl.ds(size // 2, size // 2)
    group, dev = lax.axis_index("group"), lax.axis_index("dev")
    group_count, dev_count = GROUP_Y * z_lo_count, DEV_XC * z_hi_count
    z_lo, y = group // GROUP_Y, group % GROUP_Y
    z_hi, xc = dev // DEV_XC, dev % DEV_XC
    me = y * DEV_XC + xc
    my_z = z_hi * z_lo_count + z_lo
    z_count = z_lo_count * z_hi_count
    has_prev_dev, has_next_dev = dev > 0, dev < dev_count - 1
    has_prev_group, has_next_group = group > 0, group < group_count - 1
    near_prev, near_next = dev % DEV_XC > 0, dev % DEV_XC < DEV_XC - 1
    prev_dev, next_dev = (group, dev - 1), (group, dev + 1)
    prev_group, next_group = (group - 1, dev), (group + 1, dev)

    def plane_peer(step):
        peer = lax.rem(me + step, PLANE_PEERS)
        return peer, (z_lo * GROUP_Y + lax.div(peer, DEV_XC), z_hi * DEV_XC + lax.rem(peer, DEV_XC))

    def z_peer(step):
        peer = lax.rem(my_z + step, z_count)
        return peer, (lax.rem(peer, z_lo_count) * GROUP_Y + y, lax.div(peer, z_lo_count) * DEV_XC + xc)

    def clear(ref):
        ref[...] = jnp.zeros(ref.shape, ref.dtype)

    def clear_phases(*refs_of):
        def body(f, carry):
            for ref_of in refs_of:
                clear(ref_of(f))
            return carry
        lax.fori_loop(0, PHASES, body, 0)

    @pl.when(jnp.logical_not(has_prev_dev))
    def _():
        clear_phases(lambda f: rim_in.at[f, 0])
        clear(low_in.at[0])

    @pl.when(jnp.logical_not(has_next_dev))
    def _():
        clear_phases(lambda f: rim_in.at[f, 1])
        clear(low_in.at[1])

    @pl.when(jnp.logical_not(has_prev_group))
    def _():
        clear_phases(lambda f: rim_in.at[f, 0, 0], lambda f: rim_in.at[f, 1, 0], lambda f: vec.at[f, 0])

    @pl.when(jnp.logical_not(has_next_group))
    def _():
        clear_phases(lambda f: rim_in.at[f, 0, 3], lambda f: rim_in.at[f, 1, 3], lambda f: vec.at[f, 3])
        for k in range(2):
            clear(low_in.at[k, 2])
            clear(low.at[k, 2])

    barrier = pltpu.get_barrier_semaphore()

    def greet(place):
        pl.semaphore_signal(barrier, inc=1, device_id=place, device_id_type=MESH)

    def greet_all(count, peer_of):
        def body(step, carry):
            greet(peer_of(step)[1])
            return carry
        lax.fori_loop(1, count, body, 0, unroll=True)

    around = [(1, 0), (dev_count - 1, 0), (0, 1), (0, group_count - 1)]
    around += [(a, b) for a in (1, dev_count - 1) for b in (1, group_count - 1)]
    neighbours = [((group + b) % group_count, (dev + a) % dev_count) for a, b in around]
    greet_all(PLANE_PEERS, plane_peer)
    greet_all(z_count, z_peer)
    for place in neighbours:
        greet(place)

    def left_of(shape):
        return lax.broadcasted_iota(jnp.int32, shape, len(shape) - 1) < half

    def swap(tile):
        return pltpu.roll(tile, half, axis=tile.ndim - 1)

    def turn(tile, step):
        return tile if step == 0 else pltpu.roll(tile, -step % lanes, axis=tile.ndim - 1)

    for p in range(2):
        for c in range(3):
            tile = right_ref[c, p].reshape(lanes, PARTS * size).T
            for h in range(PARTS):
                vec[h, p + 1, c] = tile[h * size : (h + 1) * size]

    left_low = left_of(low.shape[3:])
    left_half = left_of((size // 2, lanes))

    def pack_low(plane):
        low_out[0, plane] = jnp.where(left_low[None], swap(low[0, plane]), low[1, plane])
        low_out[1, plane] = jnp.where(left_low[None], low[0, plane], swap(low[1, plane]))

    column = lax.broadcasted_iota(jnp.int32, (1, lanes), 1) % half
    inside = {-1: column > 0, 0: column >= 0, 1: column < half - 1}
    for p in range(2):
        for slot, (_, _, c) in enumerate(lower_offsets):
            kept = jnp.where(inside[c], kept_ref[slot, pl.ds(p, 1), :].astype(jnp.float32), 0.0)
            for i in range(3):
                for j in range(3):
                    entry = pl.ds(i * 3 + j, 1)
                    low[0, p, slot, entry, :] = fsai_ref[i, j, slot, pl.ds(p, 1), :] * kept
                    low[1, p, slot, entry, :] = jnp.where(inside[c], stiff_ref[i, j, slot, pl.ds(p, 1), :], 0.0)
        pack_low(p)
    pl.semaphore_wait(barrier, PLANE_PEERS - 1 + z_count - 1 + len(neighbours))

    def route(number, own_way):
        along = {
            0: (next_dev, has_next_dev, has_prev_dev),
            1: (prev_dev, has_prev_dev, has_next_dev),
            2: (next_group, has_next_group, has_prev_group),
            3: (prev_group, has_prev_group, has_next_group),
        }
        if number < 2:
            return along[number]
        if number < 4:
            return along[number]
        place, to, come = along[number % 2]
        given = has_prev_group if number < 6 else has_next_group
        if own_way:
            to = to & (near_next if number % 2 == 0 else near_prev)
        return place, to & given, come & given

    def move(source, target, phase, number, method, own_way=False):
        place, to, come = route(number, own_way)

        @pl.when(come if method == "wait_recv" else to)
        def _():
            copy = pltpu.make_async_remote_copy(
                src_ref=source, dst_ref=target,
                send_sem=halo_send.at[phase, number], recv_sem=halo_recv.at[phase, number],
                device_id=place, device_id_type=MESH,
            )
            getattr(copy, method)()

    def halo_plane(f, plane, method):
        number, source = (2, 2) if plane == 0 else (3, 1)
        move(vec.at[f, source], vec.at[f, plane], f, number, method)

    def halo_rim(f, side, kind, method):
        if side == 0:
            planes = pl.ds(2, 1) if kind == UPPER else pl.ds(1, 2)
        else:
            planes = pl.ds(1, 1) if kind == LOWER else pl.ds(1, 2)
        move(rim_out.at[f, side, planes], rim_in.at[f, side, planes], f, side, method)

    def halo_corner(f, plane, side, method):
        number = (4 if plane == 0 else 6) + side
        move(rim_out.at[f, side, plane], rim_in.at[f, side, plane], f, number, method, True)

    def far_corner(f, plane, side, method):
        ahead, on = (1, has_next_group) if plane == 0 else (-1, has_prev_group)
        far = has_next_dev & jnp.logical_not(near_next) if side == 0 else has_prev_dev & jnp.logical_not(near_prev)
        number = (4 if plane == 0 else 6) + side

        @pl.when(on & far)
        def _():
            copy = pltpu.make_async_remote_copy(
                src_ref=rim_out.at[f, side, 2 if plane == 0 else 1], dst_ref=rim_in.at[f, side, plane],
                send_sem=halo_send.at[f, number + 4], recv_sem=halo_recv.at[f, number],
                device_id=(group + ahead, dev + (1 if side == 0 else -1)), device_id_type=MESH,
            )
            getattr(copy, method)()

    def low_halo(number, method):
        if number == 3:
            move(low.at[:, 0], low.at[:, 2], PHASES, number, method)
            return
        side = number % 2
        planes = pl.ds(2, 1) if number > 3 else (pl.ds(1, 1) if side == 0 else pl.ds(0, 2))
        move(low_out.at[side, planes], low_in.at[side, planes], PHASES, number, method)

    def pack(f, plane, c):
        upper_rows, lower_rows = vec[f, plane, c, top, :], vec[f, plane, c, bottom, :]
        rim_out[f, 0, plane, c] = jnp.where(left_half, swap(upper_rows), lower_rows)
        rim_out[f, 1, plane, c] = jnp.where(left_half, upper_rows, swap(lower_rows))

    def unpack(f, plane):
        for c in range(3):
            before, after = rim_in[f, 0, plane, c], rim_in[f, 1, plane, c]
            edge[plane, c, top, :] = jnp.where(left_half, before, swap(after))
            edge[plane, c, bottom, :] = jnp.where(left_half, swap(before), after)

    outer_of = {LOWER: (0,), UPPER: (3,), BOTH: (0, 3)}

    def send_own(f, kind):
        for plane in outer_of[kind]:
            halo_plane(f, plane, "start")
        for plane in (1, 2):
            for c in range(3):
                pack(f, plane, c)
        for side in (0, 1):
            halo_rim(f, side, kind, "start")
            for plane in outer_of[kind]:
                far_corner(f, plane, side, "start")

    def pass_planes(f, kind):
        for plane in outer_of[kind]:
            halo_plane(f, plane, "wait_recv")
            for c in range(3):
                pack(f, plane, c)
            for side in (0, 1):
                halo_corner(f, plane, side, "start")

    def take_rims(f, kind):
        for side in (0, 1):
            halo_rim(f, side, kind, "wait_recv")
        for plane in (1, 2):
            unpack(f, plane)

    def take_corners(f, kind):
        for plane in outer_of[kind]:
            for side in (0, 1):
                halo_corner(f, plane, side, "wait_recv")
            unpack(f, plane)

    def settle(f, kind):
        for side in (0, 1):
            halo_rim(f, side, kind, "wait_send")
            for plane in outer_of[kind]:
                halo_corner(f, plane, side, "wait_send")
                far_corner(f, plane, side, "wait_send")
        for plane in outer_of[kind]:
            halo_plane(f, plane, "wait_send")

    def raise_coefs(k):
        def body(p, carry):
            for slot, (a, b, c) in enumerate(lower_offsets):
                at = p - a
                base = low[k, at, slot]
                if b == -1:
                    rim = low_in[1, at, slot]
                    base = jnp.where(left_low, swap(base), swap(rim) if k == 0 else rim)
                elif b == 1:
                    rim = low_in[0, at, slot]
                    base = jnp.where(left_low, rim if k == 0 else swap(rim), swap(base))
                high[k, p, slot] = turn(base, -c)
            return carry
        lax.fori_loop(0, 2, body, 0)

    rows_count = 32
    left = left_of((rows_count, lanes))
    diags = (fsai_diag_ref, stiff_diag_ref)

    def uses_of(parts):
        uses = {}
        for part, (upper, plane, diagonal) in enumerate(parts):
            sign = -1 if upper else 1
            slots = [(None, (0, 0, 0))] if diagonal else []
            for slot, (a, b, c) in slots + list(enumerate(lower_offsets)):
                at = uses.setdefault(plane + 1 + sign * a, {}).setdefault(sign * b, {})
                at.setdefault(sign * c, []).append((part, slot))
        return uses

    def accumulate(acc, v, k, parts, rows):
        for at, by_row in sorted(uses_of(parts).items()):
            for j in range(3):
                own = vec[v, at, j, rows, :]
                swapped = swap(own) if set(by_row) != {0} else None
                for b, by_column in sorted(by_row.items()):
                    tile = own
                    if b != 0:
                        outside = edge[at, j, rows, :]
                        tile = jnp.where(left, outside, swapped) if b < 0 else jnp.where(left, swapped, outside)
                    for c, users in sorted(by_column.items()):
                        value = turn(tile, c)
                        for part, slot in users:
                            upper, plane, _ = parts[part]
                            for i in range(3):
                                row, col = (j, i) if upper else (i, j)
                                if slot is None:
                                    block = diags[k][row, col, pl.ds(plane, 1), :]
                                else:
                                    table = high if upper else low
                                    block = table[k, plane, slot, pl.ds(row * 3 + col, 1), :]
                                acc[part][i] = acc[part][i] + block * value
        return acc

    def apply(v, target, k, parts, add):
        def body(step, carry):
            rows = pl.ds(pl.multiple_of(step * rows_count, rows_count), rows_count)
            if add:
                acc = [[vec[target, plane + 1, i, rows, :] for i in range(3)] for _, plane, _ in parts]
            else:
                acc = [[jnp.zeros((rows_count, lanes), jnp.float32)] * 3 for _ in parts]
            acc = accumulate(acc, v, k, parts, rows)
            for (_, plane, _), values in zip(parts, acc):
                for i in range(3):
                    vec[target, plane + 1, i, rows, :] = values[i]
            return carry

        lax.fori_loop(0, size // rows_count, body, 0)

    def across(v):
        parts = [
            jnp.concatenate([vec[PARTS * v + h, p, c] for p in (1, 2) for c in range(3)], axis=1) for h in range(PARTS)
        ]
        return jnp.concatenate(parts, axis=0)

    def gram(index, v, w):
        one = across(v)
        mats[index] = mm(one, one if w is None else across(w), ((1,), (1,)))

    def emit(slot, v):
        return pltpu.make_async_copy(vec.at[pl.ds(PARTS * v, PARTS), pl.ds(1, 2)], out_ref.at[slot], out_sem.at[slot])

    def each_part(step):
        def body(h, carry):
            step(h)
            return carry
        lax.fori_loop(0, PARTS, body, 0)

    def operate(v, k, kind, then):
        early, late = {
            LOWER: (((False, 1, True),), ((False, 0, True),)),
            UPPER: (((True, 0, True),), ((True, 1, True),)),
            BOTH: (((False, 1, True), (True, 0, False)), ((False, 0, True), (True, 1, False))),
        }[kind]

        def step(h):
            f, target = PARTS * v + h, PARTS * (v + 1) + h

            @pl.when(h < PARTS - 1)
            def _():
                pass_planes(f + 1, kind)

            take_rims(f, kind)
            apply(f, target, k, early, False)
            take_corners(f, kind)
            apply(f, target, k, late, kind == BOTH)
            then(target)

        each_part(step)

    each_part(lambda h: send_own(h, LOWER))
    for number in (3, 0, 1):
        low_halo(number, "start")

    def round_body(t, carry):
        v = 3 * t
        pass_planes(PARTS * v, LOWER)

        @pl.when(t == 0)
        def _():
            low_halo(3, "wait_recv")
            pack_low(2)
            for number in (6, 7):
                low_halo(number, "start")

        operate(v, 0, LOWER, lambda f: send_own(f, UPPER))
        gram(2 * t, v + 1, None)

        @pl.when(t == 0)
        def _():
            for number in (0, 1, 6, 7):
                low_halo(number, "wait_recv")
            raise_coefs(0)

        pass_planes(PARTS * (v + 1), UPPER)
        operate(v + 1, 0, UPPER, lambda f: send_own(f, BOTH))
        emit(2 * t, v + 2).start()

        @pl.when(t == 0)
        def _():
            raise_coefs(1)

        pass_planes(PARTS * (v + 2), BOTH)

        def again(f):
            @pl.when(t == 0)
            def _():
                send_own(f, LOWER)

        operate(v + 2, 1, BOTH, again)
        emit(2 * t + 1, v + 3).start()
        gram(2 * t + 1, v + 2, v + 3)
        return carry

    lax.fori_loop(0, 2, round_body, 0)
    square = mats.shape[1:]
    row_id = lax.broadcasted_iota(jnp.int32, square, 0)
    column_id = lax.broadcasted_iota(jnp.int32, square, 1)
    count = square[0] // (grams.shape[1] - 1)
    grams[:, pl.ds(grams.shape[1] - 1, 1), :] = jnp.zeros((grams.shape[0], 1, square[1]), jnp.float32)
    for i in range(2):
        first, second = mats[2 * i], mats[2 * i + 1]
        pair = jnp.where(row_id >= column_id, first, second)
        grams[pl.ds(i * count, count), pl.ds(0, grams.shape[1] - 1), :] = pair.reshape(count, -1, square[1])
        diag = jnp.sum(jnp.where(row_id == column_id, second, 0.0), axis=0, keepdims=True)
        grams[i, pl.ds(grams.shape[1] - 1, 1), :] = diag

    def scatter(step):
        peer, place = plane_peer(step)
        return pltpu.make_async_remote_copy(
            src_ref=grams.at[peer], dst_ref=rs_buf.at[me], send_sem=send.at[step],
            recv_sem=recv.at[step], device_id=place, device_id_type=MESH,
        )

    def exchange(step):
        _, place = z_peer(step)
        return pltpu.make_async_remote_copy(
            src_ref=z_buf.at[my_z], dst_ref=z_buf.at[my_z], send_sem=z_send.at[step],
            recv_sem=z_recv.at[step], device_id=place, device_id_type=MESH,
        )

    def gather(step):
        _, place = plane_peer(step)
        return pltpu.make_async_remote_copy(
            src_ref=total_ref.at[me], dst_ref=total_ref.at[me], send_sem=a_send.at[step],
            recv_sem=a_recv.at[step], device_id=place, device_id_type=MESH,
        )

    def run(count, make, method):
        def body(step, carry):
            getattr(make(step), method)()
            return carry
        lax.fori_loop(1, count, body, 0, unroll=method != "wait_send")

    run(PLANE_PEERS, scatter, "start")
    rs_buf[me] = grams[me]

    def settle_round(t, carry):
        def settle_part(h):
            for k, kind in enumerate((LOWER, UPPER, BOTH)):
                settle(PARTS * (3 * t + k) + h, kind)

        each_part(settle_part)
        return carry

    lax.fori_loop(0, 2, settle_round, 0)
    for number in (3, 0, 1, 6, 7):
        low_halo(number, "wait_send")
    run(PLANE_PEERS, scatter, "wait_recv")
    z_buf[my_z] = jnp.sum(rs_buf[...], axis=0)
    run(z_count, exchange, "start")
    run(PLANE_PEERS, scatter, "wait_send")
    run(z_count, exchange, "wait_recv")
    total_ref[me] = jnp.sum(z_buf[...], axis=0)
    run(PLANE_PEERS, gather, "start")
    run(z_count, exchange, "wait_send")
    for slot, v in enumerate((2, 3, 5, 6)):
        emit(slot, v).wait()
    run(PLANE_PEERS, gather, "wait_recv")
    run(PLANE_PEERS, gather, "wait_send")


def krylov(right_side, *coefs):
    z_lo_count = lax.axis_size("group") // GROUP_Y
    z_hi_count = lax.axis_size("dev") // DEV_XC
    z_count = z_lo_count * z_hi_count
    comps, planes, rows, columns, size = right_side.shape
    lanes = rows * columns
    pieces = (PLANE_PEERS, 2 * size // PLANE_PEERS + 1, size)
    part = size // PARTS
    vmem = pl.BlockSpec(memory_space=pltpu.VMEM)
    dma = pltpu.SemaphoreType.DMA

    def array(*shape):
        return pltpu.VMEM(shape, jnp.float32)

    total, vectors = pl.pallas_call(
        functools.partial(krylov_kernel, z_lo_count, z_hi_count),
        out_shape=[
            jax.ShapeDtypeStruct(pieces, jnp.float32),
            jax.ShapeDtypeStruct((4, PARTS, planes, comps, part, lanes), jnp.float32),
        ],
        in_specs=[vmem] * (1 + len(coefs)),
        out_specs=[vmem, pl.BlockSpec(memory_space=pl.ANY)],
        scratch_shapes=[
            array(7 * PARTS, 4, comps, part, lanes),
            array(4, comps, part, lanes),
            array(PHASES, 2, 4, comps, part // 2, lanes),
            array(PHASES, 2, 4, comps, part // 2, lanes),
            array(2, 3, SLOTS, 9, lanes),
            array(2, 2, SLOTS, 9, lanes),
            array(2, 3, SLOTS, 9, lanes),
            array(2, 3, SLOTS, 9, lanes),
            array(4, size, size),
            array(*pieces),
            array(*pieces),
            array(z_count, *pieces[1:]),
            dma((PHASES + 1, CHANNELS)), dma((PHASES + 1, CHANNELS)),
            dma((PLANE_PEERS,)), dma((PLANE_PEERS,)),
            dma((z_count,)), dma((z_count,)),
            dma((PLANE_PEERS,)), dma((PLANE_PEERS,)),
            dma((4,)),
        ],
        compiler_params=pltpu.CompilerParams(collective_id=0, has_side_effects=True),
        name="krylov",
    )(right_side, *coefs)
    return total, vectors


def per_device(right_side, *coefs):
    grams, basis = krylov(right_side, *coefs)
    return finish(grams, right_side, basis)


def solution(mesh):
    return jax.shard_map(
        per_device,
        mesh=mesh,
        in_specs=(
            P(None, "group", "dev", None, None),
            P(None, None, "group", "dev"),
            P(None, None, None, "group", "dev"),
            P(None, None, "group", "dev"),
            P(None, None, None, "group", "dev"),
            P(None, "group", "dev"),
        ),
        out_specs=(P(None, "group", "dev", None, None), P(None, "group", "dev", None, None)),
        check_vma=False,
    )
```

```python
import functools

import jax
import jax.numpy as jnp
from jax import lax
from jax.experimental import pallas as pl
from jax.experimental.pallas import tpu as pltpu
from jax.sharding import PartitionSpec as P

MESH = pl.DeviceIdType.MESH
highest = lax.Precision.HIGHEST
GROUP_Y = 4
DEV_XC = 8
PLANE_PEERS = GROUP_Y * DEV_XC
lower_offsets = [(0, 0, -1), (0, -1, -1), (0, -1, 0), (0, -1, 1)] + [
    (-1, row_step, column_step) for row_step in (-1, 0, 1) for column_step in (-1, 0, 1)
]


def mm(left, right, dims=((1,), (0,))):
    return lax.dot_general(left, right, (dims, ((), ())), precision=highest, preferred_element_type=jnp.float32)


TRANS = ((0,), (0,))


def halves(value):
    high = value.astype(jnp.bfloat16)
    return high, (value - high.astype(jnp.float32)).astype(jnp.bfloat16)


def mm_halves(left, right):
    (a, b), (c, d) = left, halves(right)
    return sum(jnp.dot(x, y, preferred_element_type=jnp.float32) for x, y in ((a, d), (b, c), (a, c)))


def sweep(matrix, row_id, column_id):
    def body(k, m):
        on_row, on_column = row_id == k, column_id == k
        row = jnp.sum(jnp.where(on_row, m, 0.0), axis=0, keepdims=True)
        column = jnp.sum(jnp.where(on_column, m, 0.0), axis=1, keepdims=True)
        pivot = jnp.sum(jnp.where(on_row & on_column, m, 0.0), axis=(0, 1), keepdims=True)
        row = jnp.where(on_column[:1], 1.0, row) / pivot
        swept = jnp.where(on_column, 0.0, m) - column * row
        return jnp.where(on_row, jnp.broadcast_to(row, m.shape), swept)

    return lax.fori_loop(0, matrix.shape[0], body, matrix)


def invert(scratch, *matrices):
    size = matrices[0].shape[0]
    row_id = lax.broadcasted_iota(jnp.int32, (size, size), 0)
    column_id = lax.broadcasted_iota(jnp.int32, (size, size), 1)
    eye = row_id == column_id
    identity = eye.astype(jnp.float32)
    scales, scaled = [], []
    for i, m in enumerate(matrices):
        diag = jnp.where(eye, m, 0.0)
        down = lax.rsqrt(jnp.sum(diag, axis=1, keepdims=True))
        across = lax.rsqrt(jnp.sum(diag, axis=0, keepdims=True))
        scales.append((down, across))
        unit = m * down * across
        scaled.append(unit)
        bound = jnp.max(jnp.sum(jnp.abs(unit), axis=0, keepdims=True), axis=1, keepdims=True)
        gain = 2.0 / (1.0 + bound)
        scratch[i] = gain * (2.0 * identity - gain * unit)

    def more(state):
        count, error = state
        return (error > 1e-7) & (count < 16)

    def newton(state):
        error = 0.0
        for i, unit in enumerate(scaled):
            guess = scratch[i]
            miss = identity - mm(unit, guess)
            scratch[i] = guess + mm_halves(halves(guess), miss)
            error = jnp.maximum(error, jnp.sum(miss * miss))
        return state[0] + 1, error

    _, error = lax.while_loop(more, newton, (0, jnp.float32(1.0)))

    @pl.when(jnp.logical_not(error <= 1e-7))
    def _():
        for i, unit in enumerate(scaled):
            scratch[i] = sweep(unit, row_id, column_id)

    return [scratch[i] * down * across for i, (down, across) in enumerate(scales)]


def finish_kernel(
    grams_ref, right_hbm, basis_hbm, solution_hbm, residual_hbm, scratch, right_ref, basis_ref, solution_ref, residual_ref,
    in_sem, out_sem,
):
    loads = [
        pltpu.make_async_copy(basis_hbm, basis_ref, in_sem.at[0]),
        pltpu.make_async_copy(right_hbm, right_ref, in_sem.at[1]),
    ]
    for load in loads:
        load.start()
    size = grams_ref.shape[2]
    row_id = lax.broadcasted_iota(jnp.int32, (size, size), 0)
    column_id = lax.broadcasted_iota(jnp.int32, (size, size), 1)
    identity = (row_id == column_id).astype(jnp.float32)
    packed = grams_ref[:, :-1, :].reshape(2 * size, size)

    def split(i):
        pair, diag = packed[i * size : (i + 1) * size, :], grams_ref[i, -1:, :]
        first = jnp.where(row_id >= column_id, pair, pair.T)
        second = jnp.where(row_id < column_id, pair, pair.T)
        return first, jnp.where(row_id == column_id, diag, second)

    (resid, energy), (coupling, outer) = split(0), split(1)
    energy_inv, resid_inv = invert(scratch, energy, resid)
    step = mm(energy_inv, resid)
    shift = mm(energy, step)
    coupled = mm(coupling, step)
    next_gram = resid - shift - shift.T + mm(step, coupled, TRANS)
    grow = identity + mm(resid_inv, next_gram)
    cross = mm(grow, coupled, TRANS)
    next_energy = mm(grow, mm(energy, grow), TRANS) - cross - cross.T + mm(step, mm(outer, step), TRANS)
    next_energy = 0.5 * (next_energy + next_energy.T)
    (next_inv,) = invert(scratch, next_energy)
    next_step = mm(next_inv, next_gram)
    near = step + mm(grow, next_step)
    far = mm(step, next_step)
    weights = halves(jnp.concatenate([near.T, -far.T], axis=1))
    for load in loads:
        load.wait()
    parts, planes, comps = basis_ref.shape[1:4]
    stores = []
    for c in range(comps):
        for p in range(planes):
            block = right_ref.shape[2:]

            def pair(one, other):
                return jnp.concatenate([basis_ref[slot, h, p, c] for slot in (one, other) for h in range(parts)])

            solution_ref[c, p] = mm_halves(weights, pair(0, 2)).T.reshape(block)
            residual_ref[c, p] = right_ref[c, p] - mm_halves(weights, pair(1, 3)).T.reshape(block)
        for k, (source, target) in enumerate(((solution_ref, solution_hbm), (residual_ref, residual_hbm))):
            stores.append(pltpu.make_async_copy(source.at[c], target.at[c], out_sem.at[k, c]))
            stores[-1].start()
    for store in stores:
        store.wait()


def finish(grams, right_side, basis):
    vmem, whole = pl.BlockSpec(memory_space=pltpu.VMEM), pl.BlockSpec(memory_space=pl.ANY)
    size = grams.shape[2]
    scratch_of = [(2, size, size), right_side.shape, basis.shape, right_side.shape, right_side.shape]
    return tuple(
        pl.pallas_call(
            finish_kernel,
            out_shape=[jax.ShapeDtypeStruct(right_side.shape, jnp.float32)] * 2,
            in_specs=[vmem, whole, whole],
            out_specs=[whole] * 2,
            scratch_shapes=[pltpu.VMEM(shape, jnp.float32) for shape in scratch_of]
            + [pltpu.SemaphoreType.DMA((2,)), pltpu.SemaphoreType.DMA((2, right_side.shape[0]))],
            name="finish",
        )(grams, right_side, basis)
    )


CHANNELS = 12
LOWER, UPPER, BOTH = 0, 1, 2
SLOTS = len(lower_offsets)
PARTS = 4
PHASES = 6 * PARTS


def krylov_kernel(
    z_lo_count, z_hi_count, right_ref, stiff_diag_ref, stiff_ref, fsai_diag_ref, fsai_ref, kept_ref, total_ref, out_ref,
    vec, edge, rim_out, rim_in, low, high, low_out, low_in, mats, grams, rs_buf, z_buf,
    halo_send, halo_recv, send, recv, z_send, z_recv, a_send, a_recv, out_sem,
):
    size, lanes = vec.shape[3:]
    half, top, bottom = lanes // 2, pl.ds(0, size // 2), pl.ds(size // 2, size // 2)
    group, dev = lax.axis_index("group"), lax.axis_index("dev")
    group_count, dev_count = GROUP_Y * z_lo_count, DEV_XC * z_hi_count
    z_lo, y = group // GROUP_Y, group % GROUP_Y
    z_hi, xc = dev // DEV_XC, dev % DEV_XC
    me = y * DEV_XC + xc
    my_z = z_hi * z_lo_count + z_lo
    z_count = z_lo_count * z_hi_count
    has_prev_dev, has_next_dev = dev > 0, dev < dev_count - 1
    has_prev_group, has_next_group = group > 0, group < group_count - 1
    near_prev, near_next = dev % DEV_XC > 0, dev % DEV_XC < DEV_XC - 1
    prev_dev, next_dev = (group, dev - 1), (group, dev + 1)
    prev_group, next_group = (group - 1, dev), (group + 1, dev)

    def plane_peer(step):
        peer = lax.rem(me + step, PLANE_PEERS)
        return peer, (z_lo * GROUP_Y + lax.div(peer, DEV_XC), z_hi * DEV_XC + lax.rem(peer, DEV_XC))

    def z_peer(step):
        peer = lax.rem(my_z + step, z_count)
        return peer, (lax.rem(peer, z_lo_count) * GROUP_Y + y, lax.div(peer, z_lo_count) * DEV_XC + xc)

    def clear(ref):
        ref[...] = jnp.zeros(ref.shape, ref.dtype)

    def clear_phases(*refs_of):
        def body(f, carry):
            for ref_of in refs_of:
                clear(ref_of(f))
            return carry
        lax.fori_loop(0, PHASES, body, 0)

    @pl.when(jnp.logical_not(has_prev_dev))
    def _():
        clear_phases(lambda f: rim_in.at[f, 0])
        clear(low_in.at[0])

    @pl.when(jnp.logical_not(has_next_dev))
    def _():
        clear_phases(lambda f: rim_in.at[f, 1])
        clear(low_in.at[1])

    @pl.when(jnp.logical_not(has_prev_group))
    def _():
        clear_phases(lambda f: rim_in.at[f, 0, 0], lambda f: rim_in.at[f, 1, 0], lambda f: vec.at[f, 0])

    @pl.when(jnp.logical_not(has_next_group))
    def _():
        clear_phases(lambda f: rim_in.at[f, 0, 3], lambda f: rim_in.at[f, 1, 3], lambda f: vec.at[f, 3])
        for k in range(2):
            clear(low_in.at[k, 2])
            clear(low.at[k, 2])

    barrier = pltpu.get_barrier_semaphore()

    def greet(place):
        pl.semaphore_signal(barrier, inc=1, device_id=place, device_id_type=MESH)

    def greet_all(count, peer_of):
        def body(step, carry):
            greet(peer_of(step)[1])
            return carry
        lax.fori_loop(1, count, body, 0)

    around = [(1, 0), (dev_count - 1, 0), (0, 1), (0, group_count - 1)]
    around += [(a, b) for a in (1, dev_count - 1) for b in (1, group_count - 1)]
    neighbours = [((group + b) % group_count, (dev + a) % dev_count) for a, b in around]
    greet_all(PLANE_PEERS, plane_peer)
    greet_all(z_count, z_peer)
    for place in neighbours:
        greet(place)

    def left_of(shape):
        return lax.broadcasted_iota(jnp.int32, shape, len(shape) - 1) < half

    def swap(tile):
        return pltpu.roll(tile, half, axis=tile.ndim - 1)

    def turn(tile, step):
        return tile if step == 0 else pltpu.roll(tile, -step % lanes, axis=tile.ndim - 1)

    for p in range(2):
        for c in range(3):
            tile = right_ref[c, p].reshape(lanes, PARTS * size).T
            for h in range(PARTS):
                vec[h, p + 1, c] = tile[h * size : (h + 1) * size]

    left_low = left_of(low.shape[3:])
    left_half = left_of((size // 2, lanes))

    def pack_low(plane):
        low_out[0, plane] = jnp.where(left_low[None], swap(low[0, plane]), low[1, plane])
        low_out[1, plane] = jnp.where(left_low[None], low[0, plane], swap(low[1, plane]))

    column = lax.broadcasted_iota(jnp.int32, (1, lanes), 1) % half
    inside = {-1: column > 0, 0: column >= 0, 1: column < half - 1}
    for p in range(2):
        for slot, (_, _, c) in enumerate(lower_offsets):
            kept = jnp.where(inside[c], kept_ref[slot, pl.ds(p, 1), :].astype(jnp.float32), 0.0)
            for i in range(3):
                for j in range(3):
                    entry = pl.ds(i * 3 + j, 1)
                    low[0, p, slot, entry, :] = fsai_ref[i, j, slot, pl.ds(p, 1), :] * kept
                    low[1, p, slot, entry, :] = jnp.where(inside[c], stiff_ref[i, j, slot, pl.ds(p, 1), :], 0.0)
        pack_low(p)
    pl.semaphore_wait(barrier, PLANE_PEERS - 1 + z_count - 1 + len(neighbours))

    def route(number, own_way):
        along = {
            0: (next_dev, has_next_dev, has_prev_dev),
            1: (prev_dev, has_prev_dev, has_next_dev),
            2: (next_group, has_next_group, has_prev_group),
            3: (prev_group, has_prev_group, has_next_group),
        }
        if number < 2:
            return along[number]
        if number < 4:
            return along[number]
        place, to, come = along[number % 2]
        given = has_prev_group if number < 6 else has_next_group
        if own_way:
            to = to & (near_next if number % 2 == 0 else near_prev)
        return place, to & given, come & given

    def move(source, target, phase, number, method, own_way=False):
        place, to, come = route(number, own_way)

        @pl.when(come if method == "wait_recv" else to)
        def _():
            copy = pltpu.make_async_remote_copy(
                src_ref=source, dst_ref=target,
                send_sem=halo_send.at[phase, number], recv_sem=halo_recv.at[phase, number],
                device_id=place, device_id_type=MESH,
            )
            getattr(copy, method)()

    def halo_plane(f, plane, method):
        number, source = (2, 2) if plane == 0 else (3, 1)
        move(vec.at[f, source], vec.at[f, plane], f, number, method)

    def halo_rim(f, side, kind, method):
        if side == 0:
            planes = pl.ds(2, 1) if kind == UPPER else pl.ds(1, 2)
        else:
            planes = pl.ds(1, 1) if kind == LOWER else pl.ds(1, 2)
        move(rim_out.at[f, side, planes], rim_in.at[f, side, planes], f, side, method)

    def halo_corner(f, plane, side, method):
        number = (4 if plane == 0 else 6) + side
        move(rim_out.at[f, side, plane], rim_in.at[f, side, plane], f, number, method, True)

    def far_corner(f, plane, side, method):
        ahead, on = (1, has_next_group) if plane == 0 else (-1, has_prev_group)
        far = has_next_dev & jnp.logical_not(near_next) if side == 0 else has_prev_dev & jnp.logical_not(near_prev)
        number = (4 if plane == 0 else 6) + side

        @pl.when(on & far)
        def _():
            copy = pltpu.make_async_remote_copy(
                src_ref=rim_out.at[f, side, 2 if plane == 0 else 1], dst_ref=rim_in.at[f, side, plane],
                send_sem=halo_send.at[f, number + 4], recv_sem=halo_recv.at[f, number],
                device_id=(group + ahead, dev + (1 if side == 0 else -1)), device_id_type=MESH,
            )
            getattr(copy, method)()

    def low_halo(number, method):
        if number == 3:
            move(low.at[:, 0], low.at[:, 2], PHASES, number, method)
            return
        side = number % 2
        planes = pl.ds(2, 1) if number > 3 else (pl.ds(1, 1) if side == 0 else pl.ds(0, 2))
        move(low_out.at[side, planes], low_in.at[side, planes], PHASES, number, method)

    def pack(f, plane, c):
        upper_rows, lower_rows = vec[f, plane, c, top, :], vec[f, plane, c, bottom, :]
        rim_out[f, 0, plane, c] = jnp.where(left_half, swap(upper_rows), lower_rows)
        rim_out[f, 1, plane, c] = jnp.where(left_half, upper_rows, swap(lower_rows))

    def unpack(f, plane):
        for c in range(3):
            before, after = rim_in[f, 0, plane, c], rim_in[f, 1, plane, c]
            edge[plane, c, top, :] = jnp.where(left_half, before, swap(after))
            edge[plane, c, bottom, :] = jnp.where(left_half, swap(before), after)

    outer_of = {LOWER: (0,), UPPER: (3,), BOTH: (0, 3)}

    def send_own(f, kind):
        for plane in outer_of[kind]:
            halo_plane(f, plane, "start")
        for plane in (1, 2):
            for c in range(3):
                pack(f, plane, c)
        for side in (0, 1):
            halo_rim(f, side, kind, "start")
            for plane in outer_of[kind]:
                far_corner(f, plane, side, "start")

    def pass_planes(f, kind):
        for plane in outer_of[kind]:
            halo_plane(f, plane, "wait_recv")
            for c in range(3):
                pack(f, plane, c)
            for side in (0, 1):
                halo_corner(f, plane, side, "start")

    def take_rims(f, kind):
        for side in (0, 1):
            halo_rim(f, side, kind, "wait_recv")
        for plane in (1, 2):
            unpack(f, plane)

    def take_corners(f, kind):
        for plane in outer_of[kind]:
            for side in (0, 1):
                halo_corner(f, plane, side, "wait_recv")
            unpack(f, plane)

    def settle(f, kind):
        for side in (0, 1):
            halo_rim(f, side, kind, "wait_send")
            for plane in outer_of[kind]:
                halo_corner(f, plane, side, "wait_send")
                far_corner(f, plane, side, "wait_send")
        for plane in outer_of[kind]:
            halo_plane(f, plane, "wait_send")

    def raise_coefs(k):
        def body(p, carry):
            for slot, (a, b, c) in enumerate(lower_offsets):
                at = p - a
                base = low[k, at, slot]
                if b == -1:
                    rim = low_in[1, at, slot]
                    base = jnp.where(left_low, swap(base), swap(rim) if k == 0 else rim)
                elif b == 1:
                    rim = low_in[0, at, slot]
                    base = jnp.where(left_low, rim if k == 0 else swap(rim), swap(base))
                high[k, p, slot] = turn(base, -c)
            return carry
        lax.fori_loop(0, 2, body, 0)

    rows_count = 32
    left = left_of((rows_count, lanes))
    diags = (fsai_diag_ref, stiff_diag_ref)

    def uses_of(parts):
        uses = {}
        for part, (upper, plane, diagonal) in enumerate(parts):
            sign = -1 if upper else 1
            slots = [(None, (0, 0, 0))] if diagonal else []
            for slot, (a, b, c) in slots + list(enumerate(lower_offsets)):
                at = uses.setdefault(plane + 1 + sign * a, {}).setdefault(sign * b, {})
                at.setdefault(sign * c, []).append((part, slot))
        return uses

    def accumulate(acc, v, k, parts, rows):
        for at, by_row in sorted(uses_of(parts).items()):
            for j in range(3):
                own = vec[v, at, j, rows, :]
                swapped = swap(own) if set(by_row) != {0} else None
                for b, by_column in sorted(by_row.items()):
                    tile = own
                    if b != 0:
                        outside = edge[at, j, rows, :]
                        tile = jnp.where(left, outside, swapped) if b < 0 else jnp.where(left, swapped, outside)
                    for c, users in sorted(by_column.items()):
                        value = turn(tile, c)
                        for part, slot in users:
                            upper, plane, _ = parts[part]
                            for i in range(3):
                                row, col = (j, i) if upper else (i, j)
                                if slot is None:
                                    block = diags[k][row, col, pl.ds(plane, 1), :]
                                else:
                                    table = high if upper else low
                                    block = table[k, plane, slot, pl.ds(row * 3 + col, 1), :]
                                acc[part][i] = acc[part][i] + block * value
        return acc

    def apply(v, target, k, parts, add):
        def body(step, carry):
            rows = pl.ds(pl.multiple_of(step * rows_count, rows_count), rows_count)
            if add:
                acc = [[vec[target, plane + 1, i, rows, :] for i in range(3)] for _, plane, _ in parts]
            else:
                acc = [[jnp.zeros((rows_count, lanes), jnp.float32)] * 3 for _ in parts]
            acc = accumulate(acc, v, k, parts, rows)
            for (_, plane, _), values in zip(parts, acc):
                for i in range(3):
                    vec[target, plane + 1, i, rows, :] = values[i]
            return carry

        lax.fori_loop(0, size // rows_count, body, 0)

    def across(v):
        parts = [
            jnp.concatenate([vec[PARTS * v + h, p, c] for p in (1, 2) for c in range(3)], axis=1) for h in range(PARTS)
        ]
        return jnp.concatenate(parts, axis=0)

    def gram(index, v, w):
        one = across(v)
        mats[index] = mm(one, one if w is None else across(w), ((1,), (1,)))

    def emit(slot, v):
        return pltpu.make_async_copy(vec.at[pl.ds(PARTS * v, PARTS), pl.ds(1, 2)], out_ref.at[slot], out_sem.at[slot])

    def each_part(step):
        def body(h, carry):
            step(h)
            return carry
        lax.fori_loop(0, PARTS, body, 0)

    def operate(v, k, kind, then):
        early, late = {
            LOWER: (((False, 1, True),), ((False, 0, True),)),
            UPPER: (((True, 0, True),), ((True, 1, True),)),
            BOTH: (((False, 1, True), (True, 0, False)), ((False, 0, True), (True, 1, False))),
        }[kind]

        def step(h):
            f, target = PARTS * v + h, PARTS * (v + 1) + h

            @pl.when(h < PARTS - 1)
            def _():
                pass_planes(f + 1, kind)

            take_rims(f, kind)
            apply(f, target, k, early, False)
            take_corners(f, kind)
            apply(f, target, k, late, kind == BOTH)
            then(target)

        each_part(step)

    each_part(lambda h: send_own(h, LOWER))
    for number in (3, 0, 1):
        low_halo(number, "start")

    def round_body(t, carry):
        v = 3 * t
        pass_planes(PARTS * v, LOWER)

        @pl.when(t == 0)
        def _():
            low_halo(3, "wait_recv")
            pack_low(2)
            for number in (6, 7):
                low_halo(number, "start")

        operate(v, 0, LOWER, lambda f: send_own(f, UPPER))
        gram(2 * t, v + 1, None)

        @pl.when(t == 0)
        def _():
            for number in (0, 1, 6, 7):
                low_halo(number, "wait_recv")
            raise_coefs(0)

        pass_planes(PARTS * (v + 1), UPPER)
        operate(v + 1, 0, UPPER, lambda f: send_own(f, BOTH))
        emit(2 * t, v + 2).start()

        @pl.when(t == 0)
        def _():
            raise_coefs(1)

        pass_planes(PARTS * (v + 2), BOTH)

        def again(f):
            @pl.when(t == 0)
            def _():
                send_own(f, LOWER)

        operate(v + 2, 1, BOTH, again)
        emit(2 * t + 1, v + 3).start()
        gram(2 * t + 1, v + 2, v + 3)
        return carry

    lax.fori_loop(0, 2, round_body, 0)
    square = mats.shape[1:]
    row_id = lax.broadcasted_iota(jnp.int32, square, 0)
    column_id = lax.broadcasted_iota(jnp.int32, square, 1)
    count = square[0] // (grams.shape[1] - 1)
    grams[:, pl.ds(grams.shape[1] - 1, 1), :] = jnp.zeros((grams.shape[0], 1, square[1]), jnp.float32)
    for i in range(2):
        first, second = mats[2 * i], mats[2 * i + 1]
        pair = jnp.where(row_id >= column_id, first, second)
        grams[pl.ds(i * count, count), pl.ds(0, grams.shape[1] - 1), :] = pair.reshape(count, -1, square[1])
        diag = jnp.sum(jnp.where(row_id == column_id, second, 0.0), axis=0, keepdims=True)
        grams[i, pl.ds(grams.shape[1] - 1, 1), :] = diag

    def scatter(step):
        peer, place = plane_peer(step)
        return pltpu.make_async_remote_copy(
            src_ref=grams.at[peer], dst_ref=rs_buf.at[me], send_sem=send.at[step],
            recv_sem=recv.at[step], device_id=place, device_id_type=MESH,
        )

    def exchange(step):
        _, place = z_peer(step)
        return pltpu.make_async_remote_copy(
            src_ref=z_buf.at[my_z], dst_ref=z_buf.at[my_z], send_sem=z_send.at[step],
            recv_sem=z_recv.at[step], device_id=place, device_id_type=MESH,
        )

    def gather(step):
        _, place = plane_peer(step)
        return pltpu.make_async_remote_copy(
            src_ref=total_ref.at[me], dst_ref=total_ref.at[me], send_sem=a_send.at[step],
            recv_sem=a_recv.at[step], device_id=place, device_id_type=MESH,
        )

    def run(count, make, method):
        def body(step, carry):
            getattr(make(step), method)()
            return carry
        lax.fori_loop(1, count, body, 0)

    run(PLANE_PEERS, scatter, "start")
    rs_buf[me] = grams[me]

    def settle_round(t, carry):
        def settle_part(h):
            for k, kind in enumerate((LOWER, UPPER, BOTH)):
                settle(PARTS * (3 * t + k) + h, kind)

        each_part(settle_part)
        return carry

    lax.fori_loop(0, 2, settle_round, 0)
    for number in (3, 0, 1, 6, 7):
        low_halo(number, "wait_send")
    run(PLANE_PEERS, scatter, "wait_recv")
    z_buf[my_z] = jnp.sum(rs_buf[...], axis=0)
    run(z_count, exchange, "start")
    run(PLANE_PEERS, scatter, "wait_send")
    run(z_count, exchange, "wait_recv")
    total_ref[me] = jnp.sum(z_buf[...], axis=0)
    run(PLANE_PEERS, gather, "start")
    run(z_count, exchange, "wait_send")
    for slot, v in enumerate((2, 3, 5, 6)):
        emit(slot, v).wait()
    run(PLANE_PEERS, gather, "wait_recv")
    run(PLANE_PEERS, gather, "wait_send")


def krylov(right_side, *coefs):
    z_lo_count = lax.axis_size("group") // GROUP_Y
    z_hi_count = lax.axis_size("dev") // DEV_XC
    z_count = z_lo_count * z_hi_count
    comps, planes, rows, columns, size = right_side.shape
    lanes = rows * columns
    pieces = (PLANE_PEERS, 2 * size // PLANE_PEERS + 1, size)
    part = size // PARTS
    vmem = pl.BlockSpec(memory_space=pltpu.VMEM)
    dma = pltpu.SemaphoreType.DMA

    def array(*shape):
        return pltpu.VMEM(shape, jnp.float32)

    total, vectors = pl.pallas_call(
        functools.partial(krylov_kernel, z_lo_count, z_hi_count),
        out_shape=[
            jax.ShapeDtypeStruct(pieces, jnp.float32),
            jax.ShapeDtypeStruct((4, PARTS, planes, comps, part, lanes), jnp.float32),
        ],
        in_specs=[vmem] * (1 + len(coefs)),
        out_specs=[vmem, pl.BlockSpec(memory_space=pl.ANY)],
        scratch_shapes=[
            array(7 * PARTS, 4, comps, part, lanes),
            array(4, comps, part, lanes),
            array(PHASES, 2, 4, comps, part // 2, lanes),
            array(PHASES, 2, 4, comps, part // 2, lanes),
            array(2, 3, SLOTS, 9, lanes),
            array(2, 2, SLOTS, 9, lanes),
            array(2, 3, SLOTS, 9, lanes),
            array(2, 3, SLOTS, 9, lanes),
            array(4, size, size),
            array(*pieces),
            array(*pieces),
            array(z_count, *pieces[1:]),
            dma((PHASES + 1, CHANNELS)), dma((PHASES + 1, CHANNELS)),
            dma((PLANE_PEERS,)), dma((PLANE_PEERS,)),
            dma((z_count,)), dma((z_count,)),
            dma((PLANE_PEERS,)), dma((PLANE_PEERS,)),
            dma((4,)),
        ],
        compiler_params=pltpu.CompilerParams(collective_id=0, has_side_effects=True),
        name="krylov",
    )(right_side, *coefs)
    return total, vectors


def per_device(right_side, *coefs):
    grams, basis = krylov(right_side, *coefs)
    return finish(grams, right_side, basis)


def solution(mesh):
    return jax.shard_map(
        per_device,
        mesh=mesh,
        in_specs=(
            P(None, "group", "dev", None, None),
            P(None, None, "group", "dev"),
            P(None, None, None, "group", "dev"),
            P(None, None, "group", "dev"),
            P(None, None, None, "group", "dev"),
            P(None, "group", "dev"),
        ),
        out_specs=(P(None, "group", "dev", None, None), P(None, "group", "dev", None, None)),
        check_vma=False,
    )
```
